512 devices in a mesh: row: 16 (over z_hi, x), col: 32 (over z_lo, y, core).
Axes of the slice: x: 4, y: 4, z: 16 (z_hi: 4, z_lo: 4; z = z_hi * 4 + z_lo), core: 2. Of those that a mesh axis runs over, the one named last changes fastest.
Arguments:
- object_field: float32 [2, 6144, 8192], P(None, 'row', 'col'), may hold values from -6 to 6
- probe_modes: float32 [2, 2, 128, 128], replicated, may hold values from -2.1 to 2.1
- measured: float32 [16, 32, 8, 128, 128], P('row', 'col'), may hold values from 0.1 to 3
- positions: int32 [16, 32, 2, 8], P('row', 'col'), may hold values from 0 to 383, as said below
- counts: int32 [16, 32], P('row', 'col'), may hold values from 2 to 8, as said below
Outputs:
- object_new: float32 [2, 6144, 8192], P(None, 'row', 'col')
- probe_step: float32 [2, 2, 128, 128], replicated
The draws below stay inside these ranges and needn't reach their ends.
Inputs may be any that keep to these rules, and one draw needn't show every extreme that they name: `positions`: offsets lie inside the tile: row offsets below 384, column offsets below 256; both edges are reached. `counts`: some tile uses all 8 slots.
All inputs are finite; a program needn't handle non-finite values.
Results may differ from the reference program's by a relative error of at most 0.0003.
Values sent between devices are 32-bit elements; how exact they have to be, the bound alone decides.
No kernel may reach another device: no remote copies, remote signals or barrier semaphores. Data moves between devices by JAX's collectives and lax.ppermute only.
A program may use at most 64 MiB of HBM per device.

```python
import math
import jax
import jax.numpy as jnp
from jax import lax

PATCH = 128
MODES = 2
TILE_HEIGHT = 384
TILE_WIDTH = 256
SLOTS = 8
GRID_HEIGHT = 16
GRID_WIDTH = 32
OBJECT_HEIGHT = 6144
OBJECT_WIDTH = 8192


def draw_positions(key, part):
    down_offset = jax.random.randint(jax.random.fold_in(key, 11), (GRID_HEIGHT, GRID_WIDTH, SLOTS), 0, TILE_HEIGHT)
    side_offset = jax.random.randint(jax.random.fold_in(key, 12), (GRID_HEIGHT, GRID_WIDTH, SLOTS), 0, TILE_WIDTH)
    down_offset = down_offset.at[0, 0, 0].set(TILE_HEIGHT - 1).at[0, 0, 1].set(0)
    side_offset = side_offset.at[0, 0, 0].set(TILE_WIDTH - 1).at[0, 0, 1].set(0)
    return jnp.stack([down_offset, side_offset], axis=2).astype(jnp.int32)


def draw_counts(key, part):
    tiles = GRID_HEIGHT * GRID_WIDTH
    spread = jax.random.randint(jax.random.fold_in(key, 21), (tiles,), 0, SLOTS - 1)
    filled = 2 + spread * spread // max(SLOTS - 2, 1)
    chosen = jax.random.randint(jax.random.fold_in(key, 22), (), 0, tiles)
    filled = jnp.where(jnp.arange(tiles, dtype=jnp.int32) == chosen, SLOTS, filled)
    return filled.reshape(GRID_HEIGHT, GRID_WIDTH).astype(jnp.int32)


def block_levels(own_key, shape, cuts, smallest, top_value):
    factor_of = 1.0
    for dim, parts in cuts:
        steps = jax.random.uniform(jax.random.fold_in(jax.random.fold_in(own_key, 6), dim), (parts,), jnp.float32, smallest / len(cuts), top_value / len(cuts))
        factor_of = factor_of * jnp.repeat(jnp.exp(steps), shape[dim] // parts).reshape((-1,) + (1,) * (len(shape) - 1 - dim))
    return factor_of


def bell_draw(rng, extent, deviation, most, pieces=(), kind=jnp.bfloat16):
    values = jax.random.normal(rng, extent, jnp.float32) * deviation
    if len(pieces) > 0:
        values = block_levels(rng, extent, pieces, -0.22, 0.18) * values
    return jnp.clip(values, min=-most, max=most).astype(kind)


def setup_inputs(seed: int = 0) -> dict:
    keys = jax.random.split(jax.random.key(seed), 6)
    return {
        "object_field": bell_draw(keys[0], (2, OBJECT_HEIGHT, OBJECT_WIDTH), 1.0, 6.0, ((1, 16), (2, 32)), jnp.float32),
        "probe_modes": bell_draw(keys[1], (2, MODES, PATCH, PATCH), 0.35, 2.1, (), jnp.float32),
        "measured": jnp.clip(jnp.exp(math.log(3.0) - 3.4011974 * jax.random.uniform(keys[2], (GRID_HEIGHT, GRID_WIDTH, SLOTS, PATCH, PATCH), jnp.float32) ** block_levels(keys[2], (GRID_HEIGHT, GRID_WIDTH, SLOTS, PATCH, PATCH), ((0, 16), (1, 32)), -0.2, 0.2)), 0.1, 3.0),
        "positions": draw_positions(jax.random.fold_in(keys[5], 71), 0),
        "counts": draw_counts(jax.random.fold_in(keys[5], 71), 0),
    }


HIGHEST = lax.Precision.HIGHEST
AMP_FLOOR = 0.25

def fourier_tables(patch_width):
    index = jnp.arange(patch_width, dtype=jnp.int32)
    product = index[:, None] * index[None, :] % patch_width
    angle = product.astype(jnp.float32) * (2.0 * math.pi / patch_width)
    scale = 1.0 / math.sqrt(patch_width)
    return (jnp.cos(angle) * scale, jnp.sin(angle) * scale)

def transform(real_part, imag_part, cosine_table, sine_table, sign_value):
    left_real = jnp.einsum('jk,...kl->...jl', cosine_table, real_part, precision=HIGHEST) - sign_value * jnp.einsum('jk,...kl->...jl', sine_table, imag_part, precision=HIGHEST)
    left_imag = jnp.einsum('jk,...kl->...jl', cosine_table, imag_part, precision=HIGHEST) + sign_value * jnp.einsum('jk,...kl->...jl', sine_table, real_part, precision=HIGHEST)
    out_real = jnp.einsum('...jk,kl->...jl', left_real, cosine_table, precision=HIGHEST) - sign_value * jnp.einsum('...jk,kl->...jl', left_imag, sine_table, precision=HIGHEST)
    out_imag = jnp.einsum('...jk,kl->...jl', left_imag, cosine_table, precision=HIGHEST) + sign_value * jnp.einsum('...jk,kl->...jl', left_real, sine_table, precision=HIGHEST)
    return (out_real, out_imag)

def contributions(patches, probe_modes, amplitudes, live_slots, cosine_table, sine_table):
    patch_real = patches[:, 0][:, None]
    patch_imag = patches[:, 1][:, None]
    mode_real = probe_modes[0][None]
    mode_imag = probe_modes[1][None]
    exit_real = mode_real * patch_real - mode_imag * patch_imag
    exit_imag = mode_real * patch_imag + mode_imag * patch_real
    far_real, far_imag = transform(exit_real, exit_imag, cosine_table, sine_table, -1.0)
    intensity = lax.optimization_barrier(jnp.sum(far_real * far_real + far_imag * far_imag, axis=1))
    scaling = (amplitudes / jnp.maximum(jnp.sqrt(intensity), AMP_FLOOR) - 1.0) * live_slots[:, None, None]
    scaling = scaling[:, None]
    back_real, back_imag = transform(far_real * scaling, far_imag * scaling, cosine_table, sine_table, 1.0)
    object_real = lax.optimization_barrier(jnp.sum(mode_real * back_real + mode_imag * back_imag, axis=1))
    object_imag = lax.optimization_barrier(jnp.sum(mode_real * back_imag - mode_imag * back_real, axis=1))
    probe_real = lax.optimization_barrier(jnp.sum(patch_real * back_real + patch_imag * back_imag, axis=0))
    probe_imag = lax.optimization_barrier(jnp.sum(patch_real * back_imag - patch_imag * back_real, axis=0))
    density = lax.optimization_barrier(jnp.sum(live_slots[:, None, None] * (patches[:, 0] * patches[:, 0] + patches[:, 1] * patches[:, 1]), axis=0))
    return (jnp.stack([object_real, object_imag], axis=1), jnp.stack([probe_real, probe_imag]), density)

def cut_patches(field, row_starts, col_starts, patch_width):

    def one_patch(row_start, col_start):
        return lax.dynamic_slice(field, (jnp.int32(0), row_start, col_start), (2, patch_width, patch_width))
    return jax.vmap(one_patch)(row_starts.astype(jnp.int32), col_starts.astype(jnp.int32))

def accumulate(gradient, object_terms, row_starts, col_starts):
    patch_width = object_terms.shape[-1]

    def add_one(slot_index, totals):
        corner_at = (jnp.int32(0), row_starts[slot_index].astype(jnp.int32), col_starts[slot_index].astype(jnp.int32))
        current = lax.dynamic_slice(totals, corner_at, (2, patch_width, patch_width))
        return lax.dynamic_update_slice(totals, current + object_terms[slot_index], corner_at)
    return lax.fori_loop(0, object_terms.shape[0], add_one, gradient)

def reference(object_field, probe_modes, measured, positions, counts):
    patch_width = probe_modes.shape[-1]
    capacity = positions.shape[-1]
    grid_height, grid_width = counts.shape
    object_height, object_width = (object_field.shape[1], object_field.shape[2])
    tile_height = object_height // grid_height
    tile_width = object_width // grid_width
    cosine_table, sine_table = fourier_tables(patch_width)
    padded = jnp.pad(object_field, ((0, 0), (0, patch_width), (0, patch_width)))
    tiles = grid_height * grid_width
    base_rows = jnp.broadcast_to((jnp.arange(grid_height, dtype=jnp.int32) * tile_height)[:, None], (grid_height, grid_width)).reshape(tiles)
    base_cols = jnp.broadcast_to((jnp.arange(grid_width, dtype=jnp.int32) * tile_width)[None, :], (grid_height, grid_width)).reshape(tiles)
    row_offsets = positions[:, :, 0, :].reshape(tiles, capacity).astype(jnp.int32)
    col_offsets = positions[:, :, 1, :].reshape(tiles, capacity).astype(jnp.int32)
    live_all = (jnp.arange(capacity, dtype=jnp.int32)[None, :] < counts.reshape(tiles, 1)).astype(jnp.float32)
    amplitude_all = measured.reshape(tiles, capacity, patch_width, patch_width)

    def device_step(totals, inputs_now):
        gradient, probe_sum, density_sum = totals
        base_row, base_col, row_part, col_part, live_slots, amplitudes = inputs_now
        row_starts = row_part + base_row
        col_starts = col_part + base_col
        patches = cut_patches(padded, row_starts, col_starts, patch_width)
        object_terms, probe_terms, density = contributions(patches, probe_modes, amplitudes, live_slots, cosine_table, sine_table)
        gradient = accumulate(gradient, object_terms, row_starts, col_starts)
        return ((gradient, probe_sum + probe_terms, density_sum + density), None)
    initial = (jnp.zeros_like(padded), jnp.zeros_like(probe_modes), jnp.zeros((patch_width, patch_width), jnp.float32))
    (gradient, probe_sum, density_sum), _ = lax.scan(device_step, initial, (base_rows, base_cols, row_offsets, col_offsets, live_all, amplitude_all))
    peak_power = jnp.max(lax.optimization_barrier(jnp.sum(probe_modes * probe_modes, axis=(0, 1))))
    object_new = object_field + gradient[:, :object_height, :object_width] / (peak_power + 1e-06)
    probe_step = probe_sum / jnp.sqrt(density_sum + 1.0)[None, None]
    return (object_new, probe_step)
```

```python
import math

import jax
import jax.numpy as jnp
from jax import lax
from jax.sharding import PartitionSpec as P

HIGHEST = lax.Precision.HIGHEST
AMP_FLOOR = 0.25


def shifted(array, axis, by):
    length = lax.axis_size(axis)
    pairs = [(i, i + by) for i in range(length) if 0 <= i + by < length]
    return lax.ppermute(array, axis, pairs)


def coordinates(device):
    row, col = divmod(device, 32)
    z_hi, x = divmod(row, 4)
    z_lo, rest = divmod(col, 8)
    y, core = divmod(rest, 2)
    return (z_hi * 4 + z_lo, x, y, core)


def device_groups(devices):
    planes, lines = {}, {}
    for device in range(devices):
        z, x, y, core = coordinates(device)
        planes.setdefault(z, []).append(device)
        lines.setdefault((x, y, core), []).append(device)
    return (list(planes.values()), list(lines.values()))


def exchange(blocks, groups):
    return lax.all_to_all(blocks, ("row", "col"), 0, 0, axis_index_groups=groups)


def sum_over_all(flat):
    rows, lanes = flat.shape
    planes, lines = device_groups(lax.axis_size("row") * lax.axis_size("col"))
    in_plane, in_line = (len(planes[0]), len(lines[0]))
    part = rows // in_plane
    own = jnp.sum(exchange(flat.reshape(in_plane, part, lanes), planes), axis=0)
    own = jnp.sum(exchange(jnp.broadcast_to(own[None], (in_line, part, lanes)), lines), axis=0)
    everyone = exchange(jnp.broadcast_to(own[None], (in_plane, part, lanes)), planes)
    return everyone.reshape(rows, lanes)


def fourier_tables(patch_width):
    index = jnp.arange(patch_width, dtype=jnp.int32)
    product = index[:, None] * index[None, :] % patch_width
    angle = product.astype(jnp.float32) * (2.0 * math.pi / patch_width)
    scale = 1.0 / math.sqrt(patch_width)
    return (jnp.cos(angle) * scale, jnp.sin(angle) * scale)


def transform(real_part, imag_part, cosine_table, sine_table, sign_value):
    left_real = jnp.einsum(
        "jk,...kl->...jl", cosine_table, real_part, precision=HIGHEST
    ) - sign_value * jnp.einsum("jk,...kl->...jl", sine_table, imag_part, precision=HIGHEST)
    left_imag = jnp.einsum(
        "jk,...kl->...jl", cosine_table, imag_part, precision=HIGHEST
    ) + sign_value * jnp.einsum("jk,...kl->...jl", sine_table, real_part, precision=HIGHEST)
    out_real = jnp.einsum(
        "...jk,kl->...jl", left_real, cosine_table, precision=HIGHEST
    ) - sign_value * jnp.einsum("...jk,kl->...jl", left_imag, sine_table, precision=HIGHEST)
    out_imag = jnp.einsum(
        "...jk,kl->...jl", left_imag, cosine_table, precision=HIGHEST
    ) + sign_value * jnp.einsum("...jk,kl->...jl", left_real, sine_table, precision=HIGHEST)
    return (out_real, out_imag)


def contributions(patches, probe_modes, amplitudes, live_slots, cosine_table, sine_table):
    patch_real = patches[:, 0][:, None]
    patch_imag = patches[:, 1][:, None]
    mode_real = probe_modes[0][None]
    mode_imag = probe_modes[1][None]
    exit_real = mode_real * patch_real - mode_imag * patch_imag
    exit_imag = mode_real * patch_imag + mode_imag * patch_real
    far_real, far_imag = transform(exit_real, exit_imag, cosine_table, sine_table, -1.0)
    intensity = jnp.sum(far_real * far_real + far_imag * far_imag, axis=1)
    scaling = (amplitudes / jnp.maximum(jnp.sqrt(intensity), AMP_FLOOR) - 1.0) * live_slots[
        :, None, None
    ]
    scaling = scaling[:, None]
    back_real, back_imag = transform(
        far_real * scaling, far_imag * scaling, cosine_table, sine_table, 1.0
    )
    object_real = jnp.sum(mode_real * back_real + mode_imag * back_imag, axis=1)
    object_imag = jnp.sum(mode_real * back_imag - mode_imag * back_real, axis=1)
    probe_real = jnp.sum(patch_real * back_real + patch_imag * back_imag, axis=0)
    probe_imag = jnp.sum(patch_real * back_imag - patch_imag * back_real, axis=0)
    density = jnp.sum(
        live_slots[:, None, None] * (patches[:, 0] * patches[:, 0] + patches[:, 1] * patches[:, 1]),
        axis=0,
    )
    return (
        jnp.stack([object_real, object_imag], axis=1),
        jnp.stack([probe_real, probe_imag]),
        density,
    )


def cut_patches(field, row_starts, col_starts, patch_width):

    def one_patch(row_start, col_start):
        return lax.dynamic_slice(
            field, (jnp.int32(0), row_start, col_start), (2, patch_width, patch_width)
        )

    return jax.vmap(one_patch)(row_starts, col_starts)


def accumulate(gradient, object_terms, row_starts, col_starts):
    patch_width = object_terms.shape[-1]

    def add_one(slot_index, totals):
        corner_at = (jnp.int32(0), row_starts[slot_index], col_starts[slot_index])
        current = lax.dynamic_slice(totals, corner_at, (2, patch_width, patch_width))
        return lax.dynamic_update_slice(totals, current + object_terms[slot_index], corner_at)

    return lax.fori_loop(0, object_terms.shape[0], add_one, gradient)


def per_device(object_field, probe_modes, measured, positions, counts):
    patch_width = probe_modes.shape[-1]
    tile_height, tile_width = (object_field.shape[1], object_field.shape[2])
    cosine_table, sine_table = fourier_tables(patch_width)
    row_starts = positions[0, 0, 0]
    col_starts = positions[0, 0, 1]
    capacity = row_starts.shape[0]
    live_slots = (jnp.arange(capacity, dtype=jnp.int32) < counts[0, 0]).astype(jnp.float32)
    amplitudes = measured[0, 0]
    from_below = shifted(object_field[:, :patch_width, :], "row", -1)
    taller = jnp.concatenate([object_field, from_below], axis=1)
    from_right = shifted(taller[:, :, :patch_width], "col", -1)
    extended = jnp.concatenate([taller, from_right], axis=2)
    patches = cut_patches(extended, row_starts, col_starts, patch_width)
    object_terms, probe_terms, density = contributions(
        patches, probe_modes, amplitudes, live_slots, cosine_table, sine_table
    )
    gradient = accumulate(jnp.zeros_like(extended), object_terms, row_starts, col_starts)
    spilled = shifted(gradient[:, :, tile_width:], "col", 1)
    narrow = gradient[:, :, :tile_width].at[:, :, :patch_width].add(spilled)
    lower_rim = shifted(narrow[:, tile_height:, :], "row", 1)
    own_part = narrow[:, :tile_height, :].at[:, :patch_width, :].add(lower_rim)
    peak_power = jnp.max(jnp.sum(probe_modes * probe_modes, axis=(0, 1)))
    object_new = object_field + own_part / (peak_power + 1e-06)
    packed = jnp.concatenate([probe_terms.reshape(-1, patch_width), density], axis=0)
    totals = sum_over_all(packed)
    probe_sum = totals[:-patch_width].reshape(probe_terms.shape)
    density_sum = totals[-patch_width:]
    probe_step = probe_sum / jnp.sqrt(density_sum + 1.0)[None, None]
    return (object_new, probe_step)


def solution(mesh):
    in_specs = (
        P(None, "row", "col"),
        P(),
        P("row", "col", None, None, None),
        P("row", "col", None, None),
        P("row", "col"),
    )
    out_specs = (P(None, "row", "col"), P())
    return jax.shard_map(
        per_device, mesh=mesh, in_specs=in_specs, out_specs=out_specs, check_vma=False
    )
```

```python
import math

import jax
import jax.numpy as jnp
import numpy as np
from jax import lax
from jax.experimental import pallas as pl
from jax.experimental.pallas import tpu as pltpu
from jax.sharding import PartitionSpec as P

AMP_FLOOR = 0.25
PATCH = 128


def shifted(array, axis, by):
    length = lax.axis_size(axis)
    pairs = [(i, i + by) for i in range(length) if 0 <= i + by < length]
    return lax.ppermute(array, axis, pairs)


def coordinates(device):
    row, col = divmod(device, 32)
    z_hi, x = divmod(row, 4)
    z_lo, rest = divmod(col, 8)
    y, core = divmod(rest, 2)
    return (z_hi * 4 + z_lo, x, y, core)


def device_groups(devices):
    planes, lines = {}, {}
    for device in range(devices):
        z, x, y, core = coordinates(device)
        planes.setdefault(z, []).append(device)
        lines.setdefault((x, y, core), []).append(device)
    return (list(planes.values()), list(lines.values()))


def exchange(blocks, groups):
    return lax.all_to_all(blocks, ("row", "col"), 0, 0, axis_index_groups=groups)


def split(values):
    high = values.astype(jnp.bfloat16)
    low = (values - high.astype(jnp.float32)).astype(jnp.bfloat16)
    return (high, low)


def fourier_matrices(width):
    index = np.arange(width)
    angle = (index[:, None] * index[None, :] % width) * (2.0 * math.pi / width)
    cosine, sine = (np.cos(angle) / math.sqrt(width), np.sin(angle) / math.sqrt(width))
    forward = np.block([[cosine, -sine], [sine, cosine]]).astype(np.float32)
    high = forward.astype(jnp.bfloat16)
    low = (forward - high.astype(np.float32)).astype(jnp.bfloat16)
    right = np.concatenate([high, low, high], axis=0)
    left = np.concatenate([high.T, low.T, high.T], axis=1)
    back_high, back_low = (high.T, low.T)
    back_right = np.concatenate([back_high, back_low, back_high], axis=0)
    back_left = np.concatenate([high, low, high], axis=1)
    return (right, left, back_left, back_right)


def times_right(values, table):
    high, low = split(values)
    return jnp.dot(
        jnp.concatenate([high, high, low], axis=1), table, preferred_element_type=jnp.float32
    )


def times_left(table, values):
    high, low = split(values)
    return jnp.dot(
        table, jnp.concatenate([high, high, low], axis=0), preferred_element_type=jnp.float32
    )


def patch_kernel(
    positions_ref,
    counts_ref,
    own_ref,
    below_ref,
    right_ref,
    corner_ref,
    probe_ref,
    measured_ref,
    right_table_ref,
    left_table_ref,
    back_left_ref,
    back_right_ref,
    grad_own_ref,
    grad_right_ref,
    grad_lower_ref,
    packed_ref,
    field_ref,
    grad_ref,
    sums_ref,
):
    tile_height, tile_width = own_ref.shape[1:]
    width = PATCH
    field_ref[:, :tile_height, :tile_width] = own_ref[...]
    field_ref[:, tile_height:, :tile_width] = below_ref[...]
    field_ref[:, :tile_height, tile_width:] = right_ref[...]
    field_ref[:, tile_height:, tile_width:] = corner_ref[...]
    grad_ref[...] = jnp.zeros_like(grad_ref)
    sums_ref[...] = jnp.zeros_like(sums_ref)
    tall = width + 8
    lane = lax.broadcasted_iota(jnp.int32, (tall, width), 1)
    sublane = lax.broadcasted_iota(jnp.int32, (tall // 8, 8, width), 1)

    def slot(index, carry):
        row = positions_ref[0, index]
        col = positions_ref[1, index]
        down = lax.rem(row, 8)
        top = pl.multiple_of(row - down, 8)
        up_by = lax.rem(8 - down, 8)
        shift = lax.rem(col, width)
        base = pl.multiple_of(col - shift, width)
        back_by = lax.rem(width - shift, width)

        def cut(plane):
            near = field_ref[plane, pl.ds(top, tall), pl.ds(base, width)]
            far = field_ref[plane, pl.ds(top, tall), pl.ds(base + width, width)]
            turned = jnp.where(
                lane < width - shift,
                pltpu.roll(near, back_by, axis=1),
                pltpu.roll(far, back_by, axis=1),
            )
            turned = pltpu.roll(turned.reshape(tall // 8, 8, width), up_by, axis=1)
            picked = jnp.where(sublane[1:] < 8 - down, turned[:-1], turned[1:])
            return picked.reshape(width, width)

        def paste(plane, values):
            turned = pltpu.roll(values, shift, axis=1).reshape(width // 8, 8, width)
            turned = pltpu.roll(turned, down, axis=1)
            blank = jnp.zeros((1, 8, width), jnp.float32)
            moved = jnp.where(
                sublane >= down,
                jnp.concatenate([turned, blank], axis=0),
                jnp.concatenate([blank, turned], axis=0),
            ).reshape(tall, width)
            grad_ref[plane, pl.ds(top, tall), pl.ds(base, width)] += jnp.where(
                lane >= shift, moved, 0.0
            )
            grad_ref[plane, pl.ds(top, tall), pl.ds(base + width, width)] += jnp.where(
                lane < shift, moved, 0.0
            )

        patch_real, patch_imag = (cut(0), cut(1))
        exits = []
        for mode in range(2):
            mode_real, mode_imag = (probe_ref[0, mode], probe_ref[1, mode])
            exits.append(
                jnp.concatenate(
                    [
                        mode_real * patch_real - mode_imag * patch_imag,
                        mode_real * patch_imag + mode_imag * patch_real,
                    ],
                    axis=1,
                )
            )
        rows = times_right(jnp.concatenate(exits, axis=0), right_table_ref[...])
        columns = jnp.concatenate(
            [
                jnp.concatenate([rows[:width, :width], rows[width:, :width]], axis=1),
                jnp.concatenate([rows[:width, width:], rows[width:, width:]], axis=1),
            ],
            axis=0,
        )
        far = times_left(left_table_ref[...], columns)
        power = far * far
        power = power[:width] + power[width:]
        intensity = power[:, :width] + power[:, width:]
        scaling = (
            measured_ref[index] * lax.rsqrt(jnp.maximum(intensity, AMP_FLOOR * AMP_FLOOR)) - 1.0
        )
        scaling = jnp.concatenate([scaling, scaling], axis=1)
        scaling = jnp.concatenate([scaling, scaling], axis=0)
        rows = times_left(back_left_ref[...], far * scaling)
        columns = jnp.concatenate(
            [
                jnp.concatenate([rows[:width, :width], rows[width:, :width]], axis=1),
                jnp.concatenate([rows[:width, width:], rows[width:, width:]], axis=1),
            ],
            axis=0,
        )
        back = times_right(columns, back_right_ref[...])
        object_real = jnp.zeros((width, width), jnp.float32)
        object_imag = jnp.zeros((width, width), jnp.float32)
        for mode in range(2):
            mode_real, mode_imag = (probe_ref[0, mode], probe_ref[1, mode])
            back_real = back[mode * width : (mode + 1) * width, :width]
            back_imag = back[mode * width : (mode + 1) * width, width:]
            object_real += mode_real * back_real + mode_imag * back_imag
            object_imag += mode_real * back_imag - mode_imag * back_real
            sums_ref[0, mode] += patch_real * back_real + patch_imag * back_imag
            sums_ref[1, mode] += patch_real * back_imag - patch_imag * back_real
        sums_ref[2, 0] += patch_real * patch_real + patch_imag * patch_imag
        paste(0, object_real)
        paste(1, object_imag)
        return carry

    lax.fori_loop(0, counts_ref[0], slot, 0)
    grad_own_ref[...] = grad_ref[:, :tile_height, :tile_width]
    grad_lower_ref[...] = grad_ref[:, tile_height:, :tile_width]
    grad_right_ref[...] = grad_ref[:, :, tile_width:]
    for block in range(packed_ref.shape[0]):
        part, mode, start = (block // 16, block // 8 % 2, block % 8 * 16)
        packed_ref[block, :16] = sums_ref[part, mode, start : start + 16]
        packed_ref[block, 16:] = sums_ref[2, 0, block * 4 : block * 4 + 4]


def process(positions, counts, own, below, right, corner, probe, measured):
    vmem = pl.BlockSpec(memory_space=pltpu.VMEM)
    smem = pl.BlockSpec(memory_space=pltpu.SMEM)
    tile_height, tile_width = own.shape[1:]
    tables = [jnp.asarray(t) for t in fourier_matrices(PATCH)]
    full = lambda *shape: jax.ShapeDtypeStruct(shape, jnp.float32)
    return pl.pallas_call(
        patch_kernel,
        in_specs=[smem, smem] + [vmem] * 10,
        out_specs=[vmem] * 4,
        out_shape=[
            full(2, tile_height, tile_width),
            full(2, tile_height + PATCH, PATCH),
            full(2, PATCH, tile_width),
            full(32, 20, PATCH),
        ],
        scratch_shapes=[
            pltpu.VMEM((2, tile_height + PATCH, tile_width + PATCH), jnp.float32),
            pltpu.VMEM((2, tile_height + PATCH, tile_width + PATCH), jnp.float32),
            pltpu.VMEM((3, 2, PATCH, PATCH), jnp.float32),
        ],
        compiler_params=pltpu.CompilerParams(vmem_limit_bytes=48 * 1024 * 1024),
        name="patches",
    )(positions, counts, own, below, right, corner, probe, measured, *tables)


def sum_over_all(blocks):
    planes, lines = device_groups(lax.axis_size("row") * lax.axis_size("col"))
    own = jnp.sum(exchange(blocks, planes), axis=0)
    own = jnp.sum(exchange(jnp.broadcast_to(own[None], (len(lines[0]), *own.shape)), lines), axis=0)
    return exchange(jnp.broadcast_to(own[None], blocks.shape), planes)


def per_device(object_field, probe_modes, measured, positions, counts):
    tile_height, tile_width = (object_field.shape[1], object_field.shape[2])
    below = shifted(object_field[:, :PATCH, :], "row", -1)
    right = shifted(object_field[:, :, :PATCH], "col", -1)
    corner = shifted(below[:, :, :PATCH], "col", -1)
    grad_own, grad_right, grad_lower, packed = process(
        positions[0, 0], counts[0], object_field, below, right, corner, probe_modes, measured[0, 0]
    )
    spilled = shifted(grad_right, "col", 1)
    rim = shifted(
        grad_lower.at[:, :, :PATCH].add(spilled[:, tile_height:]), "row", 1
    )
    own_part = (
        grad_own.at[:, :, :PATCH].add(spilled[:, :tile_height]).at[:, :PATCH, :].add(rim)
    )
    peak_power = jnp.max(jnp.sum(probe_modes * probe_modes, axis=(0, 1)))
    object_new = object_field + own_part / (peak_power + 1e-06)
    totals = sum_over_all(packed)
    probe_sum = totals[:, :16].reshape(probe_modes.shape)
    density_sum = totals[:, 16:].reshape(PATCH, PATCH)
    probe_step = probe_sum / jnp.sqrt(density_sum + 1.0)[None, None]
    return (object_new, probe_step)


def solution(mesh):
    in_specs = (
        P(None, "row", "col"),
        P(),
        P("row", "col", None, None, None),
        P("row", "col", None, None),
        P("row", "col"),
    )
    out_specs = (P(None, "row", "col"), P())
    return jax.shard_map(
        per_device, mesh=mesh, in_specs=in_specs, out_specs=out_specs, check_vma=False
    )
```

```python
import math

import jax
import jax.numpy as jnp
import numpy as np
from jax import lax
from jax.experimental import pallas as pl
from jax.experimental.pallas import tpu as pltpu
from jax.sharding import PartitionSpec as P

AMP_FLOOR = 0.25
PATCH = 128


def shifted(array, axis, by):
    length = lax.axis_size(axis)
    pairs = [(i, i + by) for i in range(length) if 0 <= i + by < length]
    return lax.ppermute(array, axis, pairs)


def coordinates(device):
    row, col = divmod(device, 32)
    z_hi, x = divmod(row, 4)
    z_lo, rest = divmod(col, 8)
    y, core = divmod(rest, 2)
    return (z_hi * 4 + z_lo, x, y, core)


def device_groups(devices):
    planes, lines = {}, {}
    for device in range(devices):
        z, x, y, core = coordinates(device)
        planes.setdefault(z, []).append(device)
        lines.setdefault((x, y, core), []).append(device)
    return (list(planes.values()), list(lines.values()))


def exchange(blocks, groups):
    return lax.all_to_all(blocks, ("row", "col"), 0, 0, axis_index_groups=groups)


def split(values):
    high = values.astype(jnp.bfloat16)
    low = (values - high.astype(jnp.float32)).astype(jnp.bfloat16)
    return (high, low)


def fourier_parts(width):
    index = np.arange(width)
    angle = (index[:, None] * index[None, :] % width) * (2.0 * math.pi / width)
    parts = []
    for wave in (np.cos(angle), np.sin(angle)):
        values = (wave / math.sqrt(width)).astype(np.float32)
        high = values.astype(jnp.bfloat16)
        parts += [high, (values - high.astype(np.float32)).astype(jnp.bfloat16)]
    return np.stack(parts)


def fill_tables(parts_ref, table_refs):
    width = parts_ref.shape[-1]
    right_ref, left_ref, back_left_ref, back_right_ref = table_refs
    for level, places in ((0, (0, 2)), (1, (1,))):
        cosine = parts_ref[level]
        sine = parts_ref[2 + level]
        for place in places:
            start = place * 2 * width
            for i in range(2):
                for j in range(2):
                    value = cosine if i == j else (-sine if i == 0 else sine)
                    turned = cosine if i == j else (sine if i == 0 else -sine)
                    tall = (slice(start + i * width, start + (i + 1) * width), slice(j * width, (j + 1) * width))
                    wide = (slice(i * width, (i + 1) * width), slice(start + j * width, start + (j + 1) * width))
                    right_ref[tall] = value
                    back_right_ref[tall] = turned
                    left_ref[wide] = turned
                    back_left_ref[wide] = value


def times_right(values, table):
    high, low = split(values)
    return jnp.dot(
        jnp.concatenate([high, high, low], axis=1), table, preferred_element_type=jnp.float32
    )


def times_left(table, values):
    high, low = split(values)
    return jnp.dot(
        table, jnp.concatenate([high, high, low], axis=0), preferred_element_type=jnp.float32
    )


def regroup(values, width):
    blocks = values.shape[0] // width
    return jnp.concatenate(
        [
            jnp.concatenate(
                [values[b * width : (b + 1) * width, p * width : (p + 1) * width] for b in range(blocks)],
                axis=1,
            )
            for p in range(2)
        ],
        axis=0,
    )


def ungroup(values, width):
    blocks = values.shape[1] // width
    return jnp.concatenate(
        [
            jnp.concatenate(
                [values[p * width : (p + 1) * width, b * width : (b + 1) * width] for p in range(2)],
                axis=1,
            )
            for b in range(blocks)
        ],
        axis=0,
    )


def make_slots(positions_ref, first_row, field_ref, grad_ref, probe_ref, measured_ref, sums_ref, table_refs):
    width = PATCH
    modes = probe_ref.shape[1]
    tall = width + 8
    right_table, left_table, back_left, back_right = table_refs
    lane = lax.broadcasted_iota(jnp.int32, (tall, width), 1)
    sublane = lax.broadcasted_iota(jnp.int32, (tall // 8, 8, width), 1)

    def place(index):
        row = positions_ref[0, index] - first_row
        col = positions_ref[1, index]
        down = lax.rem(row, 8)
        shift = lax.rem(col, width)
        return (pl.multiple_of(row - down, 8), down, pl.multiple_of(col - shift, width), shift)

    def cut(plane, top, down, base, shift):
        near = field_ref[plane, pl.ds(top, tall), pl.ds(base, width)]
        far = field_ref[plane, pl.ds(top, tall), pl.ds(base + width, width)]
        back_by = lax.rem(width - shift, width)
        turned = jnp.where(
            lane < width - shift,
            pltpu.roll(near, back_by, axis=1),
            pltpu.roll(far, back_by, axis=1),
        )
        turned = pltpu.roll(turned.reshape(tall // 8, 8, width), lax.rem(8 - down, 8), axis=1)
        picked = jnp.where(sublane[1:] < 8 - down, turned[:-1], turned[1:])
        return picked.reshape(width, width)

    def paste(plane, top, down, base, shift, values):
        turned = pltpu.roll(values, shift, axis=1).reshape(width // 8, 8, width)
        turned = pltpu.roll(turned, down, axis=1)
        blank = jnp.zeros((1, 8, width), jnp.float32)
        moved = jnp.where(
            sublane >= down,
            jnp.concatenate([turned, blank], axis=0),
            jnp.concatenate([blank, turned], axis=0),
        ).reshape(tall, width)
        grad_ref[plane, pl.ds(top, tall), pl.ds(base, width)] += jnp.where(
            lane >= shift, moved, 0.0
        )
        grad_ref[plane, pl.ds(top, tall), pl.ds(base + width, width)] += jnp.where(
            lane < shift, moved, 0.0
        )

    def slots(indices):
        places = [place(index) for index in indices]
        patches = [(cut(0, *at), cut(1, *at)) for at in places]
        exits = []
        for patch_real, patch_imag in patches:
            for mode in range(modes):
                mode_real, mode_imag = (probe_ref[0, mode], probe_ref[1, mode])
                exits.append(
                    jnp.concatenate(
                        [
                            mode_real * patch_real - mode_imag * patch_imag,
                            mode_real * patch_imag + mode_imag * patch_real,
                        ],
                        axis=1,
                    )
                )
        rows = times_right(jnp.concatenate(exits, axis=0), right_table[...])
        far = times_left(left_table[...], regroup(rows, width))
        scalings = []
        for order, index in enumerate(indices):
            part = far[:, order * modes * width : (order + 1) * modes * width]
            power = part * part
            power = power[:width] + power[width:]
            intensity = sum(power[:, m * width : (m + 1) * width] for m in range(modes))
            scaling = (
                measured_ref[index] * lax.rsqrt(jnp.maximum(intensity, AMP_FLOOR * AMP_FLOOR)) - 1.0
            )
            scalings += [scaling] * modes
        scaling = jnp.concatenate(scalings, axis=1)
        rows = times_left(back_left[...], far * jnp.concatenate([scaling, scaling], axis=0))
        back = times_right(ungroup(rows, width), back_right[...])
        sums = [[0.0] * modes, [0.0] * modes]
        density = 0.0
        for order, (patch_real, patch_imag) in enumerate(patches):
            object_real, object_imag = (0.0, 0.0)
            for mode in range(modes):
                mode_real, mode_imag = (probe_ref[0, mode], probe_ref[1, mode])
                start = (order * modes + mode) * width
                back_real = back[start : start + width, :width]
                back_imag = back[start : start + width, width:]
                object_real += mode_real * back_real + mode_imag * back_imag
                object_imag += mode_real * back_imag - mode_imag * back_real
                sums[0][mode] += patch_real * back_real + patch_imag * back_imag
                sums[1][mode] += patch_real * back_imag - patch_imag * back_real
            density += patch_real * patch_real + patch_imag * patch_imag
            paste(0, *places[order], object_real)
            paste(1, *places[order], object_imag)
        for part in range(2):
            for mode in range(modes):
                sums_ref[part, mode] += sums[part][mode]
        sums_ref[2, 0] += density

    return slots


def run_slots(positions_ref, counts_ref, order_ref, slots, wanted):

    def note(index, found):
        order_ref[found] = index
        return found + wanted(positions_ref[0, index]).astype(jnp.int32)

    found = lax.fori_loop(0, counts_ref[0], note, jnp.int32(0))

    def run(start, stop, size):

        def step(turn, carry):
            slots([order_ref[start + turn * size + i] for i in range(size)])
            return carry

        turns = lax.div(stop - start, size)
        lax.fori_loop(0, turns, step, 0)
        return start + turns * size

    reached = run(0, found, 4)
    reached = run(reached, found, 2)
    run(reached, found, 1)


def upper_kernel(
    positions_ref, counts_ref, own_ref, right_ref, probe_ref, measured_ref, parts_ref,
    grad_ref, sums_ref, field_ref, order_ref, *table_refs,
):
    tile_height, tile_width = own_ref.shape[1:]
    fill_tables(parts_ref, table_refs)
    field_ref[:, :tile_height, :tile_width] = own_ref[...]
    field_ref[:, :tile_height, tile_width:] = right_ref[...]
    grad_ref[...] = jnp.zeros_like(grad_ref)
    sums_ref[...] = jnp.zeros_like(sums_ref)
    slots = make_slots(positions_ref, 0, field_ref, grad_ref, probe_ref, measured_ref, sums_ref, table_refs)
    run_slots(positions_ref, counts_ref, order_ref, slots, lambda row: row <= tile_height - PATCH)


def lower_kernel(
    positions_ref, counts_ref, own_ref, below_ref, right_ref, corner_ref, probe_ref, measured_ref,
    parts_ref, upper_ref, upper_sums_ref, grad_own_ref, grad_right_ref, grad_lower_ref, packed_ref,
    field_ref, grad_ref, sums_ref, order_ref, *table_refs,
):
    tile_height, tile_width = own_ref.shape[1:]
    first = tile_height - PATCH
    fill_tables(parts_ref, table_refs)
    field_ref[:, :PATCH, :tile_width] = own_ref[:, first:]
    field_ref[:, PATCH:, :tile_width] = below_ref[...]
    field_ref[:, :PATCH, tile_width:] = right_ref[:, first:]
    field_ref[:, PATCH:, tile_width:] = corner_ref[...]
    grad_ref[:, :PATCH] = upper_ref[:, first:tile_height]
    grad_ref[:, PATCH:] = jnp.zeros_like(grad_ref[:, PATCH:])
    sums_ref[...] = upper_sums_ref[...]
    slots = make_slots(positions_ref, first, field_ref, grad_ref, probe_ref, measured_ref, sums_ref, table_refs)
    run_slots(positions_ref, counts_ref, order_ref, slots, lambda row: row > first)
    for block in range(packed_ref.shape[0]):
        part, mode, start = (block // 16, block // 8 % 2, block % 8 * 16)
        packed_ref[block, :16] = sums_ref[part, mode, start : start + 16]
        packed_ref[block, 16:] = sums_ref[2, 0, block * 4 : block * 4 + 4]
    grad_right_ref[:, :first] = upper_ref[:, :first, tile_width:]
    grad_right_ref[:, first:] = grad_ref[:, :, tile_width:]
    grad_own_ref[...] = grad_ref[:, :PATCH, :tile_width]
    grad_lower_ref[...] = grad_ref[:, PATCH:, :tile_width]


def float_array(*shape):
    return jax.ShapeDtypeStruct(shape, jnp.float32)


def table_scratch():
    tall = pltpu.VMEM((6 * PATCH, 2 * PATCH), jnp.bfloat16)
    wide = pltpu.VMEM((2 * PATCH, 6 * PATCH), jnp.bfloat16)
    return [tall, wide, wide, tall]


VMEM_SPEC = pl.BlockSpec(memory_space=pltpu.VMEM)
SMEM_SPEC = pl.BlockSpec(memory_space=pltpu.SMEM)
PARAMS = pltpu.CompilerParams(vmem_limit_bytes=48 * 1024 * 1024)


def upper_slots(positions, counts, own, right, probe, measured, parts):
    tile_height, tile_width = own.shape[1:]
    wide = tile_width + PATCH
    return pl.pallas_call(
        upper_kernel,
        in_specs=[SMEM_SPEC] * 2 + [VMEM_SPEC] * 5,
        out_specs=[VMEM_SPEC] * 2,
        out_shape=[float_array(2, tile_height + 8, wide), float_array(3, 2, PATCH, PATCH)],
        scratch_shapes=[
            pltpu.VMEM((2, tile_height + 8, wide), jnp.float32),
            pltpu.SMEM((positions.shape[1],), jnp.int32),
        ]
        + table_scratch(),
        compiler_params=PARAMS,
        cost_estimate=pl.CostEstimate(flops=3_000_000_000, transcendentals=0, bytes_accessed=3_000_000),
        name="upper_slots",
    )(positions, counts, own, right, probe, measured, parts)


def lower_slots(positions, counts, own, below, right, corner, probe, measured, parts, upper, sums):
    tile_height, tile_width = own.shape[1:]
    wide = tile_width + PATCH
    return pl.pallas_call(
        lower_kernel,
        in_specs=[SMEM_SPEC] * 2 + [VMEM_SPEC] * 9,
        out_specs=[VMEM_SPEC] * 4,
        out_shape=[
            float_array(2, PATCH, tile_width),
            float_array(2, tile_height + PATCH, PATCH),
            float_array(2, PATCH, tile_width),
            float_array(32, 20, PATCH),
        ],
        scratch_shapes=[
            pltpu.VMEM((2, 2 * PATCH, wide), jnp.float32),
            pltpu.VMEM((2, 2 * PATCH, wide), jnp.float32),
            pltpu.VMEM((3, 2, PATCH, PATCH), jnp.float32),
            pltpu.SMEM((positions.shape[1],), jnp.int32),
        ]
        + table_scratch(),
        compiler_params=PARAMS,
        cost_estimate=pl.CostEstimate(flops=3_000_000_000, transcendentals=0, bytes_accessed=5_000_000),
        name="lower_slots",
    )(positions, counts, own, below, right, corner, probe, measured, parts, upper, sums)


def object_kernel(own_ref, upper_ref, lower_ref, spilled_ref, rim_ref, probe_ref, out_ref):
    tile_height, tile_width = own_ref.shape[1:]
    first = tile_height - PATCH
    power = probe_ref[...] * probe_ref[...]
    power = power[0, 0] + power[0, 1] + power[1, 0] + power[1, 1]
    weight = 1.0 / (jnp.max(power, axis=(0, 1), keepdims=True) + 1e-06)
    for plane in range(2):
        for start in range(0, tile_height, PATCH):
            for side in range(0, tile_width, PATCH):
                rows, cols = (slice(start, start + PATCH), slice(side, side + PATCH))
                if start < first:
                    total = upper_ref[plane, rows, cols]
                else:
                    total = lower_ref[plane, :, cols]
                if side == 0:
                    total += spilled_ref[plane, rows, :]
                if start == 0:
                    total += rim_ref[plane, :, cols]
                out_ref[plane, rows, cols] = own_ref[plane, rows, cols] + total * weight


def object_update(own, upper, lower, spilled, rim, probe):
    return pl.pallas_call(
        object_kernel,
        in_specs=[VMEM_SPEC] * 6,
        out_specs=VMEM_SPEC,
        out_shape=float_array(*own.shape),
        compiler_params=PARAMS,
        cost_estimate=pl.CostEstimate(flops=1_000_000, transcendentals=0, bytes_accessed=4_000_000),
        name="object_update",
    )(own, upper, lower, spilled, rim, probe)


def probe_kernel(blocks_ref, out_ref, density_ref):
    for block in range(blocks_ref.shape[0]):
        density_ref[block * 4 : block * 4 + 4] = blocks_ref[block, 16:]
    weight = lax.rsqrt(density_ref[...] + 1.0)
    for block in range(blocks_ref.shape[0]):
        part, mode, start = (block // 16, block // 8 % 2, block % 8 * 16)
        out_ref[part, mode, start : start + 16] = (
            blocks_ref[block, :16] * weight[start : start + 16]
        )


def probe_update(blocks, shape):
    return pl.pallas_call(
        probe_kernel,
        in_specs=[VMEM_SPEC],
        out_specs=VMEM_SPEC,
        out_shape=float_array(*shape),
        scratch_shapes=[pltpu.VMEM((PATCH, PATCH), jnp.float32)],
        compiler_params=PARAMS,
        name="probe_update",
    )(blocks)


def per_device(object_field, probe_modes, measured, positions, counts):
    tile_height = object_field.shape[1]
    planes, lines = device_groups(lax.axis_size("row") * lax.axis_size("col"))
    places, live, amplitudes = (positions[0, 0], counts[0], measured[0, 0])
    parts = jnp.asarray(fourier_parts(PATCH))
    below = shifted(object_field[:, :PATCH, :], "row", -1)
    right = shifted(object_field[:, :, :PATCH], "col", -1)
    upper, upper_sums = upper_slots(
        places, live, object_field, right, probe_modes, amplitudes, parts
    )
    below, upper_sums = lax.optimization_barrier((below, upper_sums))
    corner = shifted(below[:, :, :PATCH], "col", -1)
    lower, grad_right, grad_lower, packed = lower_slots(
        places, live, object_field, below, right, corner, probe_modes, amplitudes, parts, upper, upper_sums
    )
    spilled = shifted(grad_right, "col", 1)
    terms = exchange(packed, planes)
    terms, spilled = lax.optimization_barrier((terms, spilled))
    rim = grad_lower.at[:, :, :PATCH].add(spilled[:, tile_height:])
    plane_sum = jnp.sum(terms, axis=0)
    plane_sum, rim = lax.optimization_barrier((plane_sum, rim))
    rim = shifted(rim, "row", 1)
    terms = exchange(jnp.broadcast_to(plane_sum[None], (len(lines[0]), *plane_sum.shape)), lines)
    total = jnp.sum(terms, axis=0)
    blocks = exchange(jnp.broadcast_to(total[None], packed.shape), planes)
    object_new = object_update(object_field, upper, lower, spilled, rim, probe_modes)
    probe_step = probe_update(blocks, probe_modes.shape)
    return (object_new, probe_step)


def solution(mesh):
    in_specs = (
        P(None, "row", "col"),
        P(),
        P("row", "col", None, None, None),
        P("row", "col", None, None),
        P("row", "col"),
    )
    out_specs = (P(None, "row", "col"), P())
    return jax.shard_map(
        per_device, mesh=mesh, in_specs=in_specs, out_specs=out_specs, check_vma=False
    )
```

```python
import math

import jax
import jax.numpy as jnp
import numpy as np
from jax import lax
from jax.experimental import pallas as pl
from jax.experimental.pallas import tpu as pltpu
from jax.sharding import PartitionSpec as P

AMP_FLOOR = 0.25
PATCH = 128
RUN = 4
DIRECT = 72


def shifted(array, axis, by):
    length = lax.axis_size(axis)
    pairs = [(i, i + by) for i in range(length) if 0 <= i + by < length]
    return lax.ppermute(array, axis, pairs)


def coordinates(device):
    row, col = divmod(device, 32)
    z_hi, x = divmod(row, 4)
    z_lo, rest = divmod(col, 8)
    y, core = divmod(rest, 2)
    return (z_hi * 4 + z_lo, x, y, core)


def device_groups(devices):
    planes, lines = {}, {}
    for device in range(devices):
        z, x, y, core = coordinates(device)
        planes.setdefault(z, []).append(device)
        lines.setdefault((x, y, core), []).append(device)
    return (list(planes.values()), list(lines.values()))


def exchange(blocks, groups):
    return lax.all_to_all(blocks, ("row", "col"), 0, 0, axis_index_groups=groups)


def split(values):
    high = values.astype(jnp.bfloat16)
    low = (values - high.astype(jnp.float32)).astype(jnp.bfloat16)
    return (high, low)


def fourier_parts(width):
    index = np.arange(width)
    angle = (index[:, None] * index[None, :] % width) * (2.0 * math.pi / width)
    parts = []
    for wave in (np.cos(angle), np.sin(angle)):
        values = (wave / math.sqrt(width)).astype(np.float32)
        high = values.astype(jnp.bfloat16)
        parts += [high, (values - high.astype(np.float32)).astype(jnp.bfloat16)]
    return np.stack(parts)


def fill_tables(parts_ref, table_refs):
    width = parts_ref.shape[-1]
    right_ref, left_ref, back_left_ref, back_right_ref = table_refs
    for level, places in ((0, (0, 2)), (1, (1,))):
        cosine = parts_ref[level]
        sine = parts_ref[2 + level]
        for place in places:
            start = place * 2 * width
            for i in range(2):
                for j in range(2):
                    value = cosine if i == j else (-sine if i == 0 else sine)
                    turned = cosine if i == j else (sine if i == 0 else -sine)
                    tall = (slice(start + i * width, start + (i + 1) * width), slice(j * width, (j + 1) * width))
                    wide = (slice(i * width, (i + 1) * width), slice(start + j * width, start + (j + 1) * width))
                    right_ref[tall] = value
                    back_right_ref[tall] = turned
                    left_ref[wide] = turned
                    back_left_ref[wide] = value


def times_right(values, table):
    high, low = split(values)
    return jnp.dot(
        jnp.concatenate([high, high, low], axis=1), table, preferred_element_type=jnp.float32
    )


def times_left(table, values):
    high, low = split(values)
    return jnp.dot(
        table, jnp.concatenate([high, high, low], axis=0), preferred_element_type=jnp.float32
    )


def regroup(values, width):
    blocks = values.shape[0] // width
    return jnp.concatenate(
        [
            jnp.concatenate(
                [values[b * width : (b + 1) * width, p * width : (p + 1) * width] for b in range(blocks)],
                axis=1,
            )
            for p in range(2)
        ],
        axis=0,
    )


def ungroup(values, width):
    blocks = values.shape[1] // width
    return jnp.concatenate(
        [
            jnp.concatenate(
                [values[p * width : (p + 1) * width, b * width : (b + 1) * width] for p in range(2)],
                axis=1,
            )
            for b in range(blocks)
        ],
        axis=0,
    )


def make_slots(positions_ref, first_row, field_ref, grad_ref, probe_ref, measured_ref, sums_ref, table_refs):
    width = PATCH
    modes = probe_ref.shape[1]
    tall = width + 8
    right_table, left_table, back_left, back_right = table_refs
    lane = lax.broadcasted_iota(jnp.int32, (tall, width), 1)
    sublane = lax.broadcasted_iota(jnp.int32, (tall // 8, 8, width), 1)

    def place(index):
        row = positions_ref[0, index] - first_row
        col = positions_ref[1, index]
        down = lax.rem(row, 8)
        shift = lax.rem(col, width)
        return (pl.multiple_of(row - down, 8), down, pl.multiple_of(col - shift, width), shift)

    def cut(plane, top, down, base, shift):
        near = field_ref[plane, pl.ds(top, tall), pl.ds(base, width)]
        far = field_ref[plane, pl.ds(top, tall), pl.ds(base + width, width)]
        back_by = lax.rem(width - shift, width)
        turned = jnp.where(
            lane < width - shift,
            pltpu.roll(near, back_by, axis=1),
            pltpu.roll(far, back_by, axis=1),
        )
        turned = pltpu.roll(turned.reshape(tall // 8, 8, width), lax.rem(8 - down, 8), axis=1)
        picked = jnp.where(sublane[1:] < 8 - down, turned[:-1], turned[1:])
        return picked.reshape(width, width)

    def paste(plane, top, down, base, shift, values):
        turned = pltpu.roll(values, shift, axis=1).reshape(width // 8, 8, width)
        turned = pltpu.roll(turned, down, axis=1)
        blank = jnp.zeros((1, 8, width), jnp.float32)
        moved = jnp.where(
            sublane >= down,
            jnp.concatenate([turned, blank], axis=0),
            jnp.concatenate([blank, turned], axis=0),
        ).reshape(tall, width)
        grad_ref[plane, pl.ds(top, tall), pl.ds(base, width)] += jnp.where(
            lane >= shift, moved, 0.0
        )
        grad_ref[plane, pl.ds(top, tall), pl.ds(base + width, width)] += jnp.where(
            lane < shift, moved, 0.0
        )

    def slots(indices):
        places = [place(index) for index in indices]
        patches = [(cut(0, *at), cut(1, *at)) for at in places]
        exits = []
        for patch_real, patch_imag in patches:
            for mode in range(modes):
                mode_real, mode_imag = (probe_ref[0, mode], probe_ref[1, mode])
                exits.append(
                    jnp.concatenate(
                        [
                            mode_real * patch_real - mode_imag * patch_imag,
                            mode_real * patch_imag + mode_imag * patch_real,
                        ],
                        axis=1,
                    )
                )
        rows = times_right(jnp.concatenate(exits, axis=0), right_table[...])
        far = times_left(left_table[...], regroup(rows, width))
        scalings = []
        for order, index in enumerate(indices):
            part = far[:, order * modes * width : (order + 1) * modes * width]
            power = part * part
            power = power[:width] + power[width:]
            intensity = sum(power[:, m * width : (m + 1) * width] for m in range(modes))
            scaling = (
                measured_ref[index] * lax.rsqrt(jnp.maximum(intensity, AMP_FLOOR * AMP_FLOOR)) - 1.0
            )
            scalings += [scaling] * modes
        scaling = jnp.concatenate(scalings, axis=1)
        rows = times_left(back_left[...], far * jnp.concatenate([scaling, scaling], axis=0))
        back = times_right(ungroup(rows, width), back_right[...])
        sums = [[0.0] * modes, [0.0] * modes]
        density = 0.0
        for order, (patch_real, patch_imag) in enumerate(patches):
            object_real, object_imag = (0.0, 0.0)
            for mode in range(modes):
                mode_real, mode_imag = (probe_ref[0, mode], probe_ref[1, mode])
                start = (order * modes + mode) * width
                back_real = back[start : start + width, :width]
                back_imag = back[start : start + width, width:]
                object_real += mode_real * back_real + mode_imag * back_imag
                object_imag += mode_real * back_imag - mode_imag * back_real
                sums[0][mode] += patch_real * back_real + patch_imag * back_imag
                sums[1][mode] += patch_real * back_imag - patch_imag * back_real
            density += patch_real * patch_real + patch_imag * patch_imag
            paste(0, *places[order], object_real)
            paste(1, *places[order], object_imag)
        for part in range(2):
            for mode in range(modes):
                sums_ref[part, mode] += sums[part][mode]
        sums_ref[2, 0] += density

    return slots


def run_slots(positions_ref, counts_ref, order_ref, slots, wanted):

    def note(index, found):
        order_ref[found] = index
        return found + wanted(positions_ref[0, index]).astype(jnp.int32)

    found = lax.fori_loop(0, counts_ref[0], note, jnp.int32(0))

    def run(start, stop, size):

        def step(turn, carry):
            slots([order_ref[start + turn * size + i] for i in range(size)])
            return carry

        turns = lax.div(stop - start, size)
        lax.fori_loop(0, turns, step, 0)
        return start + turns * size

    reached = run(0, found, 4)
    reached = run(reached, found, 2)
    run(reached, found, 1)


def upper_kernel(
    positions_ref, counts_ref, own_ref, right_ref, probe_ref, measured_ref, parts_ref,
    grad_ref, sums_ref, field_ref, order_ref, *table_refs,
):
    tile_height, tile_width = own_ref.shape[1:]
    fill_tables(parts_ref, table_refs)
    field_ref[:, :tile_height, :tile_width] = own_ref[...]
    field_ref[:, :tile_height, tile_width:] = right_ref[...]
    grad_ref[...] = jnp.zeros_like(grad_ref)
    sums_ref[...] = jnp.zeros_like(sums_ref)
    slots = make_slots(positions_ref, 0, field_ref, grad_ref, probe_ref, measured_ref, sums_ref, table_refs)
    run_slots(positions_ref, counts_ref, order_ref, slots, lambda row: row <= tile_height - PATCH)


def lower_kernel(
    positions_ref, counts_ref, own_ref, below_ref, right_ref, corner_ref, probe_ref, measured_ref,
    parts_ref, upper_ref, upper_sums_ref, grad_own_ref, grad_right_ref, grad_lower_ref, packed_ref,
    field_ref, grad_ref, sums_ref, order_ref, *table_refs,
):
    tile_height, tile_width = own_ref.shape[1:]
    first = tile_height - PATCH
    fill_tables(parts_ref, table_refs)
    field_ref[:, :PATCH, :tile_width] = own_ref[:, first:]
    field_ref[:, PATCH:, :tile_width] = below_ref[...]
    field_ref[:, :PATCH, tile_width:] = right_ref[:, first:]
    field_ref[:, PATCH:, tile_width:] = corner_ref[...]
    grad_ref[:, :PATCH] = upper_ref[:, first:tile_height]
    grad_ref[:, PATCH:] = jnp.zeros_like(grad_ref[:, PATCH:])
    sums_ref[...] = upper_sums_ref[...]
    slots = make_slots(positions_ref, first, field_ref, grad_ref, probe_ref, measured_ref, sums_ref, table_refs)
    run_slots(positions_ref, counts_ref, order_ref, slots, lambda row: row > first)
    for block in range(packed_ref.shape[0]):
        part, mode, start = (block // 16, block // 8 % 2, block % 8 * 16)
        packed_ref[block, :16] = sums_ref[part, mode, start : start + 16]
        packed_ref[block, 16:] = sums_ref[2, 0, block * 4 : block * 4 + 4]
    grad_right_ref[:, :first] = upper_ref[:, :first, tile_width:]
    grad_right_ref[:, first:] = grad_ref[:, :, tile_width:]
    grad_own_ref[...] = grad_ref[:, :PATCH, :tile_width]
    grad_lower_ref[...] = grad_ref[:, PATCH:, :tile_width]


def float_array(*shape):
    return jax.ShapeDtypeStruct(shape, jnp.float32)


def table_scratch():
    tall = pltpu.VMEM((6 * PATCH, 2 * PATCH), jnp.bfloat16)
    wide = pltpu.VMEM((2 * PATCH, 6 * PATCH), jnp.bfloat16)
    return [tall, wide, wide, tall]


VMEM_SPEC = pl.BlockSpec(memory_space=pltpu.VMEM)
SMEM_SPEC = pl.BlockSpec(memory_space=pltpu.SMEM)
PARAMS = pltpu.CompilerParams(vmem_limit_bytes=24 * 1024 * 1024)


def upper_slots(positions, counts, own, right, probe, measured, parts):
    tile_height, tile_width = own.shape[1:]
    wide = tile_width + PATCH
    return pl.pallas_call(
        upper_kernel,
        in_specs=[SMEM_SPEC] * 2 + [VMEM_SPEC] * 5,
        out_specs=[VMEM_SPEC] * 2,
        out_shape=[float_array(2, tile_height + 8, wide), float_array(3, 2, PATCH, PATCH)],
        scratch_shapes=[
            pltpu.VMEM((2, tile_height + 8, wide), jnp.float32),
            pltpu.SMEM((positions.shape[1],), jnp.int32),
        ]
        + table_scratch(),
        compiler_params=PARAMS,
        cost_estimate=pl.CostEstimate(flops=3_000_000_000, transcendentals=0, bytes_accessed=3_000_000),
        name="upper_slots",
    )(positions, counts, own, right, probe, measured, parts)


def lower_slots(positions, counts, own, below, right, corner, probe, measured, parts, upper, sums):
    tile_height, tile_width = own.shape[1:]
    wide = tile_width + PATCH
    return pl.pallas_call(
        lower_kernel,
        in_specs=[SMEM_SPEC] * 2 + [VMEM_SPEC] * 9,
        out_specs=[VMEM_SPEC] * 4,
        out_shape=[
            float_array(2, PATCH, tile_width),
            float_array(2, tile_height + PATCH, PATCH),
            float_array(2, PATCH, tile_width),
            float_array(32, 20, PATCH),
        ],
        scratch_shapes=[
            pltpu.VMEM((2, 2 * PATCH, wide), jnp.float32),
            pltpu.VMEM((2, 2 * PATCH, wide), jnp.float32),
            pltpu.VMEM((3, 2, PATCH, PATCH), jnp.float32),
            pltpu.SMEM((positions.shape[1],), jnp.int32),
        ]
        + table_scratch(),
        compiler_params=PARAMS,
        cost_estimate=pl.CostEstimate(flops=3_000_000_000, transcendentals=0, bytes_accessed=5_000_000),
        name="lower_slots",
    )(positions, counts, own, below, right, corner, probe, measured, parts, upper, sums)


def object_kernel(own_ref, upper_ref, lower_ref, spilled_ref, rim_ref, probe_ref, out_ref):
    tile_height, tile_width = own_ref.shape[1:]
    first = tile_height - PATCH
    power = probe_ref[...] * probe_ref[...]
    power = power[0, 0] + power[0, 1] + power[1, 0] + power[1, 1]
    weight = 1.0 / (jnp.max(power, axis=(0, 1), keepdims=True) + 1e-06)
    for plane in range(2):
        for start in range(0, tile_height, PATCH):
            for side in range(0, tile_width, PATCH):
                rows, cols = (slice(start, start + PATCH), slice(side, side + PATCH))
                if start < first:
                    total = upper_ref[plane, rows, cols]
                else:
                    total = lower_ref[plane, :, cols]
                if side == 0:
                    total += spilled_ref[plane, rows, :]
                if start == 0:
                    total += rim_ref[plane, :, cols]
                out_ref[plane, rows, cols] = own_ref[plane, rows, cols] + total * weight


def object_update(own, upper, lower, spilled, rim, probe):
    return pl.pallas_call(
        object_kernel,
        in_specs=[VMEM_SPEC] * 6,
        out_specs=VMEM_SPEC,
        out_shape=float_array(*own.shape),
        compiler_params=PARAMS,
        cost_estimate=pl.CostEstimate(flops=30_000_000_000, transcendentals=0, bytes_accessed=4_000_000),
        name="object_update",
    )(own, upper, lower, spilled, rim, probe)


def probe_kernel(blocks_ref, out_ref, density_ref):
    for block in range(blocks_ref.shape[0]):
        density_ref[block * 4 : block * 4 + 4] = blocks_ref[block, 16:]
    weight = lax.rsqrt(density_ref[...] + 1.0)
    for block in range(blocks_ref.shape[0]):
        part, mode, start = (block // 16, block // 8 % 2, block % 8 * 16)
        out_ref[part, mode, start : start + 16] = (
            blocks_ref[block, :16] * weight[start : start + 16]
        )


def probe_update(blocks, shape):
    return pl.pallas_call(
        probe_kernel,
        in_specs=[VMEM_SPEC],
        out_specs=VMEM_SPEC,
        out_shape=float_array(*shape),
        scratch_shapes=[pltpu.VMEM((PATCH, PATCH), jnp.float32)],
        compiler_params=PARAMS,
        name="probe_update",
    )(blocks)


def moved(array, where):
    pairs = []
    for device in range(lax.axis_size("row") * lax.axis_size("col")):
        row, col = divmod(device, lax.axis_size("col"))
        target = where(row)
        if target is not None:
            pairs.append((device, target * lax.axis_size("col") + col))
    return lax.ppermute(array, ("row", "col"), pairs)


def side_row(row):
    return row // RUN * RUN + (row - 1) % RUN


def far_row(row):
    return row - RUN if row % RUN == RUN - 1 and row >= RUN else None


def per_device(object_field, probe_modes, measured, positions, counts):
    tile_height = object_field.shape[1]
    planes, lines = device_groups(lax.axis_size("row") * lax.axis_size("col"))
    places, live, amplitudes = (positions[0, 0], counts[0], measured[0, 0])
    parts = jnp.asarray(fourier_parts(PATCH))
    side = moved(object_field[:, DIRECT:PATCH, :], side_row)
    direct = shifted(object_field[:, :DIRECT, :], "row", -1)
    left_columns, side = lax.optimization_barrier((object_field[:, :, :PATCH], side))
    far = moved(side, far_row)
    right = shifted(left_columns, "col", -1)
    upper, upper_sums = upper_slots(
        places, live, object_field, right, probe_modes, amplitudes, parts
    )
    direct, side, far, upper_sums = lax.optimization_barrier((direct, side, far, upper_sums))
    last = lax.axis_index("row") % RUN == RUN - 1
    below = jnp.concatenate([direct, jnp.where(last, far, side)], axis=1)
    corner = shifted(below[:, :, :PATCH], "col", -1)
    lower, grad_right, grad_lower, packed = lower_slots(
        places, live, object_field, below, right, corner, probe_modes, amplitudes, parts, upper, upper_sums
    )
    spilled = shifted(grad_right, "col", 1)
    terms = exchange(packed, planes)
    terms, spilled = lax.optimization_barrier((terms, spilled))
    rim = grad_lower.at[:, :, :PATCH].add(spilled[:, tile_height:])
    plane_sum = jnp.sum(terms, axis=0)
    plane_sum, rim = lax.optimization_barrier((plane_sum, rim))
    rim = shifted(rim, "row", 1)
    terms = exchange(jnp.broadcast_to(plane_sum[None], (len(lines[0]), *plane_sum.shape)), lines)
    total = jnp.sum(terms, axis=0)
    blocks = exchange(jnp.broadcast_to(total[None], packed.shape), planes)
    object_new = object_update(object_field, upper, lower, spilled, rim, probe_modes)
    probe_step = probe_update(blocks, probe_modes.shape)
    return (object_new, probe_step)


def solution(mesh):
    in_specs = (
        P(None, "row", "col"),
        P(),
        P("row", "col", None, None, None),
        P("row", "col", None, None),
        P("row", "col"),
    )
    out_specs = (P(None, "row", "col"), P())
    return jax.shard_map(
        per_device, mesh=mesh, in_specs=in_specs, out_specs=out_specs, check_vma=False
    )
```

```python
import math

import jax
import jax.numpy as jnp
import numpy as np
from jax import lax
from jax.experimental import pallas as pl
from jax.experimental.pallas import tpu as pltpu
from jax.sharding import PartitionSpec as P

AMP_FLOOR = 0.25
PATCH = 128
RUN = 4
DIRECT = 72
RIM_COST = 10_000_000_000
OBJECT_COST = 30_000_000_000


def shifted(array, axis, by):
    length = lax.axis_size(axis)
    pairs = [(i, i + by) for i in range(length) if 0 <= i + by < length]
    return lax.ppermute(array, axis, pairs)


def coordinates(device):
    row, col = divmod(device, 32)
    z_hi, x = divmod(row, 4)
    z_lo, rest = divmod(col, 8)
    y, core = divmod(rest, 2)
    return (z_hi * 4 + z_lo, x, y, core)


def device_groups(devices):
    planes, lines = {}, {}
    for device in range(devices):
        z, x, y, core = coordinates(device)
        planes.setdefault(z, []).append(device)
        lines.setdefault((x, y, core), []).append(device)
    return (list(planes.values()), list(lines.values()))


def exchange(blocks, groups):
    return lax.all_to_all(blocks, ("row", "col"), 0, 0, axis_index_groups=groups)


def split(values):
    high = values.astype(jnp.bfloat16)
    low = (values - high.astype(jnp.float32)).astype(jnp.bfloat16)
    return (high, low)


def fourier_parts(width):
    index = np.arange(width)
    angle = (index[:, None] * index[None, :] % width) * (2.0 * math.pi / width)
    parts = []
    for wave in (np.cos(angle), np.sin(angle)):
        values = (wave / math.sqrt(width)).astype(np.float32)
        high = values.astype(jnp.bfloat16)
        parts += [high, (values - high.astype(np.float32)).astype(jnp.bfloat16)]
    return np.stack(parts)


def fill_tables(parts_ref, table_refs):
    width = parts_ref.shape[-1]
    right_ref, left_ref, back_left_ref, back_right_ref = table_refs
    for level, places in ((0, (0, 2)), (1, (1,))):
        cosine = parts_ref[level]
        sine = parts_ref[2 + level]
        for place in places:
            start = place * 2 * width
            for i in range(2):
                for j in range(2):
                    value = cosine if i == j else (-sine if i == 0 else sine)
                    turned = cosine if i == j else (sine if i == 0 else -sine)
                    tall = (slice(start + i * width, start + (i + 1) * width), slice(j * width, (j + 1) * width))
                    wide = (slice(i * width, (i + 1) * width), slice(start + j * width, start + (j + 1) * width))
                    right_ref[tall] = value
                    back_right_ref[tall] = turned
                    left_ref[wide] = turned
                    back_left_ref[wide] = value


def times_right(values, table):
    high, low = split(values)
    return jnp.dot(
        jnp.concatenate([high, high, low], axis=1), table, preferred_element_type=jnp.float32
    )


def times_left(table, values):
    high, low = split(values)
    return jnp.dot(
        table, jnp.concatenate([high, high, low], axis=0), preferred_element_type=jnp.float32
    )


def regroup(values, width):
    blocks = values.shape[0] // width
    return jnp.concatenate(
        [
            jnp.concatenate(
                [values[b * width : (b + 1) * width, p * width : (p + 1) * width] for b in range(blocks)],
                axis=1,
            )
            for p in range(2)
        ],
        axis=0,
    )


def ungroup(values, width):
    blocks = values.shape[1] // width
    return jnp.concatenate(
        [
            jnp.concatenate(
                [values[p * width : (p + 1) * width, b * width : (b + 1) * width] for p in range(2)],
                axis=1,
            )
            for b in range(blocks)
        ],
        axis=0,
    )


def make_slots(positions_ref, first_row, field_ref, grad_ref, probe_ref, measured_ref, sums_ref, table_refs):
    width = PATCH
    modes = probe_ref.shape[1]
    tall = width + 8
    right_table, left_table, back_left, back_right = table_refs
    lane = lax.broadcasted_iota(jnp.int32, (tall, width), 1)
    sublane = lax.broadcasted_iota(jnp.int32, (tall // 8, 8, width), 1)

    def place(index):
        row = positions_ref[0, index] - first_row
        col = positions_ref[1, index]
        down = lax.rem(row, 8)
        shift = lax.rem(col, width)
        return (pl.multiple_of(row - down, 8), down, pl.multiple_of(col - shift, width), shift)

    def cut(plane, top, down, base, shift):
        near = field_ref[plane, pl.ds(top, tall), pl.ds(base, width)]
        far = field_ref[plane, pl.ds(top, tall), pl.ds(base + width, width)]
        back_by = lax.rem(width - shift, width)
        turned = jnp.where(
            lane < width - shift,
            pltpu.roll(near, back_by, axis=1),
            pltpu.roll(far, back_by, axis=1),
        )
        turned = pltpu.roll(turned.reshape(tall // 8, 8, width), lax.rem(8 - down, 8), axis=1)
        picked = jnp.where(sublane[1:] < 8 - down, turned[:-1], turned[1:])
        return picked.reshape(width, width)

    def paste(plane, top, down, base, shift, values):
        turned = pltpu.roll(values, shift, axis=1).reshape(width // 8, 8, width)
        turned = pltpu.roll(turned, down, axis=1)
        blank = jnp.zeros((1, 8, width), jnp.float32)
        moved = jnp.where(
            sublane >= down,
            jnp.concatenate([turned, blank], axis=0),
            jnp.concatenate([blank, turned], axis=0),
        ).reshape(tall, width)
        grad_ref[plane, pl.ds(top, tall), pl.ds(base, width)] += jnp.where(
            lane >= shift, moved, 0.0
        )
        grad_ref[plane, pl.ds(top, tall), pl.ds(base + width, width)] += jnp.where(
            lane < shift, moved, 0.0
        )

    def slots(indices):
        places = [place(index) for index in indices]
        patches = [(cut(0, *at), cut(1, *at)) for at in places]
        exits = []
        for patch_real, patch_imag in patches:
            for mode in range(modes):
                mode_real, mode_imag = (probe_ref[0, mode], probe_ref[1, mode])
                exits.append(
                    jnp.concatenate(
                        [
                            mode_real * patch_real - mode_imag * patch_imag,
                            mode_real * patch_imag + mode_imag * patch_real,
                        ],
                        axis=1,
                    )
                )
        rows = times_right(jnp.concatenate(exits, axis=0), right_table[...])
        far = times_left(left_table[...], regroup(rows, width))
        scalings = []
        for order, index in enumerate(indices):
            part = far[:, order * modes * width : (order + 1) * modes * width]
            power = part * part
            power = power[:width] + power[width:]
            intensity = sum(power[:, m * width : (m + 1) * width] for m in range(modes))
            scaling = (
                measured_ref[index] * lax.rsqrt(jnp.maximum(intensity, AMP_FLOOR * AMP_FLOOR)) - 1.0
            )
            scalings += [scaling] * modes
        scaling = jnp.concatenate(scalings, axis=1)
        rows = times_left(back_left[...], far * jnp.concatenate([scaling, scaling], axis=0))
        back = times_right(ungroup(rows, width), back_right[...])
        sums = [[0.0] * modes, [0.0] * modes]
        density = 0.0
        for order, (patch_real, patch_imag) in enumerate(patches):
            object_real, object_imag = (0.0, 0.0)
            for mode in range(modes):
                mode_real, mode_imag = (probe_ref[0, mode], probe_ref[1, mode])
                start = (order * modes + mode) * width
                back_real = back[start : start + width, :width]
                back_imag = back[start : start + width, width:]
                object_real += mode_real * back_real + mode_imag * back_imag
                object_imag += mode_real * back_imag - mode_imag * back_real
                sums[0][mode] += patch_real * back_real + patch_imag * back_imag
                sums[1][mode] += patch_real * back_imag - patch_imag * back_real
            density += patch_real * patch_real + patch_imag * patch_imag
            paste(0, *places[order], object_real)
            paste(1, *places[order], object_imag)
        for part in range(2):
            for mode in range(modes):
                sums_ref[part, mode] += sums[part][mode]
        sums_ref[2, 0] += density

    return slots


def run_slots(positions_ref, counts_ref, order_ref, slots, wanted):

    def note(index, found):
        order_ref[found] = index
        return found + wanted(positions_ref[0, index]).astype(jnp.int32)

    found = lax.fori_loop(0, counts_ref[0], note, jnp.int32(0))

    def run(start, stop, size):

        def step(turn, carry):
            slots([order_ref[start + turn * size + i] for i in range(size)])
            return carry

        turns = lax.div(stop - start, size)
        lax.fori_loop(0, turns, step, 0)
        return start + turns * size

    reached = run(0, found, 4)
    reached = run(reached, found, 2)
    run(reached, found, 1)


def upper_kernel(
    positions_ref, counts_ref, own_ref, right_ref, probe_ref, measured_ref, parts_ref,
    grad_ref, sums_ref, field_ref, order_ref, *table_refs,
):
    tile_height, tile_width = own_ref.shape[1:]
    fill_tables(parts_ref, table_refs)
    field_ref[:, :tile_height, :tile_width] = own_ref[...]
    field_ref[:, :tile_height, tile_width:] = right_ref[...]
    grad_ref[...] = jnp.zeros_like(grad_ref)
    sums_ref[...] = jnp.zeros_like(sums_ref)
    slots = make_slots(positions_ref, 0, field_ref, grad_ref, probe_ref, measured_ref, sums_ref, table_refs)
    run_slots(positions_ref, counts_ref, order_ref, slots, lambda row: row <= tile_height - PATCH)


def lower_kernel(
    positions_ref, counts_ref, own_ref, below_ref, right_ref, corner_ref, probe_ref, measured_ref,
    parts_ref, upper_ref, upper_sums_ref, grad_own_ref, grad_right_ref, grad_lower_ref, packed_ref,
    field_ref, grad_ref, sums_ref, order_ref, *table_refs,
):
    tile_height, tile_width = own_ref.shape[1:]
    first = tile_height - PATCH
    fill_tables(parts_ref, table_refs)
    field_ref[:, :PATCH, :tile_width] = own_ref[:, first:]
    field_ref[:, PATCH:, :tile_width] = below_ref[...]
    field_ref[:, :PATCH, tile_width:] = right_ref[:, first:]
    field_ref[:, PATCH:, tile_width:] = corner_ref[...]
    grad_ref[:, :PATCH] = upper_ref[:, first:tile_height]
    grad_ref[:, PATCH:] = jnp.zeros_like(grad_ref[:, PATCH:])
    sums_ref[...] = upper_sums_ref[...]
    slots = make_slots(positions_ref, first, field_ref, grad_ref, probe_ref, measured_ref, sums_ref, table_refs)
    run_slots(positions_ref, counts_ref, order_ref, slots, lambda row: row > first)
    for block in range(packed_ref.shape[0]):
        part, mode, start = (block // 16, block // 8 % 2, block % 8 * 16)
        packed_ref[block, :16] = sums_ref[part, mode, start : start + 16]
        packed_ref[block, 16:] = sums_ref[2, 0, block * 4 : block * 4 + 4]
    grad_right_ref[:, :first] = upper_ref[:, :first, tile_width:]
    grad_right_ref[:, first:] = grad_ref[:, :, tile_width:]
    grad_own_ref[...] = grad_ref[:, :PATCH, :tile_width]
    grad_lower_ref[...] = grad_ref[:, PATCH:, :tile_width]


def float_array(*shape):
    return jax.ShapeDtypeStruct(shape, jnp.float32)


def table_scratch():
    tall = pltpu.VMEM((6 * PATCH, 2 * PATCH), jnp.bfloat16)
    wide = pltpu.VMEM((2 * PATCH, 6 * PATCH), jnp.bfloat16)
    return [tall, wide, wide, tall]


VMEM_SPEC = pl.BlockSpec(memory_space=pltpu.VMEM)
SMEM_SPEC = pl.BlockSpec(memory_space=pltpu.SMEM)
PARAMS = pltpu.CompilerParams(vmem_limit_bytes=24 * 1024 * 1024)


def upper_slots(positions, counts, own, right, probe, measured, parts):
    tile_height, tile_width = own.shape[1:]
    wide = tile_width + PATCH
    return pl.pallas_call(
        upper_kernel,
        in_specs=[SMEM_SPEC] * 2 + [VMEM_SPEC] * 5,
        out_specs=[VMEM_SPEC] * 2,
        out_shape=[float_array(2, tile_height + 8, wide), float_array(3, 2, PATCH, PATCH)],
        scratch_shapes=[
            pltpu.VMEM((2, tile_height + 8, wide), jnp.float32),
            pltpu.SMEM((positions.shape[1],), jnp.int32),
        ]
        + table_scratch(),
        compiler_params=PARAMS,
        cost_estimate=pl.CostEstimate(flops=3_000_000_000, transcendentals=0, bytes_accessed=3_000_000),
        name="upper_slots",
    )(positions, counts, own, right, probe, measured, parts)


def lower_slots(positions, counts, own, below, right, corner, probe, measured, parts, upper, sums):
    tile_height, tile_width = own.shape[1:]
    wide = tile_width + PATCH
    return pl.pallas_call(
        lower_kernel,
        in_specs=[SMEM_SPEC] * 2 + [VMEM_SPEC] * 9,
        out_specs=[VMEM_SPEC] * 4,
        out_shape=[
            float_array(2, PATCH, tile_width),
            float_array(2, tile_height + PATCH, PATCH),
            float_array(2, PATCH, tile_width),
            float_array(32, 20, PATCH),
        ],
        scratch_shapes=[
            pltpu.VMEM((2, 2 * PATCH, wide), jnp.float32),
            pltpu.VMEM((2, 2 * PATCH, wide), jnp.float32),
            pltpu.VMEM((3, 2, PATCH, PATCH), jnp.float32),
            pltpu.SMEM((positions.shape[1],), jnp.int32),
        ]
        + table_scratch(),
        compiler_params=PARAMS,
        cost_estimate=pl.CostEstimate(flops=3_000_000_000, transcendentals=0, bytes_accessed=5_000_000),
        name="lower_slots",
    )(positions, counts, own, below, right, corner, probe, measured, parts, upper, sums)


def object_kernel(
    first_ref, own_ref, upper_ref, lower_ref, spilled_ref, rim_ref, side_ref, far_ref, probe_ref, out_ref
):
    tile_height, tile_width = own_ref.shape[1:]
    first = tile_height - PATCH
    power = probe_ref[...] * probe_ref[...]
    power = power[0, 0] + power[0, 1] + power[1, 0] + power[1, 1]
    weight = 1.0 / (jnp.max(power, axis=(0, 1), keepdims=True) + 1e-06)
    from_far = first_ref[0] == 1
    for plane in range(2):
        for start in range(0, tile_height, PATCH):
            for side in range(0, tile_width, PATCH):
                rows, cols = (slice(start, start + PATCH), slice(side, side + PATCH))
                if start < first:
                    total = upper_ref[plane, rows, cols]
                else:
                    total = lower_ref[plane, :, cols]
                if side == 0:
                    total += spilled_ref[plane, rows, :]
                if start == 0:
                    rest = jnp.where(from_far, far_ref[plane, :, cols], side_ref[plane, :, cols])
                    total += jnp.concatenate([rim_ref[plane, :, cols], rest], axis=0)
                out_ref[plane, rows, cols] = own_ref[plane, rows, cols] + total * weight


def object_update(first, own, upper, lower, spilled, rim, side, far, probe):
    return pl.pallas_call(
        object_kernel,
        in_specs=[SMEM_SPEC] + [VMEM_SPEC] * 8,
        out_specs=VMEM_SPEC,
        out_shape=float_array(*own.shape),
        compiler_params=PARAMS,
        cost_estimate=pl.CostEstimate(flops=OBJECT_COST, transcendentals=0, bytes_accessed=4_000_000),
        name="object_update",
    )(first, own, upper, lower, spilled, rim, side, far, probe)


def probe_kernel(blocks_ref, out_ref, density_ref):
    for block in range(blocks_ref.shape[0]):
        density_ref[block * 4 : block * 4 + 4] = blocks_ref[block, 16:]
    weight = lax.rsqrt(density_ref[...] + 1.0)
    for block in range(blocks_ref.shape[0]):
        part, mode, start = (block // 16, block // 8 % 2, block % 8 * 16)
        out_ref[part, mode, start : start + 16] = (
            blocks_ref[block, :16] * weight[start : start + 16]
        )


def probe_update(blocks, shape):
    return pl.pallas_call(
        probe_kernel,
        in_specs=[VMEM_SPEC],
        out_specs=VMEM_SPEC,
        out_shape=float_array(*shape),
        scratch_shapes=[pltpu.VMEM((PATCH, PATCH), jnp.float32)],
        compiler_params=PARAMS,
        name="probe_update",
    )(blocks)


def halo_kernel(own_ref, side_ref, direct_ref, left_ref, sems):
    pieces = (
        (own_ref.at[:, pl.ds(DIRECT, PATCH - DIRECT), :], side_ref),
        (own_ref.at[:, pl.ds(0, DIRECT), :], direct_ref),
        (own_ref.at[:, :, pl.ds(0, PATCH)], left_ref),
    )
    copies = [
        pltpu.make_async_copy(source, target, sems.at[order])
        for order, (source, target) in enumerate(pieces)
    ]
    for copy in copies:
        copy.start()
    for copy in copies:
        copy.wait()


def halo_pieces(own):
    planes, tile_height, tile_width = own.shape
    return pl.pallas_call(
        halo_kernel,
        in_specs=[pl.BlockSpec(memory_space=pltpu.MemorySpace.HBM)],
        out_specs=[VMEM_SPEC] * 3,
        out_shape=[
            float_array(planes, PATCH - DIRECT, tile_width),
            float_array(planes, DIRECT, tile_width),
            float_array(planes, tile_height, PATCH),
        ],
        scratch_shapes=[pltpu.SemaphoreType.DMA((3,))],
        compiler_params=PARAMS,
        name="halo_pieces",
    )(own)


def sum_kernel(terms_ref, out_ref):
    total = jnp.sum(terms_ref[...], axis=0)
    out_ref[...] = jnp.broadcast_to(total[None], out_ref.shape)


def sum_for(terms, copies):
    return pl.pallas_call(
        sum_kernel,
        in_specs=[VMEM_SPEC],
        out_specs=VMEM_SPEC,
        out_shape=float_array(copies, *terms.shape[1:]),
        compiler_params=PARAMS,
        name="sum_for",
    )(terms)


def rim_kernel(lower_ref, spilled_ref, direct_ref, side_ref):
    first = spilled_ref.shape[1] - PATCH
    for plane in range(2):
        near = lower_ref[plane, :, :PATCH] + spilled_ref[plane, first:]
        direct_ref[plane, :, :PATCH] = near[:DIRECT]
        side_ref[plane, :, :PATCH] = near[DIRECT:]
        direct_ref[plane, :, PATCH:] = lower_ref[plane, :DIRECT, PATCH:]
        side_ref[plane, :, PATCH:] = lower_ref[plane, DIRECT:, PATCH:]


def rim_pieces(lower, spilled):
    planes, height, width = lower.shape
    return pl.pallas_call(
        rim_kernel,
        in_specs=[VMEM_SPEC] * 2,
        out_specs=[VMEM_SPEC] * 2,
        out_shape=[
            float_array(planes, DIRECT, width),
            float_array(planes, height - DIRECT, width),
        ],
        compiler_params=PARAMS,
        cost_estimate=pl.CostEstimate(flops=RIM_COST, transcendentals=0, bytes_accessed=1_000_000),
        name="rim_pieces",
    )(lower, spilled)


def moved(array, where):
    pairs = []
    for device in range(lax.axis_size("row") * lax.axis_size("col")):
        row, col = divmod(device, lax.axis_size("col"))
        target = where(row)
        if target is not None:
            pairs.append((device, target * lax.axis_size("col") + col))
    return lax.ppermute(array, ("row", "col"), pairs)


def around(row, by):
    return row // RUN * RUN + (row + by) % RUN


def far_up(row):
    return row - RUN if row % RUN == RUN - 1 and row >= RUN else None


def far_down(row):
    return row + RUN if row % RUN == 0 and row + RUN < lax.axis_size("row") else None


def per_device(object_field, probe_modes, measured, positions, counts):
    planes, lines = device_groups(lax.axis_size("row") * lax.axis_size("col"))
    places, live, amplitudes = (positions[0, 0], counts[0], measured[0, 0])
    parts = jnp.asarray(fourier_parts(PATCH))
    place = lax.axis_index("row") % RUN
    side_rows, direct_rows, left_columns = halo_pieces(object_field)
    side = moved(side_rows, lambda row: around(row, -1))
    direct = shifted(direct_rows, "row", -1)
    far = moved(side, far_up)
    right = shifted(left_columns, "col", -1)
    upper, upper_sums = upper_slots(
        places, live, object_field, right, probe_modes, amplitudes, parts
    )
    direct, side, far, upper_sums = lax.optimization_barrier((direct, side, far, upper_sums))
    below = jnp.concatenate([direct, jnp.where(place == RUN - 1, far, side)], axis=1)
    corner = shifted(below[:, :, :PATCH], "col", -1)
    lower, grad_right, grad_lower, packed = lower_slots(
        places, live, object_field, below, right, corner, probe_modes, amplitudes, parts, upper, upper_sums
    )
    spilled = shifted(grad_right, "col", 1)
    rim_direct, rim_side = rim_pieces(grad_lower, spilled)
    rim_direct = shifted(rim_direct, "row", 1)
    rim_side = moved(rim_side, lambda row: around(row, 1))
    rim_far = moved(rim_side, far_down)
    terms = exchange(packed, planes)
    terms = exchange(sum_for(terms, len(lines[0])), lines)
    blocks = exchange(sum_for(terms, len(planes[0])), planes)
    object_new = object_update(
        (place == 0).astype(jnp.int32)[None],
        object_field, upper, lower, spilled, rim_direct, rim_side, rim_far, probe_modes,
    )
    probe_step = probe_update(blocks, probe_modes.shape)
    return (object_new, probe_step)


def solution(mesh):
    in_specs = (
        P(None, "row", "col"),
        P(),
        P("row", "col", None, None, None),
        P("row", "col", None, None),
        P("row", "col"),
    )
    out_specs = (P(None, "row", "col"), P())
    return jax.shard_map(
        per_device, mesh=mesh, in_specs=in_specs, out_specs=out_specs, check_vma=False
    )
```

```python
import math

import jax
import jax.numpy as jnp
import numpy as np
from jax import lax
from jax.experimental import pallas as pl
from jax.experimental.pallas import tpu as pltpu
from jax.sharding import PartitionSpec as P

AMP_FLOOR = 0.25
PATCH = 128
RUN = 4
DIRECT = 88
RIM_COST = 10_000_000_000
OBJECT_COST = 30_000_000_000


def shifted(array, axis, by):
    length = lax.axis_size(axis)
    pairs = [(i, i + by) for i in range(length) if 0 <= i + by < length]
    return lax.ppermute(array, axis, pairs)


def coordinates(device):
    row, col = divmod(device, 32)
    z_hi, x = divmod(row, 4)
    z_lo, rest = divmod(col, 8)
    y, core = divmod(rest, 2)
    return (z_hi * 4 + z_lo, x, y, core)


def device_groups(devices):
    planes, lines = {}, {}
    for device in range(devices):
        z, x, y, core = coordinates(device)
        planes.setdefault(z, []).append(device)
        lines.setdefault((x, y, core), []).append(device)
    return (list(planes.values()), list(lines.values()))


def exchange(blocks, groups):
    return lax.all_to_all(blocks, ("row", "col"), 0, 0, axis_index_groups=groups)


def split(values):
    high = values.astype(jnp.bfloat16)
    low = (values - high.astype(jnp.float32)).astype(jnp.bfloat16)
    return (high, low)


def fourier_parts(width):
    index = np.arange(width)
    angle = (index[:, None] * index[None, :] % width) * (2.0 * math.pi / width)
    parts = []
    for wave in (np.cos(angle), np.sin(angle)):
        values = (wave / math.sqrt(width)).astype(np.float32)
        high = values.astype(jnp.bfloat16)
        parts += [high, (values - high.astype(np.float32)).astype(jnp.bfloat16)]
    return np.stack(parts)


def fill_tables(parts_ref, table_refs):
    width = parts_ref.shape[-1]
    right_ref, left_ref, back_left_ref, back_right_ref = table_refs
    for level, places in ((0, (0, 2)), (1, (1,))):
        cosine = parts_ref[level]
        sine = parts_ref[2 + level]
        for place in places:
            start = place * 2 * width
            for i in range(2):
                for j in range(2):
                    value = cosine if i == j else (-sine if i == 0 else sine)
                    turned = cosine if i == j else (sine if i == 0 else -sine)
                    tall = (slice(start + i * width, start + (i + 1) * width), slice(j * width, (j + 1) * width))
                    wide = (slice(i * width, (i + 1) * width), slice(start + j * width, start + (j + 1) * width))
                    right_ref[tall] = value
                    back_right_ref[tall] = turned
                    left_ref[wide] = turned
                    back_left_ref[wide] = value


def times_right(values, table):
    high, low = split(values)
    return jnp.dot(
        jnp.concatenate([high, high, low], axis=1), table, preferred_element_type=jnp.float32
    )


def times_left(table, values):
    high, low = split(values)
    return jnp.dot(
        table, jnp.concatenate([high, high, low], axis=0), preferred_element_type=jnp.float32
    )


def regroup(values, width):
    blocks = values.shape[0] // width
    return jnp.concatenate(
        [
            jnp.concatenate(
                [values[b * width : (b + 1) * width, p * width : (p + 1) * width] for b in range(blocks)],
                axis=1,
            )
            for p in range(2)
        ],
        axis=0,
    )


def ungroup(values, width):
    blocks = values.shape[1] // width
    return jnp.concatenate(
        [
            jnp.concatenate(
                [values[p * width : (p + 1) * width, b * width : (b + 1) * width] for p in range(2)],
                axis=1,
            )
            for b in range(blocks)
        ],
        axis=0,
    )


def make_slots(positions_ref, first_row, field_ref, grad_ref, probe_ref, measured_ref, sums_ref, table_refs):
    width = PATCH
    modes = probe_ref.shape[1]
    tall = width + 8
    right_table, left_table, back_left, back_right = table_refs
    lane = lax.broadcasted_iota(jnp.int32, (tall, width), 1)
    sublane = lax.broadcasted_iota(jnp.int32, (tall // 8, 8, width), 1)

    def place(index):
        row = positions_ref[0, index] - first_row
        col = positions_ref[1, index]
        down = lax.rem(row, 8)
        shift = lax.rem(col, width)
        return (pl.multiple_of(row - down, 8), down, pl.multiple_of(col - shift, width), shift)

    def cut(plane, top, down, base, shift):
        near = field_ref[plane, pl.ds(top, tall), pl.ds(base, width)]
        far = field_ref[plane, pl.ds(top, tall), pl.ds(base + width, width)]
        back_by = lax.rem(width - shift, width)
        turned = jnp.where(
            lane < width - shift,
            pltpu.roll(near, back_by, axis=1),
            pltpu.roll(far, back_by, axis=1),
        )
        turned = pltpu.roll(turned.reshape(tall // 8, 8, width), lax.rem(8 - down, 8), axis=1)
        picked = jnp.where(sublane[1:] < 8 - down, turned[:-1], turned[1:])
        return picked.reshape(width, width)

    def paste(plane, top, down, base, shift, values):
        turned = pltpu.roll(values, shift, axis=1).reshape(width // 8, 8, width)
        turned = pltpu.roll(turned, down, axis=1)
        blank = jnp.zeros((1, 8, width), jnp.float32)
        moved = jnp.where(
            sublane >= down,
            jnp.concatenate([turned, blank], axis=0),
            jnp.concatenate([blank, turned], axis=0),
        ).reshape(tall, width)
        grad_ref[plane, pl.ds(top, tall), pl.ds(base, width)] += jnp.where(
            lane >= shift, moved, 0.0
        )
        grad_ref[plane, pl.ds(top, tall), pl.ds(base + width, width)] += jnp.where(
            lane < shift, moved, 0.0
        )

    def slots(indices):
        places = [place(index) for index in indices]
        patches = [(cut(0, *at), cut(1, *at)) for at in places]
        exits = []
        for patch_real, patch_imag in patches:
            for mode in range(modes):
                mode_real, mode_imag = (probe_ref[0, mode], probe_ref[1, mode])
                exits.append(
                    jnp.concatenate(
                        [
                            mode_real * patch_real - mode_imag * patch_imag,
                            mode_real * patch_imag + mode_imag * patch_real,
                        ],
                        axis=1,
                    )
                )
        rows = times_right(jnp.concatenate(exits, axis=0), right_table[...])
        far = times_left(left_table[...], regroup(rows, width))
        scalings = []
        for order, index in enumerate(indices):
            part = far[:, order * modes * width : (order + 1) * modes * width]
            power = part * part
            power = power[:width] + power[width:]
            intensity = sum(power[:, m * width : (m + 1) * width] for m in range(modes))
            scaling = (
                measured_ref[index] * lax.rsqrt(jnp.maximum(intensity, AMP_FLOOR * AMP_FLOOR)) - 1.0
            )
            scalings += [scaling] * modes
        scaling = jnp.concatenate(scalings, axis=1)
        rows = times_left(back_left[...], far * jnp.concatenate([scaling, scaling], axis=0))
        back = times_right(ungroup(rows, width), back_right[...])
        sums = [[0.0] * modes, [0.0] * modes]
        density = 0.0
        for order, (patch_real, patch_imag) in enumerate(patches):
            object_real, object_imag = (0.0, 0.0)
            for mode in range(modes):
                mode_real, mode_imag = (probe_ref[0, mode], probe_ref[1, mode])
                start = (order * modes + mode) * width
                back_real = back[start : start + width, :width]
                back_imag = back[start : start + width, width:]
                object_real += mode_real * back_real + mode_imag * back_imag
                object_imag += mode_real * back_imag - mode_imag * back_real
                sums[0][mode] += patch_real * back_real + patch_imag * back_imag
                sums[1][mode] += patch_real * back_imag - patch_imag * back_real
            density += patch_real * patch_real + patch_imag * patch_imag
            paste(0, *places[order], object_real)
            paste(1, *places[order], object_imag)
        for part in range(2):
            for mode in range(modes):
                sums_ref[part, mode] += sums[part][mode]
        sums_ref[2, 0] += density

    return slots


def run_slots(positions_ref, counts_ref, order_ref, slots, wanted):

    def note(index, found):
        order_ref[found] = index
        return found + wanted(positions_ref[0, index]).astype(jnp.int32)

    found = lax.fori_loop(0, counts_ref[0], note, jnp.int32(0))

    def run(start, stop, size):

        def step(turn, carry):
            slots([order_ref[start + turn * size + i] for i in range(size)])
            return carry

        turns = lax.div(stop - start, size)
        lax.fori_loop(0, turns, step, 0)
        return start + turns * size

    reached = run(0, found, 4)
    reached = run(reached, found, 2)
    run(reached, found, 1)


def upper_kernel(
    positions_ref, counts_ref, own_ref, right_ref, probe_ref, measured_ref, parts_ref,
    grad_ref, sums_ref, field_ref, order_ref, *table_refs,
):
    tile_height, tile_width = own_ref.shape[1:]
    fill_tables(parts_ref, table_refs)
    field_ref[:, :tile_height, :tile_width] = own_ref[...]
    field_ref[:, :tile_height, tile_width:] = right_ref[...]
    grad_ref[...] = jnp.zeros_like(grad_ref)
    sums_ref[...] = jnp.zeros_like(sums_ref)
    slots = make_slots(positions_ref, 0, field_ref, grad_ref, probe_ref, measured_ref, sums_ref, table_refs)
    run_slots(positions_ref, counts_ref, order_ref, slots, lambda row: row <= tile_height - PATCH)


def lower_kernel(
    positions_ref, counts_ref, last_ref, own_ref, direct_ref, side_ref, far_ref, right_ref, corner_ref,
    probe_ref, measured_ref, parts_ref, upper_ref, upper_sums_ref,
    grad_own_ref, grad_right_ref, grad_corner_ref, grad_lower_ref, packed_ref,
    field_ref, grad_ref, sums_ref, order_ref, *table_refs,
):
    tile_height, tile_width = own_ref.shape[1:]
    first = tile_height - PATCH
    fill_tables(parts_ref, table_refs)
    field_ref[:, :PATCH, :tile_width] = own_ref[:, first:]
    field_ref[:, PATCH : PATCH + DIRECT, :tile_width] = direct_ref[...]
    from_far = last_ref[0] == 1
    for plane in range(2):
        field_ref[plane, PATCH + DIRECT :, :tile_width] = jnp.where(
            from_far, far_ref[plane], side_ref[plane]
        )
    field_ref[:, :PATCH, tile_width:] = right_ref[:, first:]
    field_ref[:, PATCH:, tile_width:] = corner_ref[...]
    grad_ref[:, :PATCH] = upper_ref[:, first:tile_height]
    grad_ref[:, PATCH:] = jnp.zeros_like(grad_ref[:, PATCH:])
    sums_ref[...] = upper_sums_ref[...]
    slots = make_slots(positions_ref, first, field_ref, grad_ref, probe_ref, measured_ref, sums_ref, table_refs)
    run_slots(positions_ref, counts_ref, order_ref, slots, lambda row: row > first)
    for block in range(packed_ref.shape[0]):
        part, mode, start = (block // 16, block // 8 % 2, block % 8 * 16)
        packed_ref[block, :16] = sums_ref[part, mode, start : start + 16]
        packed_ref[block, 16:] = sums_ref[2, 0, block * 4 : block * 4 + 4]
    grad_right_ref[:, :first] = upper_ref[:, :first, tile_width:]
    grad_right_ref[:, first:] = grad_ref[:, :PATCH, tile_width:]
    grad_corner_ref[...] = grad_ref[:, PATCH:, tile_width:]
    grad_own_ref[...] = grad_ref[:, :PATCH, :tile_width]
    grad_lower_ref[...] = grad_ref[:, PATCH:, :tile_width]


def float_array(*shape):
    return jax.ShapeDtypeStruct(shape, jnp.float32)


def table_scratch():
    tall = pltpu.VMEM((6 * PATCH, 2 * PATCH), jnp.bfloat16)
    wide = pltpu.VMEM((2 * PATCH, 6 * PATCH), jnp.bfloat16)
    return [tall, wide, wide, tall]


VMEM_SPEC = pl.BlockSpec(memory_space=pltpu.VMEM)
SMEM_SPEC = pl.BlockSpec(memory_space=pltpu.SMEM)
PARAMS = pltpu.CompilerParams(vmem_limit_bytes=24 * 1024 * 1024)


def upper_slots(positions, counts, own, right, probe, measured, parts):
    tile_height, tile_width = own.shape[1:]
    wide = tile_width + PATCH
    return pl.pallas_call(
        upper_kernel,
        in_specs=[SMEM_SPEC] * 2 + [VMEM_SPEC] * 5,
        out_specs=[VMEM_SPEC] * 2,
        out_shape=[float_array(2, tile_height + 8, wide), float_array(3, 2, PATCH, PATCH)],
        scratch_shapes=[
            pltpu.VMEM((2, tile_height + 8, wide), jnp.float32),
            pltpu.SMEM((positions.shape[1],), jnp.int32),
        ]
        + table_scratch(),
        compiler_params=PARAMS,
        cost_estimate=pl.CostEstimate(flops=3_000_000_000, transcendentals=0, bytes_accessed=3_000_000),
        name="upper_slots",
    )(positions, counts, own, right, probe, measured, parts)


def lower_slots(
    positions, counts, last, own, direct, side, far, right, corner, probe, measured, parts, upper, sums
):
    tile_height, tile_width = own.shape[1:]
    wide = tile_width + PATCH
    return pl.pallas_call(
        lower_kernel,
        in_specs=[SMEM_SPEC] * 3 + [VMEM_SPEC] * 11,
        out_specs=[VMEM_SPEC] * 5,
        out_shape=[
            float_array(2, PATCH, tile_width),
            float_array(2, tile_height, PATCH),
            float_array(2, PATCH, PATCH),
            float_array(2, PATCH, tile_width),
            float_array(32, 20, PATCH),
        ],
        scratch_shapes=[
            pltpu.VMEM((2, 2 * PATCH, wide), jnp.float32),
            pltpu.VMEM((2, 2 * PATCH, wide), jnp.float32),
            pltpu.VMEM((3, 2, PATCH, PATCH), jnp.float32),
            pltpu.SMEM((positions.shape[1],), jnp.int32),
        ]
        + table_scratch(),
        compiler_params=PARAMS,
        cost_estimate=pl.CostEstimate(flops=3_000_000_000, transcendentals=0, bytes_accessed=5_000_000),
        name="lower_slots",
    )(positions, counts, last, own, direct, side, far, right, corner, probe, measured, parts, upper, sums)


def object_kernel(
    first_ref, own_ref, upper_ref, lower_ref, spilled_ref, rim_ref, side_ref, far_ref, probe_ref, out_ref
):
    tile_height, tile_width = own_ref.shape[1:]
    first = tile_height - PATCH
    power = probe_ref[...] * probe_ref[...]
    power = power[0, 0] + power[0, 1] + power[1, 0] + power[1, 1]
    weight = 1.0 / (jnp.max(power, axis=(0, 1), keepdims=True) + 1e-06)
    from_far = first_ref[0] == 1
    for plane in range(2):
        for start in range(0, tile_height, PATCH):
            for side in range(0, tile_width, PATCH):
                rows, cols = (slice(start, start + PATCH), slice(side, side + PATCH))
                if start < first:
                    total = upper_ref[plane, rows, cols]
                else:
                    total = lower_ref[plane, :, cols]
                if side == 0:
                    total += spilled_ref[plane, rows, :]
                if start == 0:
                    rest = jnp.where(from_far, far_ref[plane, :, cols], side_ref[plane, :, cols])
                    total += jnp.concatenate([rim_ref[plane, :, cols], rest], axis=0)
                out_ref[plane, rows, cols] = own_ref[plane, rows, cols] + total * weight


def object_update(first, own, upper, lower, spilled, rim, side, far, probe):
    return pl.pallas_call(
        object_kernel,
        in_specs=[SMEM_SPEC] + [VMEM_SPEC] * 8,
        out_specs=VMEM_SPEC,
        out_shape=float_array(*own.shape),
        compiler_params=PARAMS,
        cost_estimate=pl.CostEstimate(flops=OBJECT_COST, transcendentals=0, bytes_accessed=4_000_000),
        name="object_update",
    )(first, own, upper, lower, spilled, rim, side, far, probe)


def probe_kernel(blocks_ref, out_ref, density_ref):
    for block in range(blocks_ref.shape[0]):
        density_ref[block * 4 : block * 4 + 4] = blocks_ref[block, 16:]
    weight = lax.rsqrt(density_ref[...] + 1.0)
    for block in range(blocks_ref.shape[0]):
        part, mode, start = (block // 16, block // 8 % 2, block % 8 * 16)
        out_ref[part, mode, start : start + 16] = (
            blocks_ref[block, :16] * weight[start : start + 16]
        )


def probe_update(blocks, shape):
    return pl.pallas_call(
        probe_kernel,
        in_specs=[VMEM_SPEC],
        out_specs=VMEM_SPEC,
        out_shape=float_array(*shape),
        scratch_shapes=[pltpu.VMEM((PATCH, PATCH), jnp.float32)],
        compiler_params=PARAMS,
        name="probe_update",
    )(blocks)


def halo_kernel(own_ref, side_ref, direct_ref, left_ref, sems):
    pieces = (
        (own_ref.at[:, pl.ds(DIRECT, PATCH - DIRECT), :], side_ref),
        (own_ref.at[:, pl.ds(0, DIRECT), :], direct_ref),
        (own_ref.at[:, :, pl.ds(0, PATCH)], left_ref),
    )
    copies = [
        pltpu.make_async_copy(source, target, sems.at[order])
        for order, (source, target) in enumerate(pieces)
    ]
    for copy in copies:
        copy.start()
    for copy in copies:
        copy.wait()


def halo_pieces(own):
    planes, tile_height, tile_width = own.shape
    return pl.pallas_call(
        halo_kernel,
        in_specs=[pl.BlockSpec(memory_space=pltpu.MemorySpace.HBM)],
        out_specs=[VMEM_SPEC] * 3,
        out_shape=[
            float_array(planes, PATCH - DIRECT, tile_width),
            float_array(planes, DIRECT, tile_width),
            float_array(planes, tile_height, PATCH),
        ],
        scratch_shapes=[pltpu.SemaphoreType.DMA((3,))],
        compiler_params=PARAMS,
        name="halo_pieces",
    )(own)


def corner_kernel(last_ref, direct_ref, side_ref, far_ref, corner_ref):
    from_far = last_ref[0] == 1
    for plane in range(2):
        corner_ref[plane, :DIRECT] = direct_ref[plane, :, :PATCH]
        corner_ref[plane, DIRECT:] = jnp.where(
            from_far, far_ref[plane, :, :PATCH], side_ref[plane, :, :PATCH]
        )


def corner_piece(last, direct, side, far):
    return pl.pallas_call(
        corner_kernel,
        in_specs=[SMEM_SPEC] + [VMEM_SPEC] * 3,
        out_specs=VMEM_SPEC,
        out_shape=float_array(2, PATCH, PATCH),
        compiler_params=PARAMS,
        name="corner_piece",
    )(last, direct, side, far)


def sum_kernel(terms_ref, out_ref):
    total = jnp.sum(terms_ref[...], axis=0)
    out_ref[...] = jnp.broadcast_to(total[None], out_ref.shape)


def sum_for(terms, copies):
    return pl.pallas_call(
        sum_kernel,
        in_specs=[VMEM_SPEC],
        out_specs=VMEM_SPEC,
        out_shape=float_array(copies, *terms.shape[1:]),
        compiler_params=PARAMS,
        name="sum_for",
    )(terms)


def rim_kernel(lower_ref, spilled_ref, direct_ref, side_ref):
    for plane in range(2):
        near = lower_ref[plane, :, :PATCH] + spilled_ref[plane]
        direct_ref[plane, :, :PATCH] = near[:DIRECT]
        side_ref[plane, :, :PATCH] = near[DIRECT:]
        direct_ref[plane, :, PATCH:] = lower_ref[plane, :DIRECT, PATCH:]
        side_ref[plane, :, PATCH:] = lower_ref[plane, DIRECT:, PATCH:]


def rim_pieces(lower, spilled):
    planes, height, width = lower.shape
    return pl.pallas_call(
        rim_kernel,
        in_specs=[VMEM_SPEC] * 2,
        out_specs=[VMEM_SPEC] * 2,
        out_shape=[
            float_array(planes, DIRECT, width),
            float_array(planes, height - DIRECT, width),
        ],
        compiler_params=PARAMS,
        cost_estimate=pl.CostEstimate(flops=RIM_COST, transcendentals=0, bytes_accessed=1_000_000),
        name="rim_pieces",
    )(lower, spilled)


def moved(array, where):
    pairs = []
    for device in range(lax.axis_size("row") * lax.axis_size("col")):
        row, col = divmod(device, lax.axis_size("col"))
        target = where(row)
        if target is not None:
            pairs.append((device, target * lax.axis_size("col") + col))
    return lax.ppermute(array, ("row", "col"), pairs)


def around(row, by):
    return row // RUN * RUN + (row + by) % RUN


def far_up(row):
    return row - RUN if row % RUN == RUN - 1 and row >= RUN else None


def far_down(row):
    return row + RUN if row % RUN == 0 and row + RUN < lax.axis_size("row") else None


def per_device(object_field, probe_modes, measured, positions, counts):
    planes, lines = device_groups(lax.axis_size("row") * lax.axis_size("col"))
    places, live, amplitudes = (positions[0, 0], counts[0], measured[0, 0])
    parts = jnp.asarray(fourier_parts(PATCH))
    place = lax.axis_index("row") % RUN
    side_rows, direct_rows, left_columns = halo_pieces(
        pltpu.with_memory_space_constraint(object_field, pltpu.MemorySpace.HBM)
    )
    side = moved(side_rows, lambda row: around(row, -1))
    direct = shifted(direct_rows, "row", -1)
    far = moved(side, far_up)
    right = shifted(left_columns, "col", -1)
    upper, upper_sums = upper_slots(
        places, live, object_field, right, probe_modes, amplitudes, parts
    )
    direct, side, far, upper_sums = lax.optimization_barrier((direct, side, far, upper_sums))
    last = (place == RUN - 1).astype(jnp.int32)[None]
    corner = shifted(corner_piece(last, direct, side, far), "col", -1)
    lower, grad_right, grad_corner, grad_lower, packed = lower_slots(
        places, live, last, object_field, direct, side, far, right, corner,
        probe_modes, amplitudes, parts, upper, upper_sums,
    )
    spilled = shifted(grad_right, "col", 1)
    spilled_corner = shifted(grad_corner, "col", 1)
    rim_direct, rim_side = rim_pieces(grad_lower, spilled_corner)
    rim_direct = shifted(rim_direct, "row", 1)
    rim_side = moved(rim_side, lambda row: around(row, 1))
    rim_far = moved(rim_side, far_down)
    terms = exchange(packed, planes)
    terms = exchange(sum_for(terms, len(lines[0])), lines)
    blocks = exchange(sum_for(terms, len(planes[0])), planes)
    object_new = object_update(
        (place == 0).astype(jnp.int32)[None],
        object_field, upper, lower, spilled, rim_direct, rim_side, rim_far, probe_modes,
    )
    probe_step = probe_update(blocks, probe_modes.shape)
    return (object_new, probe_step)


def solution(mesh):
    in_specs = (
        P(None, "row", "col"),
        P(),
        P("row", "col", None, None, None),
        P("row", "col", None, None),
        P("row", "col"),
    )
    out_specs = (P(None, "row", "col"), P())
    return jax.shard_map(
        per_device, mesh=mesh, in_specs=in_specs, out_specs=out_specs, check_vma=False
    )
```

```python
import math

import jax
import jax.numpy as jnp
import numpy as np
from jax import lax
from jax.experimental import pallas as pl
from jax.experimental.pallas import tpu as pltpu
from jax.sharding import PartitionSpec as P

AMP_FLOOR = 0.25
PATCH = 128
RUN = 4
DIRECT = 80
RIM_DIRECT = 72
RIM_COST = 10_000_000_000
OBJECT_COST = 30_000_000_000


def shifted(array, axis, by):
    length = lax.axis_size(axis)
    pairs = [(i, i + by) for i in range(length) if 0 <= i + by < length]
    return lax.ppermute(array, axis, pairs)


def coordinates(device):
    row, col = divmod(device, 32)
    z_hi, x = divmod(row, 4)
    z_lo, rest = divmod(col, 8)
    y, core = divmod(rest, 2)
    return (z_hi * 4 + z_lo, x, y, core)


def device_groups(devices):
    planes, lines = {}, {}
    for device in range(devices):
        z, x, y, core = coordinates(device)
        planes.setdefault(z, []).append(device)
        lines.setdefault((x, y, core), []).append(device)
    return (list(planes.values()), list(lines.values()))


def exchange(blocks, groups):
    return lax.all_to_all(blocks, ("row", "col"), 0, 0, axis_index_groups=groups)


def split(values):
    high = values.astype(jnp.bfloat16)
    low = (values - high.astype(jnp.float32)).astype(jnp.bfloat16)
    return (high, low)


def fourier_parts(width):
    index = np.arange(width)
    angle = (index[:, None] * index[None, :] % width) * (2.0 * math.pi / width)
    parts = []
    for wave in (np.cos(angle), np.sin(angle)):
        values = (wave / math.sqrt(width)).astype(np.float32)
        high = values.astype(jnp.bfloat16)
        parts += [high, (values - high.astype(np.float32)).astype(jnp.bfloat16)]
    return np.stack(parts)


def fill_tables(parts_ref, table_refs):
    width = parts_ref.shape[-1]
    right_ref, left_ref, back_left_ref, back_right_ref = table_refs
    for level, places in ((0, (0, 2)), (1, (1,))):
        cosine = parts_ref[level]
        sine = parts_ref[2 + level]
        for place in places:
            start = place * 2 * width
            for i in range(2):
                for j in range(2):
                    value = cosine if i == j else (-sine if i == 0 else sine)
                    turned = cosine if i == j else (sine if i == 0 else -sine)
                    tall = (slice(start + i * width, start + (i + 1) * width), slice(j * width, (j + 1) * width))
                    wide = (slice(i * width, (i + 1) * width), slice(start + j * width, start + (j + 1) * width))
                    right_ref[tall] = value
                    back_right_ref[tall] = turned
                    left_ref[wide] = turned
                    back_left_ref[wide] = value


def times_right(values, table):
    high, low = split(values)
    return jnp.dot(
        jnp.concatenate([high, high, low], axis=1), table, preferred_element_type=jnp.float32
    )


def times_left(table, values):
    high, low = split(values)
    return jnp.dot(
        table, jnp.concatenate([high, high, low], axis=0), preferred_element_type=jnp.float32
    )


def regroup(values, width):
    blocks = values.shape[0] // width
    return jnp.concatenate(
        [
            jnp.concatenate(
                [values[b * width : (b + 1) * width, p * width : (p + 1) * width] for b in range(blocks)],
                axis=1,
            )
            for p in range(2)
        ],
        axis=0,
    )


def ungroup(values, width):
    blocks = values.shape[1] // width
    return jnp.concatenate(
        [
            jnp.concatenate(
                [values[p * width : (p + 1) * width, b * width : (b + 1) * width] for p in range(2)],
                axis=1,
            )
            for b in range(blocks)
        ],
        axis=0,
    )


def make_slots(positions_ref, first_row, field_ref, grad_ref, probe_ref, measured_ref, sums_ref, table_refs):
    width = PATCH
    modes = probe_ref.shape[1]
    tall = width + 8
    right_table, left_table, back_left, back_right = table_refs
    lane = lax.broadcasted_iota(jnp.int32, (tall, width), 1)
    sublane = lax.broadcasted_iota(jnp.int32, (tall // 8, 8, width), 1)

    def place(index):
        row = positions_ref[0, index] - first_row
        col = positions_ref[1, index]
        down = lax.rem(row, 8)
        shift = lax.rem(col, width)
        return (pl.multiple_of(row - down, 8), down, pl.multiple_of(col - shift, width), shift)

    def cut(plane, top, down, base, shift):
        near = field_ref[plane, pl.ds(top, tall), pl.ds(base, width)]
        far = field_ref[plane, pl.ds(top, tall), pl.ds(base + width, width)]
        back_by = lax.rem(width - shift, width)
        turned = jnp.where(
            lane < width - shift,
            pltpu.roll(near, back_by, axis=1),
            pltpu.roll(far, back_by, axis=1),
        )
        turned = pltpu.roll(turned.reshape(tall // 8, 8, width), lax.rem(8 - down, 8), axis=1)
        picked = jnp.where(sublane[1:] < 8 - down, turned[:-1], turned[1:])
        return picked.reshape(width, width)

    def paste(plane, top, down, base, shift, values):
        turned = pltpu.roll(values, shift, axis=1).reshape(width // 8, 8, width)
        turned = pltpu.roll(turned, down, axis=1)
        blank = jnp.zeros((1, 8, width), jnp.float32)
        moved = jnp.where(
            sublane >= down,
            jnp.concatenate([turned, blank], axis=0),
            jnp.concatenate([blank, turned], axis=0),
        ).reshape(tall, width)
        grad_ref[plane, pl.ds(top, tall), pl.ds(base, width)] += jnp.where(
            lane >= shift, moved, 0.0
        )
        grad_ref[plane, pl.ds(top, tall), pl.ds(base + width, width)] += jnp.where(
            lane < shift, moved, 0.0
        )

    def slots(indices):
        places = [place(index) for index in indices]
        patches = [(cut(0, *at), cut(1, *at)) for at in places]
        exits = []
        for patch_real, patch_imag in patches:
            for mode in range(modes):
                mode_real, mode_imag = (probe_ref[0, mode], probe_ref[1, mode])
                exits.append(
                    jnp.concatenate(
                        [
                            mode_real * patch_real - mode_imag * patch_imag,
                            mode_real * patch_imag + mode_imag * patch_real,
                        ],
                        axis=1,
                    )
                )
        rows = times_right(jnp.concatenate(exits, axis=0), right_table[...])
        far = times_left(left_table[...], regroup(rows, width))
        scalings = []
        for order, index in enumerate(indices):
            part = far[:, order * modes * width : (order + 1) * modes * width]
            power = part * part
            power = power[:width] + power[width:]
            intensity = sum(power[:, m * width : (m + 1) * width] for m in range(modes))
            scaling = (
                measured_ref[index] * lax.rsqrt(jnp.maximum(intensity, AMP_FLOOR * AMP_FLOOR)) - 1.0
            )
            scalings += [scaling] * modes
        scaling = jnp.concatenate(scalings, axis=1)
        rows = times_left(back_left[...], far * jnp.concatenate([scaling, scaling], axis=0))
        back = times_right(ungroup(rows, width), back_right[...])
        sums = [[0.0] * modes, [0.0] * modes]
        density = 0.0
        for order, (patch_real, patch_imag) in enumerate(patches):
            object_real, object_imag = (0.0, 0.0)
            for mode in range(modes):
                mode_real, mode_imag = (probe_ref[0, mode], probe_ref[1, mode])
                start = (order * modes + mode) * width
                back_real = back[start : start + width, :width]
                back_imag = back[start : start + width, width:]
                object_real += mode_real * back_real + mode_imag * back_imag
                object_imag += mode_real * back_imag - mode_imag * back_real
                sums[0][mode] += patch_real * back_real + patch_imag * back_imag
                sums[1][mode] += patch_real * back_imag - patch_imag * back_real
            density += patch_real * patch_real + patch_imag * patch_imag
            paste(0, *places[order], object_real)
            paste(1, *places[order], object_imag)
        for part in range(2):
            for mode in range(modes):
                sums_ref[part, mode] += sums[part][mode]
        sums_ref[2, 0] += density

    return slots


def run_slots(positions_ref, counts_ref, order_ref, slots, wanted):

    def note(index, found):
        order_ref[found] = index
        return found + wanted(positions_ref[0, index]).astype(jnp.int32)

    found = lax.fori_loop(0, counts_ref[0], note, jnp.int32(0))

    def run(start, stop, size):

        def step(turn, carry):
            slots([order_ref[start + turn * size + i] for i in range(size)])
            return carry

        turns = lax.div(stop - start, size)
        lax.fori_loop(0, turns, step, 0)
        return start + turns * size

    reached = run(0, found, 4)
    reached = run(reached, found, 2)
    run(reached, found, 1)


def upper_kernel(
    positions_ref, counts_ref, own_ref, right_ref, probe_ref, measured_ref, parts_ref,
    grad_ref, sums_ref, field_ref, order_ref, *table_refs,
):
    tile_height, tile_width = own_ref.shape[1:]
    fill_tables(parts_ref, table_refs)
    field_ref[:, :tile_height, :tile_width] = own_ref[...]
    field_ref[:, :tile_height, tile_width:] = right_ref[...]
    grad_ref[...] = jnp.zeros_like(grad_ref)
    sums_ref[...] = jnp.zeros_like(sums_ref)
    slots = make_slots(positions_ref, 0, field_ref, grad_ref, probe_ref, measured_ref, sums_ref, table_refs)
    run_slots(positions_ref, counts_ref, order_ref, slots, lambda row: row <= tile_height - PATCH)


def lower_kernel(
    positions_ref, counts_ref, last_ref, own_ref, direct_ref, side_ref, far_ref, right_ref, corner_ref,
    probe_ref, measured_ref, parts_ref, upper_ref, upper_sums_ref,
    grad_own_ref, grad_right_ref, grad_corner_ref, grad_lower_ref, packed_ref,
    field_ref, grad_ref, sums_ref, order_ref, *table_refs,
):
    tile_height, tile_width = own_ref.shape[1:]
    first = tile_height - PATCH
    fill_tables(parts_ref, table_refs)
    field_ref[:, :PATCH, :tile_width] = own_ref[:, first:]
    field_ref[:, PATCH : PATCH + DIRECT, :tile_width] = direct_ref[...]

    @pl.when(last_ref[0] == 1)
    def _():
        field_ref[:, PATCH + DIRECT :, :tile_width] = far_ref[...]

    @pl.when(last_ref[0] == 0)
    def _():
        field_ref[:, PATCH + DIRECT :, :tile_width] = side_ref[...]

    field_ref[:, :PATCH, tile_width:] = right_ref[:, first:]
    field_ref[:, PATCH:, tile_width:] = corner_ref[...]
    grad_ref[:, :PATCH] = upper_ref[:, first:tile_height]
    grad_ref[:, PATCH:] = jnp.zeros_like(grad_ref[:, PATCH:])
    sums_ref[...] = upper_sums_ref[...]
    slots = make_slots(positions_ref, first, field_ref, grad_ref, probe_ref, measured_ref, sums_ref, table_refs)
    run_slots(positions_ref, counts_ref, order_ref, slots, lambda row: row > first)
    for block in range(packed_ref.shape[0]):
        part, mode, start = (block // 16, block // 8 % 2, block % 8 * 16)
        packed_ref[block, :16] = sums_ref[part, mode, start : start + 16]
        packed_ref[block, 16:] = sums_ref[2, 0, block * 4 : block * 4 + 4]
    grad_right_ref[:, :first] = upper_ref[:, :first, tile_width:]
    grad_right_ref[:, first:] = grad_ref[:, :PATCH, tile_width:]
    grad_corner_ref[...] = grad_ref[:, PATCH:, tile_width:]
    grad_own_ref[...] = grad_ref[:, :PATCH, :tile_width]
    grad_lower_ref[...] = grad_ref[:, PATCH:, :tile_width]


def float_array(*shape):
    return jax.ShapeDtypeStruct(shape, jnp.float32)


def table_scratch():
    tall = pltpu.VMEM((6 * PATCH, 2 * PATCH), jnp.bfloat16)
    wide = pltpu.VMEM((2 * PATCH, 6 * PATCH), jnp.bfloat16)
    return [tall, wide, wide, tall]


VMEM_SPEC = pl.BlockSpec(memory_space=pltpu.VMEM)
SMEM_SPEC = pl.BlockSpec(memory_space=pltpu.SMEM)
PARAMS = pltpu.CompilerParams(vmem_limit_bytes=24 * 1024 * 1024)


def upper_slots(positions, counts, own, right, probe, measured, parts):
    tile_height, tile_width = own.shape[1:]
    wide = tile_width + PATCH
    return pl.pallas_call(
        upper_kernel,
        in_specs=[SMEM_SPEC] * 2 + [VMEM_SPEC] * 5,
        out_specs=[VMEM_SPEC] * 2,
        out_shape=[float_array(2, tile_height + 8, wide), float_array(3, 2, PATCH, PATCH)],
        scratch_shapes=[
            pltpu.VMEM((2, tile_height + 8, wide), jnp.float32),
            pltpu.SMEM((positions.shape[1],), jnp.int32),
        ]
        + table_scratch(),
        compiler_params=PARAMS,
        cost_estimate=pl.CostEstimate(flops=3_000_000_000, transcendentals=0, bytes_accessed=3_000_000),
        name="upper_slots",
    )(positions, counts, own, right, probe, measured, parts)


def lower_slots(
    positions, counts, last, own, direct, side, far, right, corner, probe, measured, parts, upper, sums
):
    tile_height, tile_width = own.shape[1:]
    wide = tile_width + PATCH
    return pl.pallas_call(
        lower_kernel,
        in_specs=[SMEM_SPEC] * 3 + [VMEM_SPEC] * 11,
        out_specs=[VMEM_SPEC] * 5,
        out_shape=[
            float_array(2, PATCH, tile_width),
            float_array(2, tile_height, PATCH),
            float_array(2, PATCH, PATCH),
            float_array(2, PATCH, tile_width),
            float_array(32, 20, PATCH),
        ],
        scratch_shapes=[
            pltpu.VMEM((2, 2 * PATCH, wide), jnp.float32),
            pltpu.VMEM((2, 2 * PATCH, wide), jnp.float32),
            pltpu.VMEM((3, 2, PATCH, PATCH), jnp.float32),
            pltpu.SMEM((positions.shape[1],), jnp.int32),
        ]
        + table_scratch(),
        compiler_params=PARAMS,
        cost_estimate=pl.CostEstimate(flops=3_000_000_000, transcendentals=0, bytes_accessed=5_000_000),
        name="lower_slots",
    )(positions, counts, last, own, direct, side, far, right, corner, probe, measured, parts, upper, sums)


def object_kernel(
    first_ref, own_ref, upper_ref, lower_ref, spilled_ref, rim_ref, side_ref, far_ref, probe_ref, out_ref
):
    tile_height, tile_width = own_ref.shape[1:]
    first = tile_height - PATCH
    power = probe_ref[...] * probe_ref[...]
    power = power[0, 0] + power[0, 1] + power[1, 0] + power[1, 1]
    weight = 1.0 / (jnp.max(power, axis=(0, 1), keepdims=True) + 1e-06)
    from_far = first_ref[0] == 1
    for plane in range(2):
        for start in range(0, tile_height, PATCH):
            for side in range(0, tile_width, PATCH):
                rows, cols = (slice(start, start + PATCH), slice(side, side + PATCH))
                if start < first:
                    total = upper_ref[plane, rows, cols]
                else:
                    total = lower_ref[plane, :, cols]
                if side == 0:
                    total += spilled_ref[plane, rows, :]
                if start == 0:
                    rest = jnp.where(from_far, far_ref[plane, :, cols], side_ref[plane, :, cols])
                    total += jnp.concatenate([rim_ref[plane, :, cols], rest], axis=0)
                out_ref[plane, rows, cols] = own_ref[plane, rows, cols] + total * weight


def object_update(first, own, upper, lower, spilled, rim, side, far, probe):
    return pl.pallas_call(
        object_kernel,
        in_specs=[SMEM_SPEC] + [VMEM_SPEC] * 8,
        out_specs=VMEM_SPEC,
        out_shape=float_array(*own.shape),
        compiler_params=PARAMS,
        cost_estimate=pl.CostEstimate(flops=OBJECT_COST, transcendentals=0, bytes_accessed=4_000_000),
        name="object_update",
    )(first, own, upper, lower, spilled, rim, side, far, probe)


def probe_kernel(blocks_ref, out_ref, density_ref):
    for block in range(blocks_ref.shape[0]):
        density_ref[block * 4 : block * 4 + 4] = blocks_ref[block, 16:]
    weight = lax.rsqrt(density_ref[...] + 1.0)
    for block in range(blocks_ref.shape[0]):
        part, mode, start = (block // 16, block // 8 % 2, block % 8 * 16)
        out_ref[part, mode, start : start + 16] = (
            blocks_ref[block, :16] * weight[start : start + 16]
        )


def probe_update(blocks, shape):
    return pl.pallas_call(
        probe_kernel,
        in_specs=[VMEM_SPEC],
        out_specs=VMEM_SPEC,
        out_shape=float_array(*shape),
        scratch_shapes=[pltpu.VMEM((PATCH, PATCH), jnp.float32)],
        compiler_params=PARAMS,
        name="probe_update",
    )(blocks)


def halo_kernel(own_ref, side_ref, direct_ref, left_ref, sems):
    pieces = (
        (own_ref.at[:, pl.ds(DIRECT, PATCH - DIRECT), :], side_ref),
        (own_ref.at[:, pl.ds(0, DIRECT), :], direct_ref),
        (own_ref.at[:, :, pl.ds(0, PATCH)], left_ref),
    )
    copies = [
        pltpu.make_async_copy(source, target, sems.at[order])
        for order, (source, target) in enumerate(pieces)
    ]
    for copy in copies:
        copy.start()
    for copy in copies:
        copy.wait()


def halo_pieces(own):
    planes, tile_height, tile_width = own.shape
    return pl.pallas_call(
        halo_kernel,
        in_specs=[pl.BlockSpec(memory_space=pltpu.MemorySpace.HBM)],
        out_specs=[VMEM_SPEC] * 3,
        out_shape=[
            float_array(planes, PATCH - DIRECT, tile_width),
            float_array(planes, DIRECT, tile_width),
            float_array(planes, tile_height, PATCH),
        ],
        scratch_shapes=[pltpu.SemaphoreType.DMA((3,))],
        compiler_params=PARAMS,
        name="halo_pieces",
    )(own)


def corner_kernel(last_ref, direct_ref, side_ref, far_ref, corner_ref):
    from_far = last_ref[0] == 1
    for plane in range(2):
        corner_ref[plane, :DIRECT] = direct_ref[plane, :, :PATCH]
        corner_ref[plane, DIRECT:] = jnp.where(
            from_far, far_ref[plane, :, :PATCH], side_ref[plane, :, :PATCH]
        )


def corner_piece(last, direct, side, far):
    return pl.pallas_call(
        corner_kernel,
        in_specs=[SMEM_SPEC] + [VMEM_SPEC] * 3,
        out_specs=VMEM_SPEC,
        out_shape=float_array(2, PATCH, PATCH),
        compiler_params=PARAMS,
        name="corner_piece",
    )(last, direct, side, far)


def sum_kernel(terms_ref, out_ref):
    total = jnp.sum(terms_ref[...], axis=0)
    out_ref[...] = jnp.broadcast_to(total[None], out_ref.shape)


def sum_for(terms, copies):
    return pl.pallas_call(
        sum_kernel,
        in_specs=[VMEM_SPEC],
        out_specs=VMEM_SPEC,
        out_shape=float_array(copies, *terms.shape[1:]),
        compiler_params=PARAMS,
        name="sum_for",
    )(terms)


def rim_kernel(lower_ref, spilled_ref, direct_ref, side_ref):
    for plane in range(2):
        near = lower_ref[plane, :, :PATCH] + spilled_ref[plane]
        direct_ref[plane, :, :PATCH] = near[:RIM_DIRECT]
        side_ref[plane, :, :PATCH] = near[RIM_DIRECT:]
        direct_ref[plane, :, PATCH:] = lower_ref[plane, :RIM_DIRECT, PATCH:]
        side_ref[plane, :, PATCH:] = lower_ref[plane, RIM_DIRECT:, PATCH:]


def rim_pieces(lower, spilled):
    planes, height, width = lower.shape
    return pl.pallas_call(
        rim_kernel,
        in_specs=[VMEM_SPEC] * 2,
        out_specs=[VMEM_SPEC] * 2,
        out_shape=[
            float_array(planes, RIM_DIRECT, width),
            float_array(planes, height - RIM_DIRECT, width),
        ],
        compiler_params=PARAMS,
        cost_estimate=pl.CostEstimate(flops=RIM_COST, transcendentals=0, bytes_accessed=1_000_000),
        name="rim_pieces",
    )(lower, spilled)


def moved(array, where):
    pairs = []
    for device in range(lax.axis_size("row") * lax.axis_size("col")):
        row, col = divmod(device, lax.axis_size("col"))
        target = where(row)
        if target is not None:
            pairs.append((device, target * lax.axis_size("col") + col))
    return lax.ppermute(array, ("row", "col"), pairs)


def around(row, by):
    return row // RUN * RUN + (row + by) % RUN


def far_up(row):
    return row - RUN if row % RUN == RUN - 1 and row >= RUN else None


def far_down(row):
    return row + RUN if row % RUN == 0 and row + RUN < lax.axis_size("row") else None


def per_device(object_field, probe_modes, measured, positions, counts):
    planes, lines = device_groups(lax.axis_size("row") * lax.axis_size("col"))
    places, live, amplitudes = (positions[0, 0], counts[0], measured[0, 0])
    parts = jnp.asarray(fourier_parts(PATCH))
    place = lax.axis_index("row") % RUN
    side_rows, direct_rows, left_columns = halo_pieces(
        pltpu.with_memory_space_constraint(object_field, pltpu.MemorySpace.HBM)
    )
    side = moved(side_rows, lambda row: around(row, -1))
    direct = shifted(direct_rows, "row", -1)
    far = moved(side, far_up)
    right = shifted(left_columns, "col", -1)
    upper, upper_sums = upper_slots(
        places, live, object_field, right, probe_modes, amplitudes, parts
    )
    direct, side, far, upper_sums = lax.optimization_barrier((direct, side, far, upper_sums))
    last = (place == RUN - 1).astype(jnp.int32)[None]
    corner = shifted(corner_piece(last, direct, side, far), "col", -1)
    lower, grad_right, grad_corner, grad_lower, packed = lower_slots(
        places, live, last, object_field, direct, side, far, right, corner,
        probe_modes, amplitudes, parts, upper, upper_sums,
    )
    spilled = shifted(grad_right, "col", 1)
    spilled_corner = shifted(grad_corner, "col", 1)
    rim_direct, rim_side = rim_pieces(grad_lower, spilled_corner)
    rim_direct = shifted(rim_direct, "row", 1)
    rim_side = moved(rim_side, lambda row: around(row, 1))
    rim_far = moved(rim_side, far_down)
    terms = exchange(packed, planes)
    terms = exchange(sum_for(terms, len(lines[0])), lines)
    blocks = exchange(sum_for(terms, len(planes[0])), planes)
    object_new = object_update(
        (place == 0).astype(jnp.int32)[None],
        object_field, upper, lower, spilled, rim_direct, rim_side, rim_far, probe_modes,
    )
    probe_step = probe_update(blocks, probe_modes.shape)
    return (object_new, probe_step)


def solution(mesh):
    in_specs = (
        P(None, "row", "col"),
        P(),
        P("row", "col", None, None, None),
        P("row", "col", None, None),
        P("row", "col"),
    )
    out_specs = (P(None, "row", "col"), P())
    return jax.shard_map(
        per_device, mesh=mesh, in_specs=in_specs, out_specs=out_specs, check_vma=False
    )
```

```python
import math

import jax
import jax.numpy as jnp
import numpy as np
from jax import lax
from jax.experimental import pallas as pl
from jax.experimental.pallas import tpu as pltpu
from jax.sharding import PartitionSpec as P

AMP_FLOOR = 0.25
PATCH = 128
RUN = 4
DIRECT = 80
RIM_DIRECT = 72
RIM_COST = 10_000_000_000
OBJECT_COST = 30_000_000_000


def shifted(array, axis, by):
    length = lax.axis_size(axis)
    pairs = [(i, i + by) for i in range(length) if 0 <= i + by < length]
    return lax.ppermute(array, axis, pairs)


def coordinates(device):
    row, col = divmod(device, 32)
    z_hi, x = divmod(row, 4)
    z_lo, rest = divmod(col, 8)
    y, core = divmod(rest, 2)
    return (z_hi * 4 + z_lo, x, y, core)


def device_groups(devices):
    planes, lines = {}, {}
    for device in range(devices):
        z, x, y, core = coordinates(device)
        planes.setdefault(z, []).append(device)
        lines.setdefault((x, y, core), []).append(device)
    return (list(planes.values()), list(lines.values()))


def exchange(blocks, groups):
    return lax.all_to_all(blocks, ("row", "col"), 0, 0, axis_index_groups=groups)


def split(values):
    high = values.astype(jnp.bfloat16)
    low = (values - high.astype(jnp.float32)).astype(jnp.bfloat16)
    return (high, low)


def fourier_parts(width):
    index = np.arange(width)
    angle = (index[:, None] * index[None, :] % width) * (2.0 * math.pi / width)
    parts = []
    for wave in (np.cos(angle), np.sin(angle)):
        values = (wave / math.sqrt(width)).astype(np.float32)
        high = values.astype(jnp.bfloat16)
        parts += [high, (values - high.astype(np.float32)).astype(jnp.bfloat16)]
    return np.stack(parts)


def fill_tables(parts_ref, table_refs):
    width = parts_ref.shape[-1]
    right_ref, left_ref, back_left_ref, back_right_ref = table_refs
    for level, places in ((0, (0, 2)), (1, (1,))):
        cosine = parts_ref[level]
        sine = parts_ref[2 + level]
        for place in places:
            start = place * 2 * width
            for i in range(2):
                for j in range(2):
                    value = cosine if i == j else (-sine if i == 0 else sine)
                    turned = cosine if i == j else (sine if i == 0 else -sine)
                    tall = (slice(start + i * width, start + (i + 1) * width), slice(j * width, (j + 1) * width))
                    wide = (slice(i * width, (i + 1) * width), slice(start + j * width, start + (j + 1) * width))
                    right_ref[tall] = value
                    back_right_ref[tall] = turned
                    left_ref[wide] = turned
                    back_left_ref[wide] = value


def times_right(values, table):
    high, low = split(values)
    return jnp.dot(
        jnp.concatenate([high, high, low], axis=1), table, preferred_element_type=jnp.float32
    )


def times_left(table, values):
    high, low = split(values)
    return jnp.dot(
        table, jnp.concatenate([high, high, low], axis=0), preferred_element_type=jnp.float32
    )


def regroup(values, width):
    blocks = values.shape[0] // width
    return jnp.concatenate(
        [
            jnp.concatenate(
                [values[b * width : (b + 1) * width, p * width : (p + 1) * width] for b in range(blocks)],
                axis=1,
            )
            for p in range(2)
        ],
        axis=0,
    )


def ungroup(values, width):
    blocks = values.shape[1] // width
    return jnp.concatenate(
        [
            jnp.concatenate(
                [values[p * width : (p + 1) * width, b * width : (b + 1) * width] for p in range(2)],
                axis=1,
            )
            for b in range(blocks)
        ],
        axis=0,
    )


def make_slots(positions_ref, first_row, field_ref, grad_ref, probe_ref, measured_ref, sums_ref, table_refs):
    width = PATCH
    modes = probe_ref.shape[1]
    tall = width + 8
    right_table, left_table, back_left, back_right = table_refs
    lane = lax.broadcasted_iota(jnp.int32, (tall, width), 1)
    sublane = lax.broadcasted_iota(jnp.int32, (tall // 8, 8, width), 1)

    def place(index):
        row = positions_ref[0, index] - first_row
        col = positions_ref[1, index]
        down = lax.rem(row, 8)
        shift = lax.rem(col, width)
        return (pl.multiple_of(row - down, 8), down, pl.multiple_of(col - shift, width), shift)

    def cut(plane, top, down, base, shift):
        near = field_ref[plane, pl.ds(top, tall), pl.ds(base, width)]
        far = field_ref[plane, pl.ds(top, tall), pl.ds(base + width, width)]
        back_by = lax.rem(width - shift, width)
        turned = jnp.where(
            lane < width - shift,
            pltpu.roll(near, back_by, axis=1),
            pltpu.roll(far, back_by, axis=1),
        )
        turned = pltpu.roll(turned.reshape(tall // 8, 8, width), lax.rem(8 - down, 8), axis=1)
        picked = jnp.where(sublane[1:] < 8 - down, turned[:-1], turned[1:])
        return picked.reshape(width, width)

    def paste(plane, top, down, base, shift, values):
        turned = pltpu.roll(values, shift, axis=1).reshape(width // 8, 8, width)
        turned = pltpu.roll(turned, down, axis=1)
        blank = jnp.zeros((1, 8, width), jnp.float32)
        moved = jnp.where(
            sublane >= down,
            jnp.concatenate([turned, blank], axis=0),
            jnp.concatenate([blank, turned], axis=0),
        ).reshape(tall, width)
        grad_ref[plane, pl.ds(top, tall), pl.ds(base, width)] += jnp.where(
            lane >= shift, moved, 0.0
        )
        grad_ref[plane, pl.ds(top, tall), pl.ds(base + width, width)] += jnp.where(
            lane < shift, moved, 0.0
        )

    def slots(indices):
        places = [place(index) for index in indices]
        patches = [(cut(0, *at), cut(1, *at)) for at in places]
        exits = []
        for patch_real, patch_imag in patches:
            for mode in range(modes):
                mode_real, mode_imag = (probe_ref[0, mode], probe_ref[1, mode])
                exits.append(
                    jnp.concatenate(
                        [
                            mode_real * patch_real - mode_imag * patch_imag,
                            mode_real * patch_imag + mode_imag * patch_real,
                        ],
                        axis=1,
                    )
                )
        rows = times_right(jnp.concatenate(exits, axis=0), right_table[...])
        far = times_left(left_table[...], regroup(rows, width))
        scalings = []
        for order, index in enumerate(indices):
            part = far[:, order * modes * width : (order + 1) * modes * width]
            power = part * part
            power = power[:width] + power[width:]
            intensity = sum(power[:, m * width : (m + 1) * width] for m in range(modes))
            scaling = (
                measured_ref[index] * lax.rsqrt(jnp.maximum(intensity, AMP_FLOOR * AMP_FLOOR)) - 1.0
            )
            scalings += [scaling] * modes
        scaling = jnp.concatenate(scalings, axis=1)
        rows = times_left(back_left[...], far * jnp.concatenate([scaling, scaling], axis=0))
        back = times_right(ungroup(rows, width), back_right[...])
        sums = [[0.0] * modes, [0.0] * modes]
        density = 0.0
        for order, (patch_real, patch_imag) in enumerate(patches):
            object_real, object_imag = (0.0, 0.0)
            for mode in range(modes):
                mode_real, mode_imag = (probe_ref[0, mode], probe_ref[1, mode])
                start = (order * modes + mode) * width
                back_real = back[start : start + width, :width]
                back_imag = back[start : start + width, width:]
                object_real += mode_real * back_real + mode_imag * back_imag
                object_imag += mode_real * back_imag - mode_imag * back_real
                sums[0][mode] += patch_real * back_real + patch_imag * back_imag
                sums[1][mode] += patch_real * back_imag - patch_imag * back_real
            density += patch_real * patch_real + patch_imag * patch_imag
            paste(0, *places[order], object_real)
            paste(1, *places[order], object_imag)
        for part in range(2):
            for mode in range(modes):
                sums_ref[part, mode] += sums[part][mode]
        sums_ref[2, 0] += density

    return slots


def run_slots(positions_ref, counts_ref, order_ref, slots, wanted):

    def note(index, found):
        order_ref[found] = index
        return found + wanted(positions_ref[0, index]).astype(jnp.int32)

    found = lax.fori_loop(0, counts_ref[0], note, jnp.int32(0))

    def run(start, stop, size):

        def step(turn, carry):
            slots([order_ref[start + turn * size + i] for i in range(size)])
            return carry

        turns = lax.div(stop - start, size)
        lax.fori_loop(0, turns, step, 0)
        return start + turns * size

    reached = run(0, found, 4)
    reached = run(reached, found, 2)
    run(reached, found, 1)


def upper_kernel(
    positions_ref, counts_ref, own_ref, right_ref, probe_ref, measured_ref, parts_ref,
    grad_ref, sums_ref, field_ref, order_ref, *table_refs,
):
    tile_height, tile_width = own_ref.shape[1:]
    fill_tables(parts_ref, table_refs)
    field_ref[:, :tile_height, :tile_width] = own_ref[...]
    field_ref[:, :tile_height, tile_width:] = right_ref[...]
    grad_ref[...] = jnp.zeros_like(grad_ref)
    sums_ref[...] = jnp.zeros_like(sums_ref)
    slots = make_slots(positions_ref, 0, field_ref, grad_ref, probe_ref, measured_ref, sums_ref, table_refs)
    run_slots(positions_ref, counts_ref, order_ref, slots, lambda row: row <= tile_height - PATCH)


def lower_kernel(
    positions_ref, counts_ref, last_ref, own_ref, direct_ref, side_ref, far_ref, right_ref, corner_ref,
    probe_ref, measured_ref, parts_ref, upper_ref, upper_sums_ref,
    grad_own_ref, grad_right_ref, grad_corner_ref, grad_lower_ref, packed_ref,
    field_ref, grad_ref, sums_ref, order_ref, *table_refs,
):
    tile_height, tile_width = own_ref.shape[1:]
    first = tile_height - PATCH
    fill_tables(parts_ref, table_refs)
    field_ref[:, :PATCH, :tile_width] = own_ref[:, first:]
    field_ref[:, PATCH : PATCH + DIRECT, :tile_width] = direct_ref[...]

    @pl.when(last_ref[0] == 1)
    def _():
        field_ref[:, PATCH + DIRECT :, :tile_width] = far_ref[...]

    @pl.when(last_ref[0] == 0)
    def _():
        field_ref[:, PATCH + DIRECT :, :tile_width] = side_ref[...]

    field_ref[:, :PATCH, tile_width:] = right_ref[:, first:]
    field_ref[:, PATCH:, tile_width:] = corner_ref[...]
    grad_ref[:, :PATCH] = upper_ref[:, first:tile_height]
    grad_ref[:, PATCH:] = jnp.zeros_like(grad_ref[:, PATCH:])
    sums_ref[...] = upper_sums_ref[...]
    slots = make_slots(positions_ref, first, field_ref, grad_ref, probe_ref, measured_ref, sums_ref, table_refs)
    run_slots(positions_ref, counts_ref, order_ref, slots, lambda row: row > first)
    for block in range(packed_ref.shape[0]):
        part, mode, start = (block // 16, block // 8 % 2, block % 8 * 16)
        for piece in range(4):
            row = start + piece * 4
            packed_ref[block, piece] = sums_ref[part, mode, row : row + 4]
        packed_ref[block, 4] = sums_ref[2, 0, block * 4 : block * 4 + 4]
    grad_right_ref[:, :first] = upper_ref[:, :first, tile_width:]
    grad_right_ref[:, first:] = grad_ref[:, :PATCH, tile_width:]
    grad_corner_ref[...] = grad_ref[:, PATCH:, tile_width:]
    grad_own_ref[...] = grad_ref[:, :PATCH, :tile_width]
    grad_lower_ref[...] = grad_ref[:, PATCH:, :tile_width]


def float_array(*shape):
    return jax.ShapeDtypeStruct(shape, jnp.float32)


def table_scratch():
    tall = pltpu.VMEM((6 * PATCH, 2 * PATCH), jnp.bfloat16)
    wide = pltpu.VMEM((2 * PATCH, 6 * PATCH), jnp.bfloat16)
    return [tall, wide, wide, tall]


VMEM_SPEC = pl.BlockSpec(memory_space=pltpu.VMEM)
SMEM_SPEC = pl.BlockSpec(memory_space=pltpu.SMEM)
PARAMS = pltpu.CompilerParams(vmem_limit_bytes=24 * 1024 * 1024)


def upper_slots(positions, counts, own, right, probe, measured, parts):
    tile_height, tile_width = own.shape[1:]
    wide = tile_width + PATCH
    return pl.pallas_call(
        upper_kernel,
        in_specs=[SMEM_SPEC] * 2 + [VMEM_SPEC] * 5,
        out_specs=[VMEM_SPEC] * 2,
        out_shape=[float_array(2, tile_height + 8, wide), float_array(3, 2, PATCH, PATCH)],
        scratch_shapes=[
            pltpu.VMEM((2, tile_height + 8, wide), jnp.float32),
            pltpu.SMEM((positions.shape[1],), jnp.int32),
        ]
        + table_scratch(),
        compiler_params=PARAMS,
        cost_estimate=pl.CostEstimate(flops=3_000_000_000, transcendentals=0, bytes_accessed=3_000_000),
        name="upper_slots",
    )(positions, counts, own, right, probe, measured, parts)


def lower_slots(
    positions, counts, last, own, direct, side, far, right, corner, probe, measured, parts, upper, sums
):
    tile_height, tile_width = own.shape[1:]
    wide = tile_width + PATCH
    return pl.pallas_call(
        lower_kernel,
        in_specs=[SMEM_SPEC] * 3 + [VMEM_SPEC] * 11,
        out_specs=[VMEM_SPEC] * 5,
        out_shape=[
            float_array(2, PATCH, tile_width),
            float_array(2, tile_height, PATCH),
            float_array(2, PATCH, PATCH),
            float_array(2, PATCH, tile_width),
            float_array(32, 5, 4, PATCH),
        ],
        scratch_shapes=[
            pltpu.VMEM((2, 2 * PATCH, wide), jnp.float32),
            pltpu.VMEM((2, 2 * PATCH, wide), jnp.float32),
            pltpu.VMEM((3, 2, PATCH, PATCH), jnp.float32),
            pltpu.SMEM((positions.shape[1],), jnp.int32),
        ]
        + table_scratch(),
        compiler_params=PARAMS,
        cost_estimate=pl.CostEstimate(flops=3_000_000_000, transcendentals=0, bytes_accessed=5_000_000),
        name="lower_slots",
    )(positions, counts, last, own, direct, side, far, right, corner, probe, measured, parts, upper, sums)


def object_kernel(
    first_ref, own_ref, upper_ref, lower_ref, spilled_ref, rim_ref, side_ref, far_ref, probe_ref, out_ref
):
    tile_height, tile_width = own_ref.shape[1:]
    first = tile_height - PATCH
    power = probe_ref[...] * probe_ref[...]
    power = power[0, 0] + power[0, 1] + power[1, 0] + power[1, 1]
    weight = 1.0 / (jnp.max(power, axis=(0, 1), keepdims=True) + 1e-06)
    from_far = first_ref[0] == 1
    for plane in range(2):
        for start in range(0, tile_height, PATCH):
            for side in range(0, tile_width, PATCH):
                rows, cols = (slice(start, start + PATCH), slice(side, side + PATCH))
                if start < first:
                    total = upper_ref[plane, rows, cols]
                else:
                    total = lower_ref[plane, :, cols]
                if side == 0:
                    total += spilled_ref[plane, rows, :]
                if start == 0:
                    rest = jnp.where(from_far, far_ref[plane, :, cols], side_ref[plane, :, cols])
                    total += jnp.concatenate([rim_ref[plane, :, cols], rest], axis=0)
                out_ref[plane, rows, cols] = own_ref[plane, rows, cols] + total * weight


def object_update(first, own, upper, lower, spilled, rim, side, far, probe):
    return pl.pallas_call(
        object_kernel,
        in_specs=[SMEM_SPEC] + [VMEM_SPEC] * 8,
        out_specs=VMEM_SPEC,
        out_shape=float_array(*own.shape),
        compiler_params=PARAMS,
        cost_estimate=pl.CostEstimate(flops=OBJECT_COST, transcendentals=0, bytes_accessed=4_000_000),
        name="object_update",
    )(first, own, upper, lower, spilled, rim, side, far, probe)


def probe_kernel(blocks_ref, out_ref, density_ref, weight_ref):
    for block in range(blocks_ref.shape[0]):
        density_ref[block * 4 : block * 4 + 4] = blocks_ref[block, 4]
    weight_ref[...] = lax.rsqrt(density_ref[...] + 1.0)
    for block in range(blocks_ref.shape[0]):
        part, mode, start = (block // 16, block // 8 % 2, block % 8 * 16)
        for piece in range(4):
            row = start + piece * 4
            out_ref[part, mode, row : row + 4] = blocks_ref[block, piece] * weight_ref[row : row + 4]


def probe_update(blocks, shape):
    return pl.pallas_call(
        probe_kernel,
        in_specs=[VMEM_SPEC],
        out_specs=VMEM_SPEC,
        out_shape=float_array(*shape),
        scratch_shapes=[pltpu.VMEM((PATCH, PATCH), jnp.float32)] * 2,
        compiler_params=PARAMS,
        name="probe_update",
    )(blocks)


def halo_kernel(own_ref, side_ref, direct_ref, left_ref, sems):
    pieces = (
        (own_ref.at[:, pl.ds(DIRECT, PATCH - DIRECT), :], side_ref),
        (own_ref.at[:, pl.ds(0, DIRECT), :], direct_ref),
        (own_ref.at[:, :, pl.ds(0, PATCH)], left_ref),
    )
    copies = [
        pltpu.make_async_copy(source, target, sems.at[order])
        for order, (source, target) in enumerate(pieces)
    ]
    for copy in copies:
        copy.start()
    for copy in copies:
        copy.wait()


def halo_pieces(own):
    planes, tile_height, tile_width = own.shape
    return pl.pallas_call(
        halo_kernel,
        in_specs=[pl.BlockSpec(memory_space=pltpu.MemorySpace.HBM)],
        out_specs=[VMEM_SPEC] * 3,
        out_shape=[
            float_array(planes, PATCH - DIRECT, tile_width),
            float_array(planes, DIRECT, tile_width),
            float_array(planes, tile_height, PATCH),
        ],
        scratch_shapes=[pltpu.SemaphoreType.DMA((3,))],
        compiler_params=PARAMS,
        name="halo_pieces",
    )(own)


def corner_kernel(last_ref, direct_ref, side_ref, far_ref, corner_ref):
    from_far = last_ref[0] == 1
    for plane in range(2):
        corner_ref[plane, :DIRECT] = direct_ref[plane, :, :PATCH]
        corner_ref[plane, DIRECT:] = jnp.where(
            from_far, far_ref[plane, :, :PATCH], side_ref[plane, :, :PATCH]
        )


def corner_piece(last, direct, side, far):
    return pl.pallas_call(
        corner_kernel,
        in_specs=[SMEM_SPEC] + [VMEM_SPEC] * 3,
        out_specs=VMEM_SPEC,
        out_shape=float_array(2, PATCH, PATCH),
        compiler_params=PARAMS,
        name="corner_piece",
    )(last, direct, side, far)


def sum_kernel(terms_ref, out_ref):
    total = jnp.sum(terms_ref[...], axis=0)
    out_ref[...] = jnp.broadcast_to(total[None], out_ref.shape)


def sum_for(terms, copies):
    return pl.pallas_call(
        sum_kernel,
        in_specs=[VMEM_SPEC],
        out_specs=VMEM_SPEC,
        out_shape=float_array(copies, *terms.shape[1:]),
        compiler_params=PARAMS,
        name="sum_for",
    )(terms)


def rim_kernel(lower_ref, spilled_ref, direct_ref, side_ref):
    for plane in range(2):
        near = lower_ref[plane, :, :PATCH] + spilled_ref[plane]
        direct_ref[plane, :, :PATCH] = near[:RIM_DIRECT]
        side_ref[plane, :, :PATCH] = near[RIM_DIRECT:]
        direct_ref[plane, :, PATCH:] = lower_ref[plane, :RIM_DIRECT, PATCH:]
        side_ref[plane, :, PATCH:] = lower_ref[plane, RIM_DIRECT:, PATCH:]


def rim_pieces(lower, spilled):
    planes, height, width = lower.shape
    return pl.pallas_call(
        rim_kernel,
        in_specs=[VMEM_SPEC] * 2,
        out_specs=[VMEM_SPEC] * 2,
        out_shape=[
            float_array(planes, RIM_DIRECT, width),
            float_array(planes, height - RIM_DIRECT, width),
        ],
        compiler_params=PARAMS,
        cost_estimate=pl.CostEstimate(flops=RIM_COST, transcendentals=0, bytes_accessed=1_000_000),
        name="rim_pieces",
    )(lower, spilled)


def moved(array, where):
    pairs = []
    for device in range(lax.axis_size("row") * lax.axis_size("col")):
        row, col = divmod(device, lax.axis_size("col"))
        target = where(row)
        if target is not None:
            pairs.append((device, target * lax.axis_size("col") + col))
    return lax.ppermute(array, ("row", "col"), pairs)


def around(row, by):
    return row // RUN * RUN + (row + by) % RUN


def far_up(row):
    return row - RUN if row % RUN == RUN - 1 and row >= RUN else None


def far_down(row):
    return row + RUN if row % RUN == 0 and row + RUN < lax.axis_size("row") else None


def per_device(object_field, probe_modes, measured, positions, counts):
    planes, lines = device_groups(lax.axis_size("row") * lax.axis_size("col"))
    places, live, amplitudes = (positions[0, 0], counts[0], measured[0, 0])
    parts = jnp.asarray(fourier_parts(PATCH))
    place = lax.axis_index("row") % RUN
    side_rows, direct_rows, left_columns = halo_pieces(
        pltpu.with_memory_space_constraint(object_field, pltpu.MemorySpace.HBM)
    )
    side = moved(side_rows, lambda row: around(row, -1))
    direct = shifted(direct_rows, "row", -1)
    far = moved(side, far_up)
    right = shifted(left_columns, "col", -1)
    upper, upper_sums = upper_slots(
        places, live, object_field, right, probe_modes, amplitudes, parts
    )
    direct, side, far, upper_sums = lax.optimization_barrier((direct, side, far, upper_sums))
    last = (place == RUN - 1).astype(jnp.int32)[None]
    corner = shifted(corner_piece(last, direct, side, far), "col", -1)
    lower, grad_right, grad_corner, grad_lower, packed = lower_slots(
        places, live, last, object_field, direct, side, far, right, corner,
        probe_modes, amplitudes, parts, upper, upper_sums,
    )
    spilled = shifted(grad_right, "col", 1)
    spilled_corner = shifted(grad_corner, "col", 1)
    rim_direct, rim_side = rim_pieces(grad_lower, spilled_corner)
    rim_direct = shifted(rim_direct, "row", 1)
    rim_side = moved(rim_side, lambda row: around(row, 1))
    rim_far = moved(rim_side, far_down)
    terms = exchange(packed, planes)
    terms = exchange(sum_for(terms, len(lines[0])), lines)
    blocks = exchange(sum_for(terms, len(planes[0])), planes)
    object_new = object_update(
        (place == 0).astype(jnp.int32)[None],
        object_field, upper, lower, spilled, rim_direct, rim_side, rim_far, probe_modes,
    )
    probe_step = probe_update(blocks, probe_modes.shape)
    return (object_new, probe_step)


def solution(mesh):
    in_specs = (
        P(None, "row", "col"),
        P(),
        P("row", "col", None, None, None),
        P("row", "col", None, None),
        P("row", "col"),
    )
    out_specs = (P(None, "row", "col"), P())
    return jax.shard_map(
        per_device, mesh=mesh, in_specs=in_specs, out_specs=out_specs, check_vma=False
    )
```

```python
import math

import jax
import jax.numpy as jnp
import numpy as np
from jax import lax
from jax.experimental import pallas as pl
from jax.experimental.pallas import tpu as pltpu
from jax.sharding import PartitionSpec as P

AMP_FLOOR = 0.25
PATCH = 128
RUN = 4
DIRECT = 80
RIM_DIRECT = 72
RIM_COST = 10_000_000_000
OBJECT_COST = 30_000_000_000


def shifted(array, axis, by):
    length = lax.axis_size(axis)
    pairs = [(i, i + by) for i in range(length) if 0 <= i + by < length]
    return lax.ppermute(array, axis, pairs)


def coordinates(device):
    row, col = divmod(device, 32)
    z_hi, x = divmod(row, 4)
    z_lo, rest = divmod(col, 8)
    y, core = divmod(rest, 2)
    return (z_hi * 4 + z_lo, x, y, core)


def device_groups(devices):
    planes, lines = {}, {}
    for device in range(devices):
        z, x, y, core = coordinates(device)
        planes.setdefault(z, []).append(device)
        lines.setdefault((x, y, core), []).append(device)
    return (list(planes.values()), list(lines.values()))


def exchange(blocks, groups):
    return lax.all_to_all(blocks, ("row", "col"), 0, 0, axis_index_groups=groups)


def split(values):
    high = values.astype(jnp.bfloat16)
    low = (values - high.astype(jnp.float32)).astype(jnp.bfloat16)
    return (high, low)


def fourier_parts(width):
    index = np.arange(width)
    angle = (index[:, None] * index[None, :] % width) * (2.0 * math.pi / width)
    parts = []
    for wave in (np.cos(angle), np.sin(angle)):
        values = (wave / math.sqrt(width)).astype(np.float32)
        high = values.astype(jnp.bfloat16)
        parts += [high, (values - high.astype(np.float32)).astype(jnp.bfloat16)]
    return np.stack(parts)


def fill_tables(parts_ref, table_refs):
    width = parts_ref.shape[-1]
    right_ref, left_ref, back_left_ref, back_right_ref = table_refs
    for level, places in ((0, (0, 2)), (1, (1,))):
        cosine = parts_ref[level]
        sine = parts_ref[2 + level]
        for place in places:
            start = place * 2 * width
            for i in range(2):
                for j in range(2):
                    value = cosine if i == j else (-sine if i == 0 else sine)
                    turned = cosine if i == j else (sine if i == 0 else -sine)
                    tall = (slice(start + i * width, start + (i + 1) * width), slice(j * width, (j + 1) * width))
                    wide = (slice(i * width, (i + 1) * width), slice(start + j * width, start + (j + 1) * width))
                    right_ref[tall] = value
                    back_right_ref[tall] = turned
                    left_ref[wide] = turned
                    back_left_ref[wide] = value


def times_right(values, table):
    high, low = split(values)
    return jnp.dot(
        jnp.concatenate([high, high, low], axis=1), table, preferred_element_type=jnp.float32
    )


def times_left(table, values):
    high, low = split(values)
    return jnp.dot(
        table, jnp.concatenate([high, high, low], axis=0), preferred_element_type=jnp.float32
    )


def regroup(values, width):
    blocks = values.shape[0] // width
    return jnp.concatenate(
        [
            jnp.concatenate(
                [values[b * width : (b + 1) * width, p * width : (p + 1) * width] for b in range(blocks)],
                axis=1,
            )
            for p in range(2)
        ],
        axis=0,
    )


def ungroup(values, width):
    blocks = values.shape[1] // width
    return jnp.concatenate(
        [
            jnp.concatenate(
                [values[p * width : (p + 1) * width, b * width : (b + 1) * width] for p in range(2)],
                axis=1,
            )
            for b in range(blocks)
        ],
        axis=0,
    )


def make_slots(positions_ref, first_row, field_ref, grad_ref, probe_ref, measured_ref, sums_ref, table_refs):
    width = PATCH
    modes = probe_ref.shape[1]
    tall = width + 8
    right_table, left_table, back_left, back_right = table_refs
    lane = lax.broadcasted_iota(jnp.int32, (tall, width), 1)
    sublane = lax.broadcasted_iota(jnp.int32, (tall // 8, 8, width), 1)

    def place(index):
        row = positions_ref[0, index] - first_row
        col = positions_ref[1, index]
        down = lax.rem(row, 8)
        shift = lax.rem(col, width)
        return (pl.multiple_of(row - down, 8), down, pl.multiple_of(col - shift, width), shift)

    def cut(plane, top, down, base, shift):
        near = field_ref[plane, pl.ds(top, tall), pl.ds(base, width)]
        far = field_ref[plane, pl.ds(top, tall), pl.ds(base + width, width)]
        back_by = lax.rem(width - shift, width)
        turned = jnp.where(
            lane < width - shift,
            pltpu.roll(near, back_by, axis=1),
            pltpu.roll(far, back_by, axis=1),
        )
        turned = pltpu.roll(turned.reshape(tall // 8, 8, width), lax.rem(8 - down, 8), axis=1)
        picked = jnp.where(sublane[1:] < 8 - down, turned[:-1], turned[1:])
        return picked.reshape(width, width)

    def paste(plane, top, down, base, shift, values):
        turned = pltpu.roll(values, shift, axis=1).reshape(width // 8, 8, width)
        turned = pltpu.roll(turned, down, axis=1)
        blank = jnp.zeros((1, 8, width), jnp.float32)
        moved = jnp.where(
            sublane >= down,
            jnp.concatenate([turned, blank], axis=0),
            jnp.concatenate([blank, turned], axis=0),
        ).reshape(tall, width)
        grad_ref[plane, pl.ds(top, tall), pl.ds(base, width)] += jnp.where(
            lane >= shift, moved, 0.0
        )
        grad_ref[plane, pl.ds(top, tall), pl.ds(base + width, width)] += jnp.where(
            lane < shift, moved, 0.0
        )

    def slots(indices):
        places = [place(index) for index in indices]
        patches = [(cut(0, *at), cut(1, *at)) for at in places]
        exits = []
        for patch_real, patch_imag in patches:
            for mode in range(modes):
                mode_real, mode_imag = (probe_ref[0, mode], probe_ref[1, mode])
                exits.append(
                    jnp.concatenate(
                        [
                            mode_real * patch_real - mode_imag * patch_imag,
                            mode_real * patch_imag + mode_imag * patch_real,
                        ],
                        axis=1,
                    )
                )
        rows = times_right(jnp.concatenate(exits, axis=0), right_table[...])
        far = times_left(left_table[...], regroup(rows, width))
        scalings = []
        for order, index in enumerate(indices):
            part = far[:, order * modes * width : (order + 1) * modes * width]
            power = part * part
            power = power[:width] + power[width:]
            intensity = sum(power[:, m * width : (m + 1) * width] for m in range(modes))
            scaling = (
                measured_ref[index] * lax.rsqrt(jnp.maximum(intensity, AMP_FLOOR * AMP_FLOOR)) - 1.0
            )
            scalings += [scaling] * modes
        scaling = jnp.concatenate(scalings, axis=1)
        rows = times_left(back_left[...], far * jnp.concatenate([scaling, scaling], axis=0))
        back = times_right(ungroup(rows, width), back_right[...])
        sums = [[0.0] * modes, [0.0] * modes]
        density = 0.0
        for order, (patch_real, patch_imag) in enumerate(patches):
            object_real, object_imag = (0.0, 0.0)
            for mode in range(modes):
                mode_real, mode_imag = (probe_ref[0, mode], probe_ref[1, mode])
                start = (order * modes + mode) * width
                back_real = back[start : start + width, :width]
                back_imag = back[start : start + width, width:]
                object_real += mode_real * back_real + mode_imag * back_imag
                object_imag += mode_real * back_imag - mode_imag * back_real
                sums[0][mode] += patch_real * back_real + patch_imag * back_imag
                sums[1][mode] += patch_real * back_imag - patch_imag * back_real
            density += patch_real * patch_real + patch_imag * patch_imag
            paste(0, *places[order], object_real)
            paste(1, *places[order], object_imag)
        for part in range(2):
            for mode in range(modes):
                sums_ref[part, mode] += sums[part][mode]
        sums_ref[2, 0] += density

    return slots


def run_slots(positions_ref, counts_ref, order_ref, slots, wanted):

    def note(index, found):
        order_ref[found] = index
        return found + wanted(positions_ref[0, index]).astype(jnp.int32)

    found = lax.fori_loop(0, counts_ref[0], note, jnp.int32(0))

    def run(start, stop, size):

        def step(turn, carry):
            slots([order_ref[start + turn * size + i] for i in range(size)])
            return carry

        turns = lax.div(stop - start, size)
        lax.fori_loop(0, turns, step, 0)
        return start + turns * size

    reached = run(0, found, 4)
    reached = run(reached, found, 2)
    run(reached, found, 1)


def upper_kernel(
    positions_ref, counts_ref, own_ref, right_ref, probe_ref, measured_ref, parts_ref,
    grad_ref, sums_ref, field_ref, order_ref, *table_refs,
):
    tile_height, tile_width = own_ref.shape[1:]
    fill_tables(parts_ref, table_refs)
    field_ref[:, :tile_height, :tile_width] = own_ref[...]
    field_ref[:, :tile_height, tile_width:] = right_ref[...]
    grad_ref[...] = jnp.zeros_like(grad_ref)
    sums_ref[...] = jnp.zeros_like(sums_ref)
    slots = make_slots(positions_ref, 0, field_ref, grad_ref, probe_ref, measured_ref, sums_ref, table_refs)
    run_slots(positions_ref, counts_ref, order_ref, slots, lambda row: row <= tile_height - PATCH)


def lower_kernel(
    positions_ref, counts_ref, last_ref, own_ref, direct_ref, side_ref, far_ref, right_ref, corner_ref,
    probe_ref, measured_ref, parts_ref, upper_ref, upper_sums_ref,
    grad_own_ref, grad_right_ref, grad_corner_ref, grad_lower_ref, packed_ref,
    field_ref, grad_ref, sums_ref, order_ref, *table_refs,
):
    tile_height, tile_width = own_ref.shape[1:]
    first = tile_height - PATCH
    fill_tables(parts_ref, table_refs)
    field_ref[:, :PATCH, :tile_width] = own_ref[:, first:]
    field_ref[:, PATCH : PATCH + DIRECT, :tile_width] = direct_ref[...]

    @pl.when(last_ref[0] == 1)
    def _():
        field_ref[:, PATCH + DIRECT :, :tile_width] = far_ref[...]

    @pl.when(last_ref[0] == 0)
    def _():
        field_ref[:, PATCH + DIRECT :, :tile_width] = side_ref[...]

    field_ref[:, :PATCH, tile_width:] = right_ref[:, first:]
    field_ref[:, PATCH:, tile_width:] = corner_ref[...]
    grad_ref[:, :PATCH] = upper_ref[:, first:tile_height]
    grad_ref[:, PATCH:] = jnp.zeros_like(grad_ref[:, PATCH:])
    sums_ref[...] = upper_sums_ref[...]
    slots = make_slots(positions_ref, first, field_ref, grad_ref, probe_ref, measured_ref, sums_ref, table_refs)
    run_slots(positions_ref, counts_ref, order_ref, slots, lambda row: row > first)
    for block in range(packed_ref.shape[0]):
        part, mode, start = (block // 16, block // 8 % 2, block % 8 * 16)
        for piece in range(4):
            row = start + piece * 4
            packed_ref[block, piece] = sums_ref[part, mode, row : row + 4]
        packed_ref[block, 4] = sums_ref[2, 0, block * 4 : block * 4 + 4]
    grad_right_ref[:, :first] = upper_ref[:, :first, tile_width:]
    grad_right_ref[:, first:] = grad_ref[:, :PATCH, tile_width:]
    grad_corner_ref[...] = grad_ref[:, PATCH:, tile_width:]
    grad_own_ref[...] = grad_ref[:, :PATCH, :tile_width]
    grad_lower_ref[...] = grad_ref[:, PATCH:, :tile_width]


def float_array(*shape):
    return jax.ShapeDtypeStruct(shape, jnp.float32)


def table_scratch():
    tall = pltpu.VMEM((6 * PATCH, 2 * PATCH), jnp.bfloat16)
    wide = pltpu.VMEM((2 * PATCH, 6 * PATCH), jnp.bfloat16)
    return [tall, wide, wide, tall]


VMEM_SPEC = pl.BlockSpec(memory_space=pltpu.VMEM)
SMEM_SPEC = pl.BlockSpec(memory_space=pltpu.SMEM)
PARAMS = pltpu.CompilerParams(vmem_limit_bytes=24 * 1024 * 1024)


def upper_slots(positions, counts, own, right, probe, measured, parts):
    tile_height, tile_width = own.shape[1:]
    wide = tile_width + PATCH
    return pl.pallas_call(
        upper_kernel,
        in_specs=[SMEM_SPEC] * 2 + [VMEM_SPEC] * 5,
        out_specs=[VMEM_SPEC] * 2,
        out_shape=[float_array(2, tile_height + 8, wide), float_array(3, 2, PATCH, PATCH)],
        scratch_shapes=[
            pltpu.VMEM((2, tile_height + 8, wide), jnp.float32),
            pltpu.SMEM((positions.shape[1],), jnp.int32),
        ]
        + table_scratch(),
        compiler_params=PARAMS,
        cost_estimate=pl.CostEstimate(flops=3_000_000_000, transcendentals=0, bytes_accessed=3_000_000),
        name="upper_slots",
    )(positions, counts, own, right, probe, measured, parts)


def lower_slots(
    positions, counts, last, own, direct, side, far, right, corner, probe, measured, parts, upper, sums
):
    tile_height, tile_width = own.shape[1:]
    wide = tile_width + PATCH
    return pl.pallas_call(
        lower_kernel,
        in_specs=[SMEM_SPEC] * 3 + [VMEM_SPEC] * 11,
        out_specs=[VMEM_SPEC] * 5,
        out_shape=[
            float_array(2, PATCH, tile_width),
            float_array(2, tile_height, PATCH),
            float_array(2, PATCH, PATCH),
            float_array(2, PATCH, tile_width),
            float_array(32, 5, 4, PATCH),
        ],
        scratch_shapes=[
            pltpu.VMEM((2, 2 * PATCH, wide), jnp.float32),
            pltpu.VMEM((2, 2 * PATCH, wide), jnp.float32),
            pltpu.VMEM((3, 2, PATCH, PATCH), jnp.float32),
            pltpu.SMEM((positions.shape[1],), jnp.int32),
        ]
        + table_scratch(),
        compiler_params=PARAMS,
        cost_estimate=pl.CostEstimate(flops=3_000_000_000, transcendentals=0, bytes_accessed=5_000_000),
        name="lower_slots",
    )(positions, counts, last, own, direct, side, far, right, corner, probe, measured, parts, upper, sums)


def object_kernel(
    first_ref, own_ref, upper_ref, lower_ref, spilled_ref, rim_ref, side_ref, far_ref, probe_ref, out_ref
):
    tile_height, tile_width = own_ref.shape[1:]
    first = tile_height - PATCH
    power = probe_ref[...] * probe_ref[...]
    power = power[0, 0] + power[0, 1] + power[1, 0] + power[1, 1]
    weight = 1.0 / (jnp.max(power, axis=(0, 1), keepdims=True) + 1e-06)
    from_far = first_ref[0] == 1
    for plane in range(2):
        for start in range(0, tile_height, PATCH):
            for side in range(0, tile_width, PATCH):
                rows, cols = (slice(start, start + PATCH), slice(side, side + PATCH))
                if start < first:
                    total = upper_ref[plane, rows, cols]
                else:
                    total = lower_ref[plane, :, cols]
                if side == 0:
                    total += spilled_ref[plane, rows, :]
                if start == 0:
                    rest = jnp.where(from_far, far_ref[plane, :, cols], side_ref[plane, :, cols])
                    total += jnp.concatenate([rim_ref[plane, :, cols], rest], axis=0)
                out_ref[plane, rows, cols] = own_ref[plane, rows, cols] + total * weight


def object_update(first, own, upper, lower, spilled, rim, side, far, probe):
    return pl.pallas_call(
        object_kernel,
        in_specs=[SMEM_SPEC] + [VMEM_SPEC] * 8,
        out_specs=VMEM_SPEC,
        out_shape=float_array(*own.shape),
        compiler_params=PARAMS,
        cost_estimate=pl.CostEstimate(flops=OBJECT_COST, transcendentals=0, bytes_accessed=4_000_000),
        name="object_update",
    )(first, own, upper, lower, spilled, rim, side, far, probe)


def probe_kernel(blocks_ref, out_ref, density_ref, weight_ref):
    for block in range(blocks_ref.shape[0]):
        density_ref[block * 4 : block * 4 + 4] = blocks_ref[block, 4]
    weight_ref[...] = lax.rsqrt(density_ref[...] + 1.0)
    for block in range(blocks_ref.shape[0]):
        part, mode, start = (block // 16, block // 8 % 2, block % 8 * 16)
        for piece in range(4):
            row = start + piece * 4
            out_ref[part, mode, row : row + 4] = blocks_ref[block, piece] * weight_ref[row : row + 4]


def probe_update(blocks, shape):
    return pl.pallas_call(
        probe_kernel,
        in_specs=[VMEM_SPEC],
        out_specs=VMEM_SPEC,
        out_shape=float_array(*shape),
        scratch_shapes=[pltpu.VMEM((PATCH, PATCH), jnp.float32)] * 2,
        compiler_params=PARAMS,
        name="probe_update",
    )(blocks)


def halo_kernel(own_ref, side_ref, direct_ref, left_ref, sems):
    pieces = (
        (own_ref.at[:, pl.ds(DIRECT, PATCH - DIRECT), :], side_ref),
        (own_ref.at[:, pl.ds(0, DIRECT), :], direct_ref),
        (own_ref.at[:, :, pl.ds(0, PATCH)], left_ref),
    )
    copies = [
        pltpu.make_async_copy(source, target, sems.at[order])
        for order, (source, target) in enumerate(pieces)
    ]
    for copy in copies:
        copy.start()
    for copy in copies:
        copy.wait()


def halo_pieces(own):
    planes, tile_height, tile_width = own.shape
    return pl.pallas_call(
        halo_kernel,
        in_specs=[pl.BlockSpec(memory_space=pltpu.MemorySpace.HBM)],
        out_specs=[VMEM_SPEC] * 3,
        out_shape=[
            float_array(planes, PATCH - DIRECT, tile_width),
            float_array(planes, DIRECT, tile_width),
            float_array(planes, tile_height, PATCH),
        ],
        scratch_shapes=[pltpu.SemaphoreType.DMA((3,))],
        compiler_params=PARAMS,
        name="halo_pieces",
    )(own)


def corner_kernel(last_ref, direct_ref, side_ref, far_ref, corner_ref):
    from_far = last_ref[0] == 1
    for plane in range(2):
        corner_ref[plane, :DIRECT] = direct_ref[plane, :, :PATCH]
        corner_ref[plane, DIRECT:] = jnp.where(
            from_far, far_ref[plane, :, :PATCH], side_ref[plane, :, :PATCH]
        )


def corner_piece(last, direct, side, far):
    return pl.pallas_call(
        corner_kernel,
        in_specs=[SMEM_SPEC] + [VMEM_SPEC] * 3,
        out_specs=VMEM_SPEC,
        out_shape=float_array(2, PATCH, PATCH),
        compiler_params=PARAMS,
        name="corner_piece",
    )(last, direct, side, far)


def sum_kernel(terms_ref, out_ref):
    total = jnp.sum(terms_ref[...], axis=0)
    out_ref[...] = jnp.broadcast_to(total[None], out_ref.shape)


def sum_for(terms, copies):
    return pl.pallas_call(
        sum_kernel,
        in_specs=[VMEM_SPEC],
        out_specs=VMEM_SPEC,
        out_shape=float_array(copies, *terms.shape[1:]),
        compiler_params=PARAMS,
        name="sum_for",
    )(terms)


def rim_kernel(lower_ref, spilled_ref, direct_ref, side_ref):
    for plane in range(2):
        near = lower_ref[plane, :, :PATCH] + spilled_ref[plane]
        direct_ref[plane, :, :PATCH] = near[:RIM_DIRECT]
        side_ref[plane, :, :PATCH] = near[RIM_DIRECT:]
        direct_ref[plane, :, PATCH:] = lower_ref[plane, :RIM_DIRECT, PATCH:]
        side_ref[plane, :, PATCH:] = lower_ref[plane, RIM_DIRECT:, PATCH:]


def rim_pieces(lower, spilled):
    planes, height, width = lower.shape
    return pl.pallas_call(
        rim_kernel,
        in_specs=[VMEM_SPEC] * 2,
        out_specs=[VMEM_SPEC] * 2,
        out_shape=[
            float_array(planes, RIM_DIRECT, width),
            float_array(planes, height - RIM_DIRECT, width),
        ],
        compiler_params=PARAMS,
        cost_estimate=pl.CostEstimate(flops=RIM_COST, transcendentals=0, bytes_accessed=1_000_000),
        name="rim_pieces",
    )(lower, spilled)


def moved(array, where):
    pairs = []
    for device in range(lax.axis_size("row") * lax.axis_size("col")):
        row, col = divmod(device, lax.axis_size("col"))
        target = where(row)
        if target is not None:
            pairs.append((device, target * lax.axis_size("col") + col))
    return lax.ppermute(array, ("row", "col"), pairs)


def around(row, by):
    return row // RUN * RUN + (row + by) % RUN


def far_up(row):
    return row - RUN if row % RUN == RUN - 1 and row >= RUN else None


def far_down(row):
    return row + RUN if row % RUN == 0 and row + RUN < lax.axis_size("row") else None


def per_device(object_field, probe_modes, measured, positions, counts):
    planes, lines = device_groups(lax.axis_size("row") * lax.axis_size("col"))
    places, live, amplitudes = (positions[0, 0], counts[0], measured[0, 0])
    parts = jnp.asarray(fourier_parts(PATCH))
    place = lax.axis_index("row") % RUN
    side_rows, direct_rows, left_columns = halo_pieces(
        pltpu.with_memory_space_constraint(object_field, pltpu.MemorySpace.HBM)
    )
    side = moved(side_rows, lambda row: around(row, -1))
    direct = shifted(direct_rows, "row", -1)
    far = moved(side, far_up)
    right = shifted(left_columns, "col", -1)
    upper, upper_sums = upper_slots(
        places, live, object_field, right, probe_modes, amplitudes, parts
    )
    direct, side, far, upper_sums = lax.optimization_barrier((direct, side, far, upper_sums))
    last = (place == RUN - 1).astype(jnp.int32)[None]
    corner = shifted(corner_piece(last, direct, side, far), "col", -1)
    lower, grad_right, grad_corner, grad_lower, packed = lower_slots(
        places, live, last, object_field, direct, side, far, right, corner,
        probe_modes, amplitudes, parts, upper, upper_sums,
    )
    spilled = shifted(grad_right, "col", 1)
    spilled_corner = shifted(grad_corner, "col", 1)
    rim_direct, rim_side = rim_pieces(grad_lower, spilled_corner)
    rim_side = moved(rim_side, lambda row: around(row, 1))
    terms = exchange(packed, planes)
    terms, rim_side, rim_direct = lax.optimization_barrier((terms, rim_side, rim_direct))
    rim_direct = shifted(rim_direct, "row", 1)
    rim_far = moved(rim_side, far_down)
    terms = exchange(sum_for(terms, len(lines[0])), lines)
    blocks = exchange(sum_for(terms, len(planes[0])), planes)
    object_new = object_update(
        (place == 0).astype(jnp.int32)[None],
        object_field, upper, lower, spilled, rim_direct, rim_side, rim_far, probe_modes,
    )
    probe_step = probe_update(blocks, probe_modes.shape)
    return (object_new, probe_step)


def solution(mesh):
    in_specs = (
        P(None, "row", "col"),
        P(),
        P("row", "col", None, None, None),
        P("row", "col", None, None),
        P("row", "col"),
    )
    out_specs = (P(None, "row", "col"), P())
    return jax.shard_map(
        per_device, mesh=mesh, in_specs=in_specs, out_specs=out_specs, check_vma=False
    )
```

```python
import math

import jax
import jax.numpy as jnp
import numpy as np
from jax import lax
from jax.experimental import pallas as pl
from jax.experimental.pallas import tpu as pltpu
from jax.sharding import PartitionSpec as P

AMP_FLOOR = 0.25
PATCH = 128
RUN = 4
DIRECT = 80
RIM_DIRECT = 72
RIM_COST = 10_000_000_000
OBJECT_COST = 30_000_000_000


def shifted(array, axis, by):
    length = lax.axis_size(axis)
    pairs = [(i, i + by) for i in range(length) if 0 <= i + by < length]
    return lax.ppermute(array, axis, pairs)


def coordinates(device):
    row, col = divmod(device, 32)
    z_hi, x = divmod(row, 4)
    z_lo, rest = divmod(col, 8)
    y, core = divmod(rest, 2)
    return (z_hi * 4 + z_lo, x, y, core)


def device_groups(devices):
    planes, lines = {}, {}
    for device in range(devices):
        z, x, y, core = coordinates(device)
        planes.setdefault(z, []).append(device)
        lines.setdefault((x, y, core), []).append(device)
    return (list(planes.values()), list(lines.values()))


def exchange(blocks, groups):
    return lax.all_to_all(blocks, ("row", "col"), 0, 0, axis_index_groups=groups)


def split(values):
    high = values.astype(jnp.bfloat16)
    low = (values - high.astype(jnp.float32)).astype(jnp.bfloat16)
    return (high, low)


def fourier_parts(width):
    index = np.arange(width)
    angle = (index[:, None] * index[None, :] % width) * (2.0 * math.pi / width)
    parts = []
    for wave in (np.cos(angle), np.sin(angle)):
        values = (wave / math.sqrt(width)).astype(np.float32)
        high = values.astype(jnp.bfloat16)
        parts += [high, (values - high.astype(np.float32)).astype(jnp.bfloat16)]
    return np.stack(parts)


def fill_tables(parts_ref, table_refs):
    width = parts_ref.shape[-1]
    right_ref, left_ref, back_left_ref, back_right_ref = table_refs
    for level, places in ((0, (0, 2)), (1, (1,))):
        cosine = parts_ref[level]
        sine = parts_ref[2 + level]
        for place in places:
            start = place * 2 * width
            for i in range(2):
                for j in range(2):
                    value = cosine if i == j else (-sine if i == 0 else sine)
                    turned = cosine if i == j else (sine if i == 0 else -sine)
                    tall = (slice(start + i * width, start + (i + 1) * width), slice(j * width, (j + 1) * width))
                    wide = (slice(i * width, (i + 1) * width), slice(start + j * width, start + (j + 1) * width))
                    right_ref[tall] = value
                    back_right_ref[tall] = turned
                    left_ref[wide] = turned
                    back_left_ref[wide] = value


def times_right(values, table):
    high, low = split(values)
    return jnp.dot(
        jnp.concatenate([high, high, low], axis=1), table, preferred_element_type=jnp.float32
    )


def times_left(table, values):
    high, low = split(values)
    return jnp.dot(
        table, jnp.concatenate([high, high, low], axis=0), preferred_element_type=jnp.float32
    )


def regroup(values, width):
    blocks = values.shape[0] // width
    return jnp.concatenate(
        [
            jnp.concatenate(
                [values[b * width : (b + 1) * width, p * width : (p + 1) * width] for b in range(blocks)],
                axis=1,
            )
            for p in range(2)
        ],
        axis=0,
    )


def ungroup(values, width):
    blocks = values.shape[1] // width
    return jnp.concatenate(
        [
            jnp.concatenate(
                [values[p * width : (p + 1) * width, b * width : (b + 1) * width] for p in range(2)],
                axis=1,
            )
            for b in range(blocks)
        ],
        axis=0,
    )


def make_slots(positions_ref, first_row, field_ref, grad_ref, probe_ref, measured_ref, sums_ref, table_refs):
    width = PATCH
    modes = probe_ref.shape[1]
    tall = width + 8
    right_table, left_table, back_left, back_right = table_refs
    lane = lax.broadcasted_iota(jnp.int32, (tall, width), 1)
    sublane = lax.broadcasted_iota(jnp.int32, (tall // 8, 8, width), 1)

    def place(index):
        row = positions_ref[0, index] - first_row
        col = positions_ref[1, index]
        down = lax.rem(row, 8)
        shift = lax.rem(col, width)
        return (pl.multiple_of(row - down, 8), down, pl.multiple_of(col - shift, width), shift)

    def cut(plane, top, down, base, shift):
        near = field_ref[plane, pl.ds(top, tall), pl.ds(base, width)]
        far = field_ref[plane, pl.ds(top, tall), pl.ds(base + width, width)]
        back_by = lax.rem(width - shift, width)
        turned = jnp.where(
            lane < width - shift,
            pltpu.roll(near, back_by, axis=1),
            pltpu.roll(far, back_by, axis=1),
        )
        turned = pltpu.roll(turned.reshape(tall // 8, 8, width), lax.rem(8 - down, 8), axis=1)
        picked = jnp.where(sublane[1:] < 8 - down, turned[:-1], turned[1:])
        return picked.reshape(width, width)

    def paste(plane, top, down, base, shift, values):
        turned = pltpu.roll(values, shift, axis=1).reshape(width // 8, 8, width)
        turned = pltpu.roll(turned, down, axis=1)
        blank = jnp.zeros((1, 8, width), jnp.float32)
        moved = jnp.where(
            sublane >= down,
            jnp.concatenate([turned, blank], axis=0),
            jnp.concatenate([blank, turned], axis=0),
        ).reshape(tall, width)
        grad_ref[plane, pl.ds(top, tall), pl.ds(base, width)] += jnp.where(
            lane >= shift, moved, 0.0
        )
        grad_ref[plane, pl.ds(top, tall), pl.ds(base + width, width)] += jnp.where(
            lane < shift, moved, 0.0
        )

    def slots(indices):
        places = [place(index) for index in indices]
        patches = [(cut(0, *at), cut(1, *at)) for at in places]
        exits = []
        for patch_real, patch_imag in patches:
            for mode in range(modes):
                mode_real, mode_imag = (probe_ref[0, mode], probe_ref[1, mode])
                exits.append(
                    jnp.concatenate(
                        [
                            mode_real * patch_real - mode_imag * patch_imag,
                            mode_real * patch_imag + mode_imag * patch_real,
                        ],
                        axis=1,
                    )
                )
        rows = times_right(jnp.concatenate(exits, axis=0), right_table[...])
        far = times_left(left_table[...], regroup(rows, width))
        scalings = []
        for order, index in enumerate(indices):
            part = far[:, order * modes * width : (order + 1) * modes * width]
            power = part * part
            power = power[:width] + power[width:]
            intensity = sum(power[:, m * width : (m + 1) * width] for m in range(modes))
            scaling = (
                measured_ref[index] * lax.rsqrt(jnp.maximum(intensity, AMP_FLOOR * AMP_FLOOR)) - 1.0
            )
            scalings += [scaling] * modes
        scaling = jnp.concatenate(scalings, axis=1)
        rows = times_left(back_left[...], far * jnp.concatenate([scaling, scaling], axis=0))
        back = times_right(ungroup(rows, width), back_right[...])
        sums = [[0.0] * modes, [0.0] * modes]
        density = 0.0
        for order, (patch_real, patch_imag) in enumerate(patches):
            object_real, object_imag = (0.0, 0.0)
            for mode in range(modes):
                mode_real, mode_imag = (probe_ref[0, mode], probe_ref[1, mode])
                start = (order * modes + mode) * width
                back_real = back[start : start + width, :width]
                back_imag = back[start : start + width, width:]
                object_real += mode_real * back_real + mode_imag * back_imag
                object_imag += mode_real * back_imag - mode_imag * back_real
                sums[0][mode] += patch_real * back_real + patch_imag * back_imag
                sums[1][mode] += patch_real * back_imag - patch_imag * back_real
            density += patch_real * patch_real + patch_imag * patch_imag
            paste(0, *places[order], object_real)
            paste(1, *places[order], object_imag)
        for part in range(2):
            for mode in range(modes):
                sums_ref[part, mode] += sums[part][mode]
        sums_ref[2, 0] += density

    return slots


def run_slots(positions_ref, counts_ref, order_ref, slots, wanted):

    def note(index, found):
        order_ref[found] = index
        return found + wanted(positions_ref[0, index], positions_ref[1, index]).astype(jnp.int32)

    found = lax.fori_loop(0, counts_ref[0], note, jnp.int32(0))

    def run(start, stop, size):

        def step(turn, carry):
            slots([order_ref[start + turn * size + i] for i in range(size)])
            return carry

        turns = lax.div(stop - start, size)
        lax.fori_loop(0, turns, step, 0)
        return start + turns * size

    reached = run(0, found, 4)
    reached = run(reached, found, 2)
    run(reached, found, 1)


def upper_kernel(
    positions_ref, counts_ref, own_ref, right_ref, probe_ref, measured_ref, parts_ref,
    grad_ref, sums_ref, field_ref, order_ref, *table_refs,
):
    tile_height, tile_width = own_ref.shape[1:]
    fill_tables(parts_ref, table_refs)
    field_ref[:, :tile_height, :tile_width] = own_ref[...]
    field_ref[:, :tile_height, tile_width:] = right_ref[...]
    grad_ref[...] = jnp.zeros_like(grad_ref)
    sums_ref[...] = jnp.zeros_like(sums_ref)
    slots = make_slots(positions_ref, 0, field_ref, grad_ref, probe_ref, measured_ref, sums_ref, table_refs)
    run_slots(positions_ref, counts_ref, order_ref, slots, lambda row, col: row <= tile_height - PATCH)


def fill_lower(last_ref, own_ref, direct_ref, side_ref, far_ref, right_ref, field_ref):
    tile_height, tile_width = own_ref.shape[1:]
    first = tile_height - PATCH
    field_ref[:, :PATCH, :tile_width] = own_ref[:, first:]
    field_ref[:, PATCH : PATCH + DIRECT, :tile_width] = direct_ref[...]
    field_ref[:, :PATCH, tile_width:] = right_ref[:, first:]

    @pl.when(last_ref[0] == 1)
    def _():
        field_ref[:, PATCH + DIRECT :, :tile_width] = far_ref[...]

    @pl.when(last_ref[0] == 0)
    def _():
        field_ref[:, PATCH + DIRECT :, :tile_width] = side_ref[...]


def lower_kernel(
    positions_ref, counts_ref, last_ref, own_ref, direct_ref, side_ref, far_ref, right_ref,
    probe_ref, measured_ref, parts_ref, upper_ref, upper_sums_ref, grad_ref, sums_ref,
    field_ref, order_ref, *table_refs,
):
    tile_height, tile_width = own_ref.shape[1:]
    first = tile_height - PATCH
    fill_tables(parts_ref, table_refs)
    fill_lower(last_ref, own_ref, direct_ref, side_ref, far_ref, right_ref, field_ref)
    field_ref[:, PATCH:, tile_width:] = jnp.zeros_like(field_ref[:, PATCH:, tile_width:])
    grad_ref[:, :PATCH] = upper_ref[:, first:tile_height]
    grad_ref[:, PATCH:] = jnp.zeros_like(grad_ref[:, PATCH:])
    sums_ref[...] = upper_sums_ref[...]
    slots = make_slots(positions_ref, first, field_ref, grad_ref, probe_ref, measured_ref, sums_ref, table_refs)
    run_slots(
        positions_ref, counts_ref, order_ref, slots,
        lambda row, col: (row > first) & (col <= tile_width - PATCH),
    )


def corner_slots_kernel(
    positions_ref, counts_ref, last_ref, own_ref, direct_ref, side_ref, far_ref, right_ref, corner_ref,
    probe_ref, measured_ref, parts_ref, upper_ref, lower_ref, lower_sums_ref,
    grad_own_ref, grad_right_ref, grad_corner_ref, grad_lower_ref, packed_ref,
    field_ref, grad_ref, sums_ref, order_ref, *table_refs,
):
    tile_height, tile_width = own_ref.shape[1:]
    first = tile_height - PATCH
    fill_tables(parts_ref, table_refs)
    fill_lower(last_ref, own_ref, direct_ref, side_ref, far_ref, right_ref, field_ref)
    field_ref[:, PATCH:, tile_width:] = corner_ref[...]
    grad_ref[...] = lower_ref[...]
    sums_ref[...] = lower_sums_ref[...]
    slots = make_slots(positions_ref, first, field_ref, grad_ref, probe_ref, measured_ref, sums_ref, table_refs)
    run_slots(
        positions_ref, counts_ref, order_ref, slots,
        lambda row, col: (row > first) & (col > tile_width - PATCH),
    )
    for block in range(packed_ref.shape[0]):
        part, mode, start = (block // 16, block // 8 % 2, block % 8 * 16)
        for piece in range(4):
            row = start + piece * 4
            packed_ref[block, piece] = sums_ref[part, mode, row : row + 4]
        packed_ref[block, 4] = sums_ref[2, 0, block * 4 : block * 4 + 4]
    grad_right_ref[:, :first] = upper_ref[:, :first, tile_width:]
    grad_right_ref[:, first:] = grad_ref[:, :PATCH, tile_width:]
    grad_corner_ref[...] = grad_ref[:, PATCH:, tile_width:]
    grad_own_ref[...] = grad_ref[:, :PATCH, :tile_width]
    grad_lower_ref[...] = grad_ref[:, PATCH:, :tile_width]


def float_array(*shape):
    return jax.ShapeDtypeStruct(shape, jnp.float32)


def table_scratch():
    tall = pltpu.VMEM((6 * PATCH, 2 * PATCH), jnp.bfloat16)
    wide = pltpu.VMEM((2 * PATCH, 6 * PATCH), jnp.bfloat16)
    return [tall, wide, wide, tall]


VMEM_SPEC = pl.BlockSpec(memory_space=pltpu.VMEM)
SMEM_SPEC = pl.BlockSpec(memory_space=pltpu.SMEM)
PARAMS = pltpu.CompilerParams(vmem_limit_bytes=24 * 1024 * 1024)


def upper_slots(positions, counts, own, right, probe, measured, parts):
    tile_height, tile_width = own.shape[1:]
    wide = tile_width + PATCH
    return pl.pallas_call(
        upper_kernel,
        in_specs=[SMEM_SPEC] * 2 + [VMEM_SPEC] * 5,
        out_specs=[VMEM_SPEC] * 2,
        out_shape=[float_array(2, tile_height + 8, wide), float_array(3, 2, PATCH, PATCH)],
        scratch_shapes=[
            pltpu.VMEM((2, tile_height + 8, wide), jnp.float32),
            pltpu.SMEM((positions.shape[1],), jnp.int32),
        ]
        + table_scratch(),
        compiler_params=PARAMS,
        cost_estimate=pl.CostEstimate(flops=3_000_000_000, transcendentals=0, bytes_accessed=3_000_000),
        name="upper_slots",
    )(positions, counts, own, right, probe, measured, parts)


def lower_slots(
    positions, counts, last, own, direct, side, far, right, probe, measured, parts, upper, sums
):
    wide = own.shape[2] + PATCH
    return pl.pallas_call(
        lower_kernel,
        in_specs=[SMEM_SPEC] * 3 + [VMEM_SPEC] * 10,
        out_specs=[VMEM_SPEC] * 2,
        out_shape=[float_array(2, 2 * PATCH, wide), float_array(3, 2, PATCH, PATCH)],
        scratch_shapes=[
            pltpu.VMEM((2, 2 * PATCH, wide), jnp.float32),
            pltpu.SMEM((positions.shape[1],), jnp.int32),
        ]
        + table_scratch(),
        compiler_params=PARAMS,
        cost_estimate=pl.CostEstimate(flops=3_000_000_000, transcendentals=0, bytes_accessed=3_000_000),
        name="lower_slots",
    )(positions, counts, last, own, direct, side, far, right, probe, measured, parts, upper, sums)


def corner_slots(
    positions, counts, last, own, direct, side, far, right, corner, probe, measured, parts, upper, lower, sums
):
    tile_height, tile_width = own.shape[1:]
    wide = tile_width + PATCH
    return pl.pallas_call(
        corner_slots_kernel,
        in_specs=[SMEM_SPEC] * 3 + [VMEM_SPEC] * 12,
        out_specs=[VMEM_SPEC] * 5,
        out_shape=[
            float_array(2, PATCH, tile_width),
            float_array(2, tile_height, PATCH),
            float_array(2, PATCH, PATCH),
            float_array(2, PATCH, tile_width),
            float_array(32, 5, 4, PATCH),
        ],
        scratch_shapes=[
            pltpu.VMEM((2, 2 * PATCH, wide), jnp.float32),
            pltpu.VMEM((2, 2 * PATCH, wide), jnp.float32),
            pltpu.VMEM((3, 2, PATCH, PATCH), jnp.float32),
            pltpu.SMEM((positions.shape[1],), jnp.int32),
        ]
        + table_scratch(),
        compiler_params=PARAMS,
        cost_estimate=pl.CostEstimate(flops=3_000_000_000, transcendentals=0, bytes_accessed=5_000_000),
        name="corner_slots",
    )(positions, counts, last, own, direct, side, far, right, corner, probe, measured, parts, upper, lower, sums)


def object_kernel(
    first_ref, own_ref, upper_ref, lower_ref, spilled_ref, rim_ref, side_ref, far_ref, probe_ref, out_ref
):
    tile_height, tile_width = own_ref.shape[1:]
    first = tile_height - PATCH
    power = probe_ref[...] * probe_ref[...]
    power = power[0, 0] + power[0, 1] + power[1, 0] + power[1, 1]
    weight = 1.0 / (jnp.max(power, axis=(0, 1), keepdims=True) + 1e-06)
    from_far = first_ref[0] == 1
    for plane in range(2):
        for start in range(0, tile_height, PATCH):
            for side in range(0, tile_width, PATCH):
                rows, cols = (slice(start, start + PATCH), slice(side, side + PATCH))
                if start < first:
                    total = upper_ref[plane, rows, cols]
                else:
                    total = lower_ref[plane, :, cols]
                if side == 0:
                    total += spilled_ref[plane, rows, :]
                if start == 0:
                    rest = jnp.where(from_far, far_ref[plane, :, cols], side_ref[plane, :, cols])
                    total += jnp.concatenate([rim_ref[plane, :, cols], rest], axis=0)
                out_ref[plane, rows, cols] = own_ref[plane, rows, cols] + total * weight


def object_update(first, own, upper, lower, spilled, rim, side, far, probe):
    return pl.pallas_call(
        object_kernel,
        in_specs=[SMEM_SPEC] + [VMEM_SPEC] * 8,
        out_specs=VMEM_SPEC,
        out_shape=float_array(*own.shape),
        compiler_params=PARAMS,
        cost_estimate=pl.CostEstimate(flops=OBJECT_COST, transcendentals=0, bytes_accessed=4_000_000),
        name="object_update",
    )(first, own, upper, lower, spilled, rim, side, far, probe)


def probe_kernel(blocks_ref, out_ref, density_ref, weight_ref):
    for block in range(blocks_ref.shape[0]):
        density_ref[block * 4 : block * 4 + 4] = blocks_ref[block, 4]
    weight_ref[...] = lax.rsqrt(density_ref[...] + 1.0)
    for block in range(blocks_ref.shape[0]):
        part, mode, start = (block // 16, block // 8 % 2, block % 8 * 16)
        for piece in range(4):
            row = start + piece * 4
            out_ref[part, mode, row : row + 4] = blocks_ref[block, piece] * weight_ref[row : row + 4]


def probe_update(blocks, shape):
    return pl.pallas_call(
        probe_kernel,
        in_specs=[VMEM_SPEC],
        out_specs=VMEM_SPEC,
        out_shape=float_array(*shape),
        scratch_shapes=[pltpu.VMEM((PATCH, PATCH), jnp.float32)] * 2,
        compiler_params=PARAMS,
        name="probe_update",
    )(blocks)


def halo_kernel(own_ref, side_ref, direct_ref, left_ref, sems):
    pieces = (
        (own_ref.at[:, pl.ds(DIRECT, PATCH - DIRECT), :], side_ref),
        (own_ref.at[:, pl.ds(0, DIRECT), :], direct_ref),
        (own_ref.at[:, :, pl.ds(0, PATCH)], left_ref),
    )
    copies = [
        pltpu.make_async_copy(source, target, sems.at[order])
        for order, (source, target) in enumerate(pieces)
    ]
    for copy in copies:
        copy.start()
    for copy in copies:
        copy.wait()


def halo_pieces(own):
    planes, tile_height, tile_width = own.shape
    return pl.pallas_call(
        halo_kernel,
        in_specs=[pl.BlockSpec(memory_space=pltpu.MemorySpace.HBM)],
        out_specs=[VMEM_SPEC] * 3,
        out_shape=[
            float_array(planes, PATCH - DIRECT, tile_width),
            float_array(planes, DIRECT, tile_width),
            float_array(planes, tile_height, PATCH),
        ],
        scratch_shapes=[pltpu.SemaphoreType.DMA((3,))],
        compiler_params=PARAMS,
        name="halo_pieces",
    )(own)


def corner_kernel(last_ref, direct_ref, side_ref, far_ref, corner_ref):
    from_far = last_ref[0] == 1
    for plane in range(2):
        corner_ref[plane, :DIRECT] = direct_ref[plane, :, :PATCH]
        corner_ref[plane, DIRECT:] = jnp.where(
            from_far, far_ref[plane, :, :PATCH], side_ref[plane, :, :PATCH]
        )


def corner_piece(last, direct, side, far):
    return pl.pallas_call(
        corner_kernel,
        in_specs=[SMEM_SPEC] + [VMEM_SPEC] * 3,
        out_specs=VMEM_SPEC,
        out_shape=float_array(2, PATCH, PATCH),
        compiler_params=PARAMS,
        name="corner_piece",
    )(last, direct, side, far)


def sum_kernel(terms_ref, out_ref):
    total = jnp.sum(terms_ref[...], axis=0)
    out_ref[...] = jnp.broadcast_to(total[None], out_ref.shape)


def sum_for(terms, copies):
    return pl.pallas_call(
        sum_kernel,
        in_specs=[VMEM_SPEC],
        out_specs=VMEM_SPEC,
        out_shape=float_array(copies, *terms.shape[1:]),
        compiler_params=PARAMS,
        name="sum_for",
    )(terms)


def rim_kernel(lower_ref, spilled_ref, direct_ref, side_ref):
    for plane in range(2):
        near = lower_ref[plane, :, :PATCH] + spilled_ref[plane]
        direct_ref[plane, :, :PATCH] = near[:RIM_DIRECT]
        side_ref[plane, :, :PATCH] = near[RIM_DIRECT:]
        direct_ref[plane, :, PATCH:] = lower_ref[plane, :RIM_DIRECT, PATCH:]
        side_ref[plane, :, PATCH:] = lower_ref[plane, RIM_DIRECT:, PATCH:]


def rim_pieces(lower, spilled):
    planes, height, width = lower.shape
    return pl.pallas_call(
        rim_kernel,
        in_specs=[VMEM_SPEC] * 2,
        out_specs=[VMEM_SPEC] * 2,
        out_shape=[
            float_array(planes, RIM_DIRECT, width),
            float_array(planes, height - RIM_DIRECT, width),
        ],
        compiler_params=PARAMS,
        cost_estimate=pl.CostEstimate(flops=RIM_COST, transcendentals=0, bytes_accessed=1_000_000),
        name="rim_pieces",
    )(lower, spilled)


def moved(array, where):
    pairs = []
    for device in range(lax.axis_size("row") * lax.axis_size("col")):
        row, col = divmod(device, lax.axis_size("col"))
        target = where(row)
        if target is not None:
            pairs.append((device, target * lax.axis_size("col") + col))
    return lax.ppermute(array, ("row", "col"), pairs)


def around(row, by):
    return row // RUN * RUN + (row + by) % RUN


def far_up(row):
    return row - RUN if row % RUN == RUN - 1 and row >= RUN else None


def far_down(row):
    return row + RUN if row % RUN == 0 and row + RUN < lax.axis_size("row") else None


def per_device(object_field, probe_modes, measured, positions, counts):
    planes, lines = device_groups(lax.axis_size("row") * lax.axis_size("col"))
    places, live, amplitudes = (positions[0, 0], counts[0], measured[0, 0])
    parts = jnp.asarray(fourier_parts(PATCH))
    place = lax.axis_index("row") % RUN
    side_rows, direct_rows, left_columns = halo_pieces(
        pltpu.with_memory_space_constraint(object_field, pltpu.MemorySpace.HBM)
    )
    side = moved(side_rows, lambda row: around(row, -1))
    direct = shifted(direct_rows, "row", -1)
    far = moved(side, far_up)
    right = shifted(left_columns, "col", -1)
    upper, upper_sums = upper_slots(
        places, live, object_field, right, probe_modes, amplitudes, parts
    )
    direct, side, far, upper_sums = lax.optimization_barrier((direct, side, far, upper_sums))
    last = (place == RUN - 1).astype(jnp.int32)[None]
    corner = shifted(corner_piece(last, direct, side, far), "col", -1)
    edge, edge_sums = lower_slots(
        places, live, last, object_field, direct, side, far, right,
        probe_modes, amplitudes, parts, upper, upper_sums,
    )
    lower, grad_right, grad_corner, grad_lower, packed = corner_slots(
        places, live, last, object_field, direct, side, far, right, corner,
        probe_modes, amplitudes, parts, upper, edge, edge_sums,
    )
    spilled = shifted(grad_right, "col", 1)
    spilled_corner = shifted(grad_corner, "col", 1)
    rim_direct, rim_side = rim_pieces(grad_lower, spilled_corner)
    rim_direct = shifted(rim_direct, "row", 1)
    rim_side = moved(rim_side, lambda row: around(row, 1))
    rim_far = moved(rim_side, far_down)
    terms = exchange(packed, planes)
    terms = exchange(sum_for(terms, len(lines[0])), lines)
    blocks = exchange(sum_for(terms, len(planes[0])), planes)
    object_new = object_update(
        (place == 0).astype(jnp.int32)[None],
        object_field, upper, lower, spilled, rim_direct, rim_side, rim_far, probe_modes,
    )
    probe_step = probe_update(blocks, probe_modes.shape)
    return (object_new, probe_step)


def solution(mesh):
    in_specs = (
        P(None, "row", "col"),
        P(),
        P("row", "col", None, None, None),
        P("row", "col", None, None),
        P("row", "col"),
    )
    out_specs = (P(None, "row", "col"), P())
    return jax.shard_map(
        per_device, mesh=mesh, in_specs=in_specs, out_specs=out_specs, check_vma=False
    )
```

```python
import math

import jax
import jax.numpy as jnp
import numpy as np
from jax import lax
from jax.experimental import pallas as pl
from jax.experimental.pallas import tpu as pltpu
from jax.sharding import PartitionSpec as P

AMP_FLOOR = 0.25
PATCH = 128
RUN = 4
DIRECT = 80
RIM_DIRECT = 64
RIM_COST = 10_000_000_000
OBJECT_COST = 30_000_000_000


def shifted(array, axis, by):
    length = lax.axis_size(axis)
    pairs = [(i, i + by) for i in range(length) if 0 <= i + by < length]
    return lax.ppermute(array, axis, pairs)


def coordinates(device):
    row, col = divmod(device, 32)
    z_hi, x = divmod(row, 4)
    z_lo, rest = divmod(col, 8)
    y, core = divmod(rest, 2)
    return (z_hi * 4 + z_lo, x, y, core)


def device_groups(devices):
    planes, lines = {}, {}
    for device in range(devices):
        z, x, y, core = coordinates(device)
        planes.setdefault(z, []).append(device)
        lines.setdefault((x, y, core), []).append(device)
    return (list(planes.values()), list(lines.values()))


def exchange(blocks, groups):
    return lax.all_to_all(blocks, ("row", "col"), 0, 0, axis_index_groups=groups)


def split(values):
    high = values.astype(jnp.bfloat16)
    low = (values - high.astype(jnp.float32)).astype(jnp.bfloat16)
    return (high, low)


def fourier_parts(width):
    index = np.arange(width)
    angle = (index[:, None] * index[None, :] % width) * (2.0 * math.pi / width)
    parts = []
    for wave in (np.cos(angle), np.sin(angle)):
        values = (wave / math.sqrt(width)).astype(np.float32)
        high = values.astype(jnp.bfloat16)
        parts += [high, (values - high.astype(np.float32)).astype(jnp.bfloat16)]
    return np.stack(parts)


def fill_tables(parts_ref, table_refs):
    width = parts_ref.shape[-1]
    right_ref, left_ref, back_left_ref, back_right_ref = table_refs
    for level, places in ((0, (0, 2)), (1, (1,))):
        cosine = parts_ref[level]
        sine = parts_ref[2 + level]
        for place in places:
            start = place * 2 * width
            for i in range(2):
                for j in range(2):
                    value = cosine if i == j else (-sine if i == 0 else sine)
                    turned = cosine if i == j else (sine if i == 0 else -sine)
                    tall = (slice(start + i * width, start + (i + 1) * width), slice(j * width, (j + 1) * width))
                    wide = (slice(i * width, (i + 1) * width), slice(start + j * width, start + (j + 1) * width))
                    right_ref[tall] = value
                    back_right_ref[tall] = turned
                    left_ref[wide] = turned
                    back_left_ref[wide] = value


def times_right(values, table):
    high, low = split(values)
    return jnp.dot(
        jnp.concatenate([high, high, low], axis=1), table, preferred_element_type=jnp.float32
    )


def times_left(table, values):
    high, low = split(values)
    return jnp.dot(
        table, jnp.concatenate([high, high, low], axis=0), preferred_element_type=jnp.float32
    )


def regroup(values, width):
    blocks = values.shape[0] // width
    return jnp.concatenate(
        [
            jnp.concatenate(
                [values[b * width : (b + 1) * width, p * width : (p + 1) * width] for b in range(blocks)],
                axis=1,
            )
            for p in range(2)
        ],
        axis=0,
    )


def ungroup(values, width):
    blocks = values.shape[1] // width
    return jnp.concatenate(
        [
            jnp.concatenate(
                [values[p * width : (p + 1) * width, b * width : (b + 1) * width] for p in range(2)],
                axis=1,
            )
            for b in range(blocks)
        ],
        axis=0,
    )


def make_slots(positions_ref, first_row, field_ref, grad_ref, probe_ref, measured_ref, sums_ref, table_refs):
    width = PATCH
    modes = probe_ref.shape[1]
    tall = width + 8
    right_table, left_table, back_left, back_right = table_refs
    lane = lax.broadcasted_iota(jnp.int32, (tall, width), 1)
    sublane = lax.broadcasted_iota(jnp.int32, (tall // 8, 8, width), 1)

    def place(index):
        row = positions_ref[0, index] - first_row
        col = positions_ref[1, index]
        down = lax.rem(row, 8)
        shift = lax.rem(col, width)
        return (pl.multiple_of(row - down, 8), down, pl.multiple_of(col - shift, width), shift)

    def cut(plane, top, down, base, shift):
        near = field_ref[plane, pl.ds(top, tall), pl.ds(base, width)]
        far = field_ref[plane, pl.ds(top, tall), pl.ds(base + width, width)]
        back_by = lax.rem(width - shift, width)
        turned = jnp.where(
            lane < width - shift,
            pltpu.roll(near, back_by, axis=1),
            pltpu.roll(far, back_by, axis=1),
        )
        turned = pltpu.roll(turned.reshape(tall // 8, 8, width), lax.rem(8 - down, 8), axis=1)
        picked = jnp.where(sublane[1:] < 8 - down, turned[:-1], turned[1:])
        return picked.reshape(width, width)

    def paste(plane, top, down, base, shift, values):
        turned = pltpu.roll(values, shift, axis=1).reshape(width // 8, 8, width)
        turned = pltpu.roll(turned, down, axis=1)
        blank = jnp.zeros((1, 8, width), jnp.float32)
        moved = jnp.where(
            sublane >= down,
            jnp.concatenate([turned, blank], axis=0),
            jnp.concatenate([blank, turned], axis=0),
        ).reshape(tall, width)
        grad_ref[plane, pl.ds(top, tall), pl.ds(base, width)] += jnp.where(
            lane >= shift, moved, 0.0
        )
        grad_ref[plane, pl.ds(top, tall), pl.ds(base + width, width)] += jnp.where(
            lane < shift, moved, 0.0
        )

    def slots(indices):
        places = [place(index) for index in indices]
        patches = [(cut(0, *at), cut(1, *at)) for at in places]
        exits = []
        for patch_real, patch_imag in patches:
            for mode in range(modes):
                mode_real, mode_imag = (probe_ref[0, mode], probe_ref[1, mode])
                exits.append(
                    jnp.concatenate(
                        [
                            mode_real * patch_real - mode_imag * patch_imag,
                            mode_real * patch_imag + mode_imag * patch_real,
                        ],
                        axis=1,
                    )
                )
        rows = times_right(jnp.concatenate(exits, axis=0), right_table[...])
        far = times_left(left_table[...], regroup(rows, width))
        scalings = []
        for order, index in enumerate(indices):
            part = far[:, order * modes * width : (order + 1) * modes * width]
            power = part * part
            power = power[:width] + power[width:]
            intensity = sum(power[:, m * width : (m + 1) * width] for m in range(modes))
            scaling = (
                measured_ref[index] * lax.rsqrt(jnp.maximum(intensity, AMP_FLOOR * AMP_FLOOR)) - 1.0
            )
            scalings += [scaling] * modes
        scaling = jnp.concatenate(scalings, axis=1)
        rows = times_left(back_left[...], far * jnp.concatenate([scaling, scaling], axis=0))
        back = times_right(ungroup(rows, width), back_right[...])
        sums = [[0.0] * modes, [0.0] * modes]
        density = 0.0
        for order, (patch_real, patch_imag) in enumerate(patches):
            object_real, object_imag = (0.0, 0.0)
            for mode in range(modes):
                mode_real, mode_imag = (probe_ref[0, mode], probe_ref[1, mode])
                start = (order * modes + mode) * width
                back_real = back[start : start + width, :width]
                back_imag = back[start : start + width, width:]
                object_real += mode_real * back_real + mode_imag * back_imag
                object_imag += mode_real * back_imag - mode_imag * back_real
                sums[0][mode] += patch_real * back_real + patch_imag * back_imag
                sums[1][mode] += patch_real * back_imag - patch_imag * back_real
            density += patch_real * patch_real + patch_imag * patch_imag
            paste(0, *places[order], object_real)
            paste(1, *places[order], object_imag)
        for part in range(2):
            for mode in range(modes):
                sums_ref[part, mode] += sums[part][mode]
        sums_ref[2, 0] += density

    return slots


def run_slots(positions_ref, counts_ref, order_ref, slots, wanted):

    def note(index, found):
        order_ref[found] = index
        return found + wanted(positions_ref[0, index]).astype(jnp.int32)

    found = lax.fori_loop(0, counts_ref[0], note, jnp.int32(0))

    def run(start, stop, size):

        def step(turn, carry):
            slots([order_ref[start + turn * size + i] for i in range(size)])
            return carry

        turns = lax.div(stop - start, size)
        lax.fori_loop(0, turns, step, 0)
        return start + turns * size

    reached = run(0, found, 4)
    reached = run(reached, found, 2)
    run(reached, found, 1)


def upper_kernel(
    positions_ref, counts_ref, own_ref, right_ref, probe_ref, measured_ref, parts_ref,
    grad_ref, sums_ref, field_ref, order_ref, *table_refs,
):
    tile_height, tile_width = own_ref.shape[1:]
    fill_tables(parts_ref, table_refs)
    field_ref[:, :tile_height, :tile_width] = own_ref[...]
    field_ref[:, :tile_height, tile_width:] = right_ref[...]
    grad_ref[...] = jnp.zeros_like(grad_ref)
    sums_ref[...] = jnp.zeros_like(sums_ref)
    slots = make_slots(positions_ref, 0, field_ref, grad_ref, probe_ref, measured_ref, sums_ref, table_refs)
    run_slots(positions_ref, counts_ref, order_ref, slots, lambda row: row <= tile_height - PATCH)


def lower_kernel(
    positions_ref, counts_ref, last_ref, own_ref, direct_ref, side_ref, far_ref, right_ref, corner_ref,
    probe_ref, measured_ref, parts_ref, upper_ref, upper_sums_ref,
    grad_own_ref, grad_right_ref, grad_corner_ref, grad_lower_ref, packed_ref,
    field_ref, grad_ref, sums_ref, order_ref, *table_refs,
):
    tile_height, tile_width = own_ref.shape[1:]
    first = tile_height - PATCH
    fill_tables(parts_ref, table_refs)
    field_ref[:, :PATCH, :tile_width] = own_ref[:, first:]
    field_ref[:, PATCH : PATCH + DIRECT, :tile_width] = direct_ref[...]

    @pl.when(last_ref[0] == 1)
    def _():
        field_ref[:, PATCH + DIRECT :, :tile_width] = far_ref[...]

    @pl.when(last_ref[0] == 0)
    def _():
        field_ref[:, PATCH + DIRECT :, :tile_width] = side_ref[...]

    field_ref[:, :PATCH, tile_width:] = right_ref[:, first:]
    field_ref[:, PATCH:, tile_width:] = corner_ref[...]
    grad_ref[:, :PATCH] = upper_ref[:, first:tile_height]
    grad_ref[:, PATCH:] = jnp.zeros_like(grad_ref[:, PATCH:])
    sums_ref[...] = upper_sums_ref[...]
    slots = make_slots(positions_ref, first, field_ref, grad_ref, probe_ref, measured_ref, sums_ref, table_refs)
    run_slots(positions_ref, counts_ref, order_ref, slots, lambda row: row > first)
    for block in range(packed_ref.shape[0]):
        part, mode, start = (block // 16, block // 8 % 2, block % 8 * 16)
        for piece in range(4):
            row = start + piece * 4
            packed_ref[block, piece] = sums_ref[part, mode, row : row + 4]
        packed_ref[block, 4] = sums_ref[2, 0, block * 4 : block * 4 + 4]
    grad_right_ref[:, :first] = upper_ref[:, :first, tile_width:]
    grad_right_ref[:, first:] = grad_ref[:, :PATCH, tile_width:]
    grad_corner_ref[...] = grad_ref[:, PATCH:, tile_width:]
    grad_own_ref[...] = grad_ref[:, :PATCH, :tile_width]
    grad_lower_ref[...] = grad_ref[:, PATCH:, :tile_width]


def float_array(*shape):
    return jax.ShapeDtypeStruct(shape, jnp.float32)


def table_scratch():
    tall = pltpu.VMEM((6 * PATCH, 2 * PATCH), jnp.bfloat16)
    wide = pltpu.VMEM((2 * PATCH, 6 * PATCH), jnp.bfloat16)
    return [tall, wide, wide, tall]


VMEM_SPEC = pl.BlockSpec(memory_space=pltpu.VMEM)
SMEM_SPEC = pl.BlockSpec(memory_space=pltpu.SMEM)
PARAMS = pltpu.CompilerParams(vmem_limit_bytes=24 * 1024 * 1024)


def upper_slots(positions, counts, own, right, probe, measured, parts):
    tile_height, tile_width = own.shape[1:]
    wide = tile_width + PATCH
    return pl.pallas_call(
        upper_kernel,
        in_specs=[SMEM_SPEC] * 2 + [VMEM_SPEC] * 5,
        out_specs=[VMEM_SPEC] * 2,
        out_shape=[float_array(2, tile_height + 8, wide), float_array(3, 2, PATCH, PATCH)],
        scratch_shapes=[
            pltpu.VMEM((2, tile_height + 8, wide), jnp.float32),
            pltpu.SMEM((positions.shape[1],), jnp.int32),
        ]
        + table_scratch(),
        compiler_params=PARAMS,
        cost_estimate=pl.CostEstimate(flops=3_000_000_000, transcendentals=0, bytes_accessed=3_000_000),
        name="upper_slots",
    )(positions, counts, own, right, probe, measured, parts)


def lower_slots(
    positions, counts, last, own, direct, side, far, right, corner, probe, measured, parts, upper, sums
):
    tile_height, tile_width = own.shape[1:]
    wide = tile_width + PATCH
    return pl.pallas_call(
        lower_kernel,
        in_specs=[SMEM_SPEC] * 3 + [VMEM_SPEC] * 11,
        out_specs=[VMEM_SPEC] * 5,
        out_shape=[
            float_array(2, PATCH, tile_width),
            float_array(2, tile_height, PATCH),
            float_array(2, PATCH, PATCH),
            float_array(2, PATCH, tile_width),
            float_array(32, 5, 4, PATCH),
        ],
        scratch_shapes=[
            pltpu.VMEM((2, 2 * PATCH, wide), jnp.float32),
            pltpu.VMEM((2, 2 * PATCH, wide), jnp.float32),
            pltpu.VMEM((3, 2, PATCH, PATCH), jnp.float32),
            pltpu.SMEM((positions.shape[1],), jnp.int32),
        ]
        + table_scratch(),
        compiler_params=PARAMS,
        cost_estimate=pl.CostEstimate(flops=3_000_000_000, transcendentals=0, bytes_accessed=5_000_000),
        name="lower_slots",
    )(positions, counts, last, own, direct, side, far, right, corner, probe, measured, parts, upper, sums)


def object_kernel(
    first_ref, own_ref, upper_ref, lower_ref, spilled_ref, rim_ref, side_ref, far_ref, probe_ref, out_ref
):
    tile_height, tile_width = own_ref.shape[1:]
    first = tile_height - PATCH
    power = probe_ref[...] * probe_ref[...]
    power = power[0, 0] + power[0, 1] + power[1, 0] + power[1, 1]
    weight = 1.0 / (jnp.max(power, axis=(0, 1), keepdims=True) + 1e-06)
    from_far = first_ref[0] == 1
    for plane in range(2):
        for start in range(0, tile_height, PATCH):
            for side in range(0, tile_width, PATCH):
                rows, cols = (slice(start, start + PATCH), slice(side, side + PATCH))
                if start < first:
                    total = upper_ref[plane, rows, cols]
                else:
                    total = lower_ref[plane, :, cols]
                if side == 0:
                    total += spilled_ref[plane, rows, :]
                if start == 0:
                    rest = jnp.where(from_far, far_ref[plane, :, cols], side_ref[plane, :, cols])
                    total += jnp.concatenate([rim_ref[plane, :, cols], rest], axis=0)
                out_ref[plane, rows, cols] = own_ref[plane, rows, cols] + total * weight


def object_update(first, own, upper, lower, spilled, rim, side, far, probe):
    return pl.pallas_call(
        object_kernel,
        in_specs=[SMEM_SPEC] + [VMEM_SPEC] * 8,
        out_specs=VMEM_SPEC,
        out_shape=float_array(*own.shape),
        compiler_params=PARAMS,
        cost_estimate=pl.CostEstimate(flops=OBJECT_COST, transcendentals=0, bytes_accessed=4_000_000),
        name="object_update",
    )(first, own, upper, lower, spilled, rim, side, far, probe)


def probe_kernel(blocks_ref, out_ref, density_ref, weight_ref):
    for block in range(blocks_ref.shape[0]):
        density_ref[block * 4 : block * 4 + 4] = blocks_ref[block, 4]
    weight_ref[...] = lax.rsqrt(density_ref[...] + 1.0)
    for block in range(blocks_ref.shape[0]):
        part, mode, start = (block // 16, block // 8 % 2, block % 8 * 16)
        for piece in range(4):
            row = start + piece * 4
            out_ref[part, mode, row : row + 4] = blocks_ref[block, piece] * weight_ref[row : row + 4]


def probe_update(blocks, shape):
    return pl.pallas_call(
        probe_kernel,
        in_specs=[VMEM_SPEC],
        out_specs=VMEM_SPEC,
        out_shape=float_array(*shape),
        scratch_shapes=[pltpu.VMEM((PATCH, PATCH), jnp.float32)] * 2,
        compiler_params=PARAMS,
        name="probe_update",
    )(blocks)


def halo_kernel(own_ref, side_ref, direct_ref, left_ref, sems):
    pieces = (
        (own_ref.at[:, pl.ds(DIRECT, PATCH - DIRECT), :], side_ref),
        (own_ref.at[:, pl.ds(0, DIRECT), :], direct_ref),
        (own_ref.at[:, :, pl.ds(0, PATCH)], left_ref),
    )
    copies = [
        pltpu.make_async_copy(source, target, sems.at[order])
        for order, (source, target) in enumerate(pieces)
    ]
    for copy in copies:
        copy.start()
    for copy in copies:
        copy.wait()


def halo_pieces(own):
    planes, tile_height, tile_width = own.shape
    return pl.pallas_call(
        halo_kernel,
        in_specs=[pl.BlockSpec(memory_space=pltpu.MemorySpace.HBM)],
        out_specs=[VMEM_SPEC] * 3,
        out_shape=[
            float_array(planes, PATCH - DIRECT, tile_width),
            float_array(planes, DIRECT, tile_width),
            float_array(planes, tile_height, PATCH),
        ],
        scratch_shapes=[pltpu.SemaphoreType.DMA((3,))],
        compiler_params=PARAMS,
        name="halo_pieces",
    )(own)


def corner_kernel(last_ref, direct_ref, side_ref, far_ref, corner_ref):
    from_far = last_ref[0] == 1
    for plane in range(2):
        corner_ref[plane, :DIRECT] = direct_ref[plane, :, :PATCH]
        corner_ref[plane, DIRECT:] = jnp.where(
            from_far, far_ref[plane, :, :PATCH], side_ref[plane, :, :PATCH]
        )


def corner_piece(last, direct, side, far):
    return pl.pallas_call(
        corner_kernel,
        in_specs=[SMEM_SPEC] + [VMEM_SPEC] * 3,
        out_specs=VMEM_SPEC,
        out_shape=float_array(2, PATCH, PATCH),
        compiler_params=PARAMS,
        name="corner_piece",
    )(last, direct, side, far)


def sum_kernel(terms_ref, out_ref):
    total = jnp.sum(terms_ref[...], axis=0)
    out_ref[...] = jnp.broadcast_to(total[None], out_ref.shape)


def sum_for(terms, copies):
    return pl.pallas_call(
        sum_kernel,
        in_specs=[VMEM_SPEC],
        out_specs=VMEM_SPEC,
        out_shape=float_array(copies, *terms.shape[1:]),
        compiler_params=PARAMS,
        name="sum_for",
    )(terms)


def rim_kernel(lower_ref, spilled_ref, direct_ref, side_ref):
    for plane in range(2):
        near = lower_ref[plane, :, :PATCH] + spilled_ref[plane]
        direct_ref[plane, :, :PATCH] = near[:RIM_DIRECT]
        side_ref[plane, :, :PATCH] = near[RIM_DIRECT:]
        direct_ref[plane, :, PATCH:] = lower_ref[plane, :RIM_DIRECT, PATCH:]
        side_ref[plane, :, PATCH:] = lower_ref[plane, RIM_DIRECT:, PATCH:]


def rim_pieces(lower, spilled):
    planes, height, width = lower.shape
    return pl.pallas_call(
        rim_kernel,
        in_specs=[VMEM_SPEC] * 2,
        out_specs=[VMEM_SPEC] * 2,
        out_shape=[
            float_array(planes, RIM_DIRECT, width),
            float_array(planes, height - RIM_DIRECT, width),
        ],
        compiler_params=PARAMS,
        cost_estimate=pl.CostEstimate(flops=RIM_COST, transcendentals=0, bytes_accessed=1_000_000),
        name="rim_pieces",
    )(lower, spilled)


def moved(array, where):
    pairs = []
    for device in range(lax.axis_size("row") * lax.axis_size("col")):
        row, col = divmod(device, lax.axis_size("col"))
        target = where(row)
        if target is not None:
            pairs.append((device, target * lax.axis_size("col") + col))
    return lax.ppermute(array, ("row", "col"), pairs)


def around(row, by):
    return row // RUN * RUN + (row + by) % RUN


def far_up(row):
    return row - RUN if row % RUN == RUN - 1 and row >= RUN else None


def far_down(row):
    return row + RUN if row % RUN == 0 and row + RUN < lax.axis_size("row") else None


def per_device(object_field, probe_modes, measured, positions, counts):
    planes, lines = device_groups(lax.axis_size("row") * lax.axis_size("col"))
    places, live, amplitudes = (positions[0, 0], counts[0], measured[0, 0])
    parts = jnp.asarray(fourier_parts(PATCH))
    place = lax.axis_index("row") % RUN
    side_rows, direct_rows, left_columns = halo_pieces(
        pltpu.with_memory_space_constraint(object_field, pltpu.MemorySpace.HBM)
    )
    side = moved(side_rows, lambda row: around(row, -1))
    direct = shifted(direct_rows, "row", -1)
    far = moved(side, far_up)
    right = shifted(left_columns, "col", -1)
    upper, upper_sums = upper_slots(
        places, live, object_field, right, probe_modes, amplitudes, parts
    )
    direct, side, far, upper_sums = lax.optimization_barrier((direct, side, far, upper_sums))
    last = (place == RUN - 1).astype(jnp.int32)[None]
    corner = shifted(corner_piece(last, direct, side, far), "col", -1)
    lower, grad_right, grad_corner, grad_lower, packed = lower_slots(
        places, live, last, object_field, direct, side, far, right, corner,
        probe_modes, amplitudes, parts, upper, upper_sums,
    )
    spilled = shifted(grad_right, "col", 1)
    spilled_corner = shifted(grad_corner, "col", 1)
    rim_direct, rim_side = rim_pieces(grad_lower, spilled_corner)
    rim_direct = shifted(rim_direct, "row", 1)
    rim_side = moved(rim_side, lambda row: around(row, 1))
    rim_far = moved(rim_side, far_down)
    terms = exchange(packed, planes)
    terms = exchange(sum_for(terms, len(lines[0])), lines)
    blocks = exchange(sum_for(terms, len(planes[0])), planes)
    object_new = object_update(
        (place == 0).astype(jnp.int32)[None],
        object_field, upper, lower, spilled, rim_direct, rim_side, rim_far, probe_modes,
    )
    probe_step = probe_update(blocks, probe_modes.shape)
    return (object_new, probe_step)


def solution(mesh):
    in_specs = (
        P(None, "row", "col"),
        P(),
        P("row", "col", None, None, None),
        P("row", "col", None, None),
        P("row", "col"),
    )
    out_specs = (P(None, "row", "col"), P())
    return jax.shard_map(
        per_device, mesh=mesh, in_specs=in_specs, out_specs=out_specs, check_vma=False
    )
```

```python
import math

import jax
import jax.numpy as jnp
import numpy as np
from jax import lax
from jax.experimental import pallas as pl
from jax.experimental.pallas import tpu as pltpu
from jax.sharding import PartitionSpec as P

AMP_FLOOR = 0.25
PATCH = 128
RUN = 4
DIRECT = 80
RIM_DIRECT = 72
RIM_COST = 10_000_000_000
OBJECT_COST = 30_000_000_000


def shifted(array, axis, by):
    length = lax.axis_size(axis)
    pairs = [(i, i + by) for i in range(length) if 0 <= i + by < length]
    return lax.ppermute(array, axis, pairs)


def coordinates(device):
    row, col = divmod(device, 32)
    z_hi, x = divmod(row, 4)
    z_lo, rest = divmod(col, 8)
    y, core = divmod(rest, 2)
    return (z_hi * 4 + z_lo, x, y, core)


def device_groups(devices):
    planes, lines = {}, {}
    for device in range(devices):
        z, x, y, core = coordinates(device)
        planes.setdefault(z, []).append(device)
        lines.setdefault((x, y, core), []).append(device)
    return (list(planes.values()), list(lines.values()))


def exchange(blocks, groups):
    return lax.all_to_all(blocks, ("row", "col"), 0, 0, axis_index_groups=groups)


def split(values):
    high = values.astype(jnp.bfloat16)
    low = (values - high.astype(jnp.float32)).astype(jnp.bfloat16)
    return (high, low)


def fourier_parts(width):
    index = np.arange(width)
    angle = (index[:, None] * index[None, :] % width) * (2.0 * math.pi / width)
    parts = []
    for wave in (np.cos(angle), np.sin(angle)):
        values = (wave / math.sqrt(width)).astype(np.float32)
        high = values.astype(jnp.bfloat16)
        parts += [high, (values - high.astype(np.float32)).astype(jnp.bfloat16)]
    return np.stack(parts)


def fill_tables(parts_ref, table_refs):
    width = parts_ref.shape[-1]
    right_ref, left_ref, back_left_ref, back_right_ref = table_refs
    for level, places in ((0, (0, 2)), (1, (1,))):
        cosine = parts_ref[level]
        sine = parts_ref[2 + level]
        for place in places:
            start = place * 2 * width
            for i in range(2):
                for j in range(2):
                    value = cosine if i == j else (-sine if i == 0 else sine)
                    turned = cosine if i == j else (sine if i == 0 else -sine)
                    tall = (slice(start + i * width, start + (i + 1) * width), slice(j * width, (j + 1) * width))
                    wide = (slice(i * width, (i + 1) * width), slice(start + j * width, start + (j + 1) * width))
                    right_ref[tall] = value
                    back_right_ref[tall] = turned
                    left_ref[wide] = turned
                    back_left_ref[wide] = value


def times_right(values, table):
    high, low = split(values)
    return jnp.dot(
        jnp.concatenate([high, high, low], axis=1), table, preferred_element_type=jnp.float32
    )


def times_left(table, values):
    high, low = split(values)
    return jnp.dot(
        table, jnp.concatenate([high, high, low], axis=0), preferred_element_type=jnp.float32
    )


def regroup(values, width):
    blocks = values.shape[0] // width
    return jnp.concatenate(
        [
            jnp.concatenate(
                [values[b * width : (b + 1) * width, p * width : (p + 1) * width] for b in range(blocks)],
                axis=1,
            )
            for p in range(2)
        ],
        axis=0,
    )


def ungroup(values, width):
    blocks = values.shape[1] // width
    return jnp.concatenate(
        [
            jnp.concatenate(
                [values[p * width : (p + 1) * width, b * width : (b + 1) * width] for p in range(2)],
                axis=1,
            )
            for b in range(blocks)
        ],
        axis=0,
    )


def make_slots(positions_ref, first_row, field_ref, grad_ref, probe_ref, measured_ref, sums_ref, table_refs):
    width = PATCH
    modes = probe_ref.shape[1]
    tall = width + 8
    right_table, left_table, back_left, back_right = table_refs
    lane = lax.broadcasted_iota(jnp.int32, (tall, width), 1)
    sublane = lax.broadcasted_iota(jnp.int32, (tall // 8, 8, width), 1)

    def place(index):
        row = positions_ref[0, index] - first_row
        col = positions_ref[1, index]
        down = lax.rem(row, 8)
        shift = lax.rem(col, width)
        return (pl.multiple_of(row - down, 8), down, pl.multiple_of(col - shift, width), shift)

    def cut(plane, top, down, base, shift):
        near = field_ref[plane, pl.ds(top, tall), pl.ds(base, width)]
        far = field_ref[plane, pl.ds(top, tall), pl.ds(base + width, width)]
        back_by = lax.rem(width - shift, width)
        turned = jnp.where(
            lane < width - shift,
            pltpu.roll(near, back_by, axis=1),
            pltpu.roll(far, back_by, axis=1),
        )
        turned = pltpu.roll(turned.reshape(tall // 8, 8, width), lax.rem(8 - down, 8), axis=1)
        picked = jnp.where(sublane[1:] < 8 - down, turned[:-1], turned[1:])
        return picked.reshape(width, width)

    def paste(plane, top, down, base, shift, values):
        turned = pltpu.roll(values, shift, axis=1).reshape(width // 8, 8, width)
        turned = pltpu.roll(turned, down, axis=1)
        blank = jnp.zeros((1, 8, width), jnp.float32)
        moved = jnp.where(
            sublane >= down,
            jnp.concatenate([turned, blank], axis=0),
            jnp.concatenate([blank, turned], axis=0),
        ).reshape(tall, width)
        grad_ref[plane, pl.ds(top, tall), pl.ds(base, width)] += jnp.where(
            lane >= shift, moved, 0.0
        )
        grad_ref[plane, pl.ds(top, tall), pl.ds(base + width, width)] += jnp.where(
            lane < shift, moved, 0.0
        )

    def slots(indices):
        places = [place(index) for index in indices]
        patches = [(cut(0, *at), cut(1, *at)) for at in places]
        exits = []
        for patch_real, patch_imag in patches:
            for mode in range(modes):
                mode_real, mode_imag = (probe_ref[0, mode], probe_ref[1, mode])
                exits.append(
                    jnp.concatenate(
                        [
                            mode_real * patch_real - mode_imag * patch_imag,
                            mode_real * patch_imag + mode_imag * patch_real,
                        ],
                        axis=1,
                    )
                )
        rows = times_right(jnp.concatenate(exits, axis=0), right_table[...])
        far = times_left(left_table[...], regroup(rows, width))
        scalings = []
        for order, index in enumerate(indices):
            part = far[:, order * modes * width : (order + 1) * modes * width]
            power = part * part
            power = power[:width] + power[width:]
            intensity = sum(power[:, m * width : (m + 1) * width] for m in range(modes))
            scaling = (
                measured_ref[index] * lax.rsqrt(jnp.maximum(intensity, AMP_FLOOR * AMP_FLOOR)) - 1.0
            )
            scalings += [scaling] * modes
        scaling = jnp.concatenate(scalings, axis=1)
        rows = times_left(back_left[...], far * jnp.concatenate([scaling, scaling], axis=0))
        back = times_right(ungroup(rows, width), back_right[...])
        sums = [[0.0] * modes, [0.0] * modes]
        density = 0.0
        for order, (patch_real, patch_imag) in enumerate(patches):
            object_real, object_imag = (0.0, 0.0)
            for mode in range(modes):
                mode_real, mode_imag = (probe_ref[0, mode], probe_ref[1, mode])
                start = (order * modes + mode) * width
                back_real = back[start : start + width, :width]
                back_imag = back[start : start + width, width:]
                object_real += mode_real * back_real + mode_imag * back_imag
                object_imag += mode_real * back_imag - mode_imag * back_real
                sums[0][mode] += patch_real * back_real + patch_imag * back_imag
                sums[1][mode] += patch_real * back_imag - patch_imag * back_real
            density += patch_real * patch_real + patch_imag * patch_imag
            paste(0, *places[order], object_real)
            paste(1, *places[order], object_imag)
        for part in range(2):
            for mode in range(modes):
                sums_ref[part, mode] += sums[part][mode]
        sums_ref[2, 0] += density

    return slots


def run_slots(positions_ref, counts_ref, order_ref, slots, wanted):

    def note(index, found):
        order_ref[found] = index
        return found + wanted(positions_ref[0, index]).astype(jnp.int32)

    found = lax.fori_loop(0, counts_ref[0], note, jnp.int32(0))

    def run(start, stop, size):

        def step(turn, carry):
            slots([order_ref[start + turn * size + i] for i in range(size)])
            return carry

        turns = lax.div(stop - start, size)
        lax.fori_loop(0, turns, step, 0)
        return start + turns * size

    reached = run(0, found, 4)
    reached = run(reached, found, 2)
    run(reached, found, 1)


def upper_kernel(
    positions_ref, counts_ref, own_ref, right_ref, probe_ref, measured_ref, parts_ref,
    grad_ref, sums_ref, field_ref, order_ref, *table_refs,
):
    tile_height, tile_width = own_ref.shape[1:]
    fill_tables(parts_ref, table_refs)
    field_ref[:, :tile_height, :tile_width] = own_ref[...]
    field_ref[:, :tile_height, tile_width:] = right_ref[...]
    grad_ref[...] = jnp.zeros_like(grad_ref)
    sums_ref[...] = jnp.zeros_like(sums_ref)
    slots = make_slots(positions_ref, 0, field_ref, grad_ref, probe_ref, measured_ref, sums_ref, table_refs)
    run_slots(positions_ref, counts_ref, order_ref, slots, lambda row: row <= tile_height - PATCH)


def lower_kernel(
    positions_ref, counts_ref, last_ref, own_ref, direct_ref, side_ref, far_ref, right_ref, corner_ref,
    probe_ref, measured_ref, parts_ref, upper_ref, upper_sums_ref,
    grad_own_ref, grad_right_ref, grad_corner_ref, grad_lower_ref, packed_out_ref,
    field_ref, grad_ref, sums_ref, order_ref, packed_ref, sem, *table_refs,
):
    tile_height, tile_width = own_ref.shape[1:]
    first = tile_height - PATCH
    fill_tables(parts_ref, table_refs)
    field_ref[:, :PATCH, :tile_width] = own_ref[:, first:]
    field_ref[:, PATCH : PATCH + DIRECT, :tile_width] = direct_ref[...]

    @pl.when(last_ref[0] == 1)
    def _():
        field_ref[:, PATCH + DIRECT :, :tile_width] = far_ref[...]

    @pl.when(last_ref[0] == 0)
    def _():
        field_ref[:, PATCH + DIRECT :, :tile_width] = side_ref[...]

    field_ref[:, :PATCH, tile_width:] = right_ref[:, first:]
    field_ref[:, PATCH:, tile_width:] = corner_ref[...]
    grad_ref[:, :PATCH] = upper_ref[:, first:tile_height]
    grad_ref[:, PATCH:] = jnp.zeros_like(grad_ref[:, PATCH:])
    sums_ref[...] = upper_sums_ref[...]
    slots = make_slots(positions_ref, first, field_ref, grad_ref, probe_ref, measured_ref, sums_ref, table_refs)
    run_slots(positions_ref, counts_ref, order_ref, slots, lambda row: row > first)
    for block in range(packed_ref.shape[0]):
        part, mode, start = (block // 16, block // 8 % 2, block % 8 * 16)
        for piece in range(4):
            row = start + piece * 4
            packed_ref[block, piece] = sums_ref[part, mode, row : row + 4]
        packed_ref[block, 4] = sums_ref[2, 0, block * 4 : block * 4 + 4]
    packed_copy = pltpu.make_async_copy(packed_ref, packed_out_ref, sem)
    packed_copy.start()
    grad_right_ref[:, :first] = upper_ref[:, :first, tile_width:]
    grad_right_ref[:, first:] = grad_ref[:, :PATCH, tile_width:]
    grad_corner_ref[...] = grad_ref[:, PATCH:, tile_width:]
    grad_own_ref[...] = grad_ref[:, :PATCH, :tile_width]
    grad_lower_ref[...] = grad_ref[:, PATCH:, :tile_width]
    packed_copy.wait()


def float_array(*shape):
    return jax.ShapeDtypeStruct(shape, jnp.float32)


def table_scratch():
    tall = pltpu.VMEM((6 * PATCH, 2 * PATCH), jnp.bfloat16)
    wide = pltpu.VMEM((2 * PATCH, 6 * PATCH), jnp.bfloat16)
    return [tall, wide, wide, tall]


VMEM_SPEC = pl.BlockSpec(memory_space=pltpu.VMEM)
SMEM_SPEC = pl.BlockSpec(memory_space=pltpu.SMEM)
PARAMS = pltpu.CompilerParams(vmem_limit_bytes=24 * 1024 * 1024)


def upper_slots(positions, counts, own, right, probe, measured, parts):
    tile_height, tile_width = own.shape[1:]
    wide = tile_width + PATCH
    return pl.pallas_call(
        upper_kernel,
        in_specs=[SMEM_SPEC] * 2 + [VMEM_SPEC] * 5,
        out_specs=[VMEM_SPEC] * 2,
        out_shape=[float_array(2, tile_height + 8, wide), float_array(3, 2, PATCH, PATCH)],
        scratch_shapes=[
            pltpu.VMEM((2, tile_height + 8, wide), jnp.float32),
            pltpu.SMEM((positions.shape[1],), jnp.int32),
        ]
        + table_scratch(),
        compiler_params=PARAMS,
        cost_estimate=pl.CostEstimate(flops=3_000_000_000, transcendentals=0, bytes_accessed=3_000_000),
        name="upper_slots",
    )(positions, counts, own, right, probe, measured, parts)


def lower_slots(
    positions, counts, last, own, direct, side, far, right, corner, probe, measured, parts, upper, sums
):
    tile_height, tile_width = own.shape[1:]
    wide = tile_width + PATCH
    return pl.pallas_call(
        lower_kernel,
        in_specs=[SMEM_SPEC] * 3 + [VMEM_SPEC] * 11,
        out_specs=[VMEM_SPEC] * 4 + [pl.BlockSpec(memory_space=pl.ANY)],
        out_shape=[
            float_array(2, PATCH, tile_width),
            float_array(2, tile_height, PATCH),
            float_array(2, PATCH, PATCH),
            float_array(2, PATCH, tile_width),
            float_array(32, 5, 4, PATCH),
        ],
        scratch_shapes=[
            pltpu.VMEM((2, 2 * PATCH, wide), jnp.float32),
            pltpu.VMEM((2, 2 * PATCH, wide), jnp.float32),
            pltpu.VMEM((3, 2, PATCH, PATCH), jnp.float32),
            pltpu.SMEM((positions.shape[1],), jnp.int32),
            pltpu.VMEM((32, 5, 4, PATCH), jnp.float32),
            pltpu.SemaphoreType.DMA,
        ]
        + table_scratch(),
        compiler_params=PARAMS,
        cost_estimate=pl.CostEstimate(flops=3_000_000_000, transcendentals=0, bytes_accessed=5_000_000),
        name="lower_slots",
    )(positions, counts, last, own, direct, side, far, right, corner, probe, measured, parts, upper, sums)


def object_kernel(
    first_ref, own_ref, upper_ref, lower_ref, spilled_ref, rim_ref, side_ref, far_ref, probe_ref, out_ref
):
    tile_height, tile_width = own_ref.shape[1:]
    first = tile_height - PATCH
    power = probe_ref[...] * probe_ref[...]
    power = power[0, 0] + power[0, 1] + power[1, 0] + power[1, 1]
    weight = 1.0 / (jnp.max(power, axis=(0, 1), keepdims=True) + 1e-06)
    from_far = first_ref[0] == 1
    for plane in range(2):
        for start in range(0, tile_height, PATCH):
            for side in range(0, tile_width, PATCH):
                rows, cols = (slice(start, start + PATCH), slice(side, side + PATCH))
                if start < first:
                    total = upper_ref[plane, rows, cols]
                else:
                    total = lower_ref[plane, :, cols]
                if side == 0:
                    total += spilled_ref[plane, rows, :]
                if start == 0:
                    rest = jnp.where(from_far, far_ref[plane, :, cols], side_ref[plane, :, cols])
                    total += jnp.concatenate([rim_ref[plane, :, cols], rest], axis=0)
                out_ref[plane, rows, cols] = own_ref[plane, rows, cols] + total * weight


def object_update(first, own, upper, lower, spilled, rim, side, far, probe):
    return pl.pallas_call(
        object_kernel,
        in_specs=[SMEM_SPEC] + [VMEM_SPEC] * 8,
        out_specs=VMEM_SPEC,
        out_shape=float_array(*own.shape),
        compiler_params=PARAMS,
        cost_estimate=pl.CostEstimate(flops=OBJECT_COST, transcendentals=0, bytes_accessed=4_000_000),
        name="object_update",
    )(first, own, upper, lower, spilled, rim, side, far, probe)


def probe_kernel(blocks_ref, out_ref, density_ref, weight_ref):
    for block in range(blocks_ref.shape[0]):
        density_ref[block * 4 : block * 4 + 4] = blocks_ref[block, 4]
    weight_ref[...] = lax.rsqrt(density_ref[...] + 1.0)
    for block in range(blocks_ref.shape[0]):
        part, mode, start = (block // 16, block // 8 % 2, block % 8 * 16)
        for piece in range(4):
            row = start + piece * 4
            out_ref[part, mode, row : row + 4] = blocks_ref[block, piece] * weight_ref[row : row + 4]


def probe_update(blocks, shape):
    return pl.pallas_call(
        probe_kernel,
        in_specs=[VMEM_SPEC],
        out_specs=VMEM_SPEC,
        out_shape=float_array(*shape),
        scratch_shapes=[pltpu.VMEM((PATCH, PATCH), jnp.float32)] * 2,
        compiler_params=PARAMS,
        name="probe_update",
    )(blocks)


def halo_kernel(own_ref, side_ref, direct_ref, left_ref, sems):
    pieces = (
        (own_ref.at[:, pl.ds(DIRECT, PATCH - DIRECT), :], side_ref),
        (own_ref.at[:, pl.ds(0, DIRECT), :], direct_ref),
        (own_ref.at[:, :, pl.ds(0, PATCH)], left_ref),
    )
    copies = [
        pltpu.make_async_copy(source, target, sems.at[order])
        for order, (source, target) in enumerate(pieces)
    ]
    for copy in copies:
        copy.start()
    for copy in copies:
        copy.wait()


def halo_pieces(own):
    planes, tile_height, tile_width = own.shape
    return pl.pallas_call(
        halo_kernel,
        in_specs=[pl.BlockSpec(memory_space=pltpu.MemorySpace.HBM)],
        out_specs=[VMEM_SPEC] * 3,
        out_shape=[
            float_array(planes, PATCH - DIRECT, tile_width),
            float_array(planes, DIRECT, tile_width),
            float_array(planes, tile_height, PATCH),
        ],
        scratch_shapes=[pltpu.SemaphoreType.DMA((3,))],
        compiler_params=PARAMS,
        name="halo_pieces",
    )(own)


def corner_kernel(last_ref, direct_ref, side_ref, far_ref, corner_ref):
    from_far = last_ref[0] == 1
    for plane in range(2):
        corner_ref[plane, :DIRECT] = direct_ref[plane, :, :PATCH]
        corner_ref[plane, DIRECT:] = jnp.where(
            from_far, far_ref[plane, :, :PATCH], side_ref[plane, :, :PATCH]
        )


def corner_piece(last, direct, side, far):
    return pl.pallas_call(
        corner_kernel,
        in_specs=[SMEM_SPEC] + [VMEM_SPEC] * 3,
        out_specs=VMEM_SPEC,
        out_shape=float_array(2, PATCH, PATCH),
        compiler_params=PARAMS,
        name="corner_piece",
    )(last, direct, side, far)


def sum_kernel(terms_ref, out_ref):
    total = jnp.sum(terms_ref[...], axis=0)
    out_ref[...] = jnp.broadcast_to(total[None], out_ref.shape)


def sum_for(terms, copies):
    return pl.pallas_call(
        sum_kernel,
        in_specs=[VMEM_SPEC],
        out_specs=VMEM_SPEC,
        out_shape=float_array(copies, *terms.shape[1:]),
        compiler_params=PARAMS,
        name="sum_for",
    )(terms)


def rim_kernel(lower_ref, spilled_ref, direct_ref, side_ref):
    for plane in range(2):
        near = lower_ref[plane, :, :PATCH] + spilled_ref[plane]
        direct_ref[plane, :, :PATCH] = near[:RIM_DIRECT]
        side_ref[plane, :, :PATCH] = near[RIM_DIRECT:]
        direct_ref[plane, :, PATCH:] = lower_ref[plane, :RIM_DIRECT, PATCH:]
        side_ref[plane, :, PATCH:] = lower_ref[plane, RIM_DIRECT:, PATCH:]


def rim_pieces(lower, spilled):
    planes, height, width = lower.shape
    return pl.pallas_call(
        rim_kernel,
        in_specs=[VMEM_SPEC] * 2,
        out_specs=[VMEM_SPEC] * 2,
        out_shape=[
            float_array(planes, RIM_DIRECT, width),
            float_array(planes, height - RIM_DIRECT, width),
        ],
        compiler_params=PARAMS,
        cost_estimate=pl.CostEstimate(flops=RIM_COST, transcendentals=0, bytes_accessed=1_000_000),
        name="rim_pieces",
    )(lower, spilled)


def moved(array, where):
    pairs = []
    for device in range(lax.axis_size("row") * lax.axis_size("col")):
        row, col = divmod(device, lax.axis_size("col"))
        target = where(row)
        if target is not None:
            pairs.append((device, target * lax.axis_size("col") + col))
    return lax.ppermute(array, ("row", "col"), pairs)


def around(row, by):
    return row // RUN * RUN + (row + by) % RUN


def far_up(row):
    return row - RUN if row % RUN == RUN - 1 and row >= RUN else None


def far_down(row):
    return row + RUN if row % RUN == 0 and row + RUN < lax.axis_size("row") else None


def per_device(object_field, probe_modes, measured, positions, counts):
    planes, lines = device_groups(lax.axis_size("row") * lax.axis_size("col"))
    places, live, amplitudes = (positions[0, 0], counts[0], measured[0, 0])
    parts = jnp.asarray(fourier_parts(PATCH))
    place = lax.axis_index("row") % RUN
    side_rows, direct_rows, left_columns = halo_pieces(
        pltpu.with_memory_space_constraint(object_field, pltpu.MemorySpace.HBM)
    )
    side = moved(side_rows, lambda row: around(row, -1))
    direct = shifted(direct_rows, "row", -1)
    far = moved(side, far_up)
    right = shifted(left_columns, "col", -1)
    upper, upper_sums = upper_slots(
        places, live, object_field, right, probe_modes, amplitudes, parts
    )
    direct, side, far, upper_sums = lax.optimization_barrier((direct, side, far, upper_sums))
    last = (place == RUN - 1).astype(jnp.int32)[None]
    corner = shifted(corner_piece(last, direct, side, far), "col", -1)
    lower, grad_right, grad_corner, grad_lower, packed = lower_slots(
        places, live, last, object_field, direct, side, far, right, corner,
        probe_modes, amplitudes, parts, upper, upper_sums,
    )
    spilled = shifted(grad_right, "col", 1)
    spilled_corner = shifted(grad_corner, "col", 1)
    rim_direct, rim_side = rim_pieces(grad_lower, spilled_corner)
    rim_direct = shifted(rim_direct, "row", 1)
    rim_side = moved(rim_side, lambda row: around(row, 1))
    rim_far = moved(rim_side, far_down)
    terms = exchange(packed, planes)
    terms = exchange(sum_for(terms, len(lines[0])), lines)
    blocks = exchange(sum_for(terms, len(planes[0])), planes)
    object_new = object_update(
        (place == 0).astype(jnp.int32)[None],
        object_field, upper, lower, spilled, rim_direct, rim_side, rim_far, probe_modes,
    )
    probe_step = probe_update(blocks, probe_modes.shape)
    return (object_new, probe_step)


def solution(mesh):
    in_specs = (
        P(None, "row", "col"),
        P(),
        P("row", "col", None, None, None),
        P("row", "col", None, None),
        P("row", "col"),
    )
    out_specs = (P(None, "row", "col"), P())
    return jax.shard_map(
        per_device, mesh=mesh, in_specs=in_specs, out_specs=out_specs, check_vma=False
    )
```
